32 devices in a mesh: dp: 16 (over z, y, x), tensor: 2 (over core).
Axes of the slice: x: 2, y: 2, z: 4, core: 2. Of those that a mesh axis runs over, the one named last changes fastest.
Arguments:
- tokens: bfloat16 [32768, 768], P('dp'), may hold values from -6 to 6
- first_values: bfloat16 [32768, 384], P('dp'), may hold values from -6 to 6
- seq_count: int32 [16], P('dp'), may hold values from 1 to 2, as said below
- skip_map: int32 [6], P('tensor'), may hold values from 0 to 5, as said below
- norm1_gain: float32 [768], replicated, may hold values from 0.5 to 1.5
- norm1_shift: float32 [768], replicated, may hold values from -1 to 1
- query_weight: bfloat16 [768, 768], P(None, 'tensor'), may hold values from -0.3125 to 0.3125
- key_weight: bfloat16 [768, 768], P(None, 'tensor'), may hold values from -0.3125 to 0.3125
- value_weight: bfloat16 [768, 384], P(None, 'tensor'), may hold values from -0.21875 to 0.21875
- out_weight: bfloat16 [768, 768], P('tensor'), may hold values from -1.75 to 1.75
- norm2_gain: float32 [768], replicated, may hold values from 0.5 to 1.5
- norm2_shift: float32 [768], replicated, may hold values from -1 to 1
- up_weight: bfloat16 [768, 3072], P(None, 'tensor'), may hold values from -0.21875 to 0.21875
- down_weight: bfloat16 [3072, 768], P('tensor'), may hold values from -0.109375 to 0.109375
- cotangent: bfloat16 [32768, 768], P('dp'), may hold values from -6 to 6
Outputs:
- layer_out: float32 [32768, 768], P('dp')
- input_grad: float32 [32768, 768], P('dp')
- first_value_grad: float32 [32768, 384], P('dp', 'tensor')
- norm1_gain_grad: float32 [768], P('dp')
- norm1_shift_grad: float32 [768], P('dp')
- query_weight_grad: float32 [768, 768], P('dp', 'tensor')
- key_weight_grad: float32 [768, 768], P('dp', 'tensor')
- value_weight_grad: float32 [768, 384], P('dp', 'tensor')
- out_weight_grad: float32 [768, 768], P('tensor', 'dp')
- norm2_gain_grad: float32 [768], P('dp')
- norm2_shift_grad: float32 [768], P('dp')
- up_weight_grad: float32 [768, 3072], P('dp', 'tensor')
- down_weight_grad: float32 [3072, 768], P('tensor', 'dp')
The draws below stay inside these ranges and needn't reach their ends.
Inputs may be any that keep to these rules, and one draw needn't show every extreme that they name: `seq_count`: some index of dp holds 2 live sequences in every draw; slots below the count are live. `skip_map`: A permutation: each first-layer value head is read by exactly one slot; the slots of each index of tensor read exactly one head of the other index's half.
All inputs are finite; a program needn't handle non-finite values.
Results may differ from the reference program's by a relative error of at most 0.012.
The reference program's roundings to bfloat16 on the way count: a program that leaves them out, or rounds other values in their place, can miss the bound.
Values sent between devices are 32-bit elements; how exact they have to be, the bound alone decides.
A program may use at most 192 MiB of HBM per device.

```python
import jax
import jax.numpy as jnp
from jax import lax

D = 768
HEADS = 12
HEAD_DIM = 64
FF = 3072
SEQ_LEN = 1024
SEQ_DEV = 2
SKIP_HEADS = 6
TOKENS = 32768
N_DP = 16
N_TENSOR = 2


def draw_seq_count(key, part):
    key = jax.random.fold_in(key, 11)
    first_key, second_key = jax.random.split(key)
    counts = jax.random.randint(first_key, (N_DP,), 1, SEQ_DEV + 1)
    chosen = jax.random.randint(second_key, (), 0, N_DP)
    return jnp.where(jnp.arange(N_DP) == chosen, SEQ_DEV, counts).astype(jnp.int32)


def draw_skip_map(key, part):
    key = jax.random.fold_in(key, 23)
    key_list = jax.random.split(key, 4)
    half_count = SKIP_HEADS // 2
    lower_pick = jax.random.randint(key_list[0], (), 0, half_count)
    upper_pick = jax.random.randint(key_list[1], (), half_count, SKIP_HEADS)
    base = jnp.arange(SKIP_HEADS)
    swapped = jnp.where(base == lower_pick, upper_pick, jnp.where(base == upper_pick, lower_pick, base))
    lower_half = swapped[:half_count][jax.random.permutation(key_list[2], half_count)]
    upper_half = swapped[half_count:][jax.random.permutation(key_list[3], half_count)]
    return jnp.concatenate([lower_half, upper_half]).astype(jnp.int32)


def level_of(stream_key, shape, cuts, smallest, top_value):
    level, own = 1.0, jax.random.fold_in(stream_key, 6)
    for dim, shards_of in cuts:
        heights = jnp.exp(jax.random.uniform(jax.random.fold_in(own, dim), (shards_of,), jnp.float32, smallest / len(cuts), top_value / len(cuts)))
        level = level * jnp.repeat(heights, shape[dim] // shards_of).reshape([-1 if axis == dim else 1 for axis in range(len(shape))])
    return level


def centred(rng, dims, width, limit, shards=(), kind=jnp.bfloat16):
    result = width * jax.random.normal(rng, dims, jnp.float32)
    if shards:
        result = result * level_of(rng, dims, shards, -0.22, 0.18)
    return jnp.clip(result, -limit, limit).astype(kind)


def setup_inputs(seed: int = 0) -> dict:
    arg_keys = jax.random.split(jax.random.key(seed), 16)
    return {
        "tokens": centred(arg_keys[0], (TOKENS, D), 1.0, 6.0, ((0, 16),)),
        "first_values": centred(arg_keys[1], (TOKENS, SKIP_HEADS * HEAD_DIM), 1.0, 6.0, ((0, 16),)),
        "seq_count": draw_seq_count(jax.random.fold_in(arg_keys[15], 71), 0),
        "skip_map": draw_skip_map(jax.random.fold_in(arg_keys[15], 71), 0),
        "norm1_gain": jnp.clip(1.0 + 0.1 * jax.random.normal(arg_keys[4], (D,), jnp.float32), 0.5, 1.5),
        "norm1_shift": centred(arg_keys[5], (D,), 0.2, 1.0, (), jnp.float32),
        "query_weight": centred(arg_keys[6], (D, D), (D // 2) ** -0.5, 0.3125, ((1, 2),)),
        "key_weight": centred(arg_keys[7], (D, D), (D // 2) ** -0.5, 0.3125, ((1, 2),)),
        "value_weight": centred(arg_keys[8], (D, SKIP_HEADS * HEAD_DIM), D ** -0.5, 0.21875, ((1, 2),)),
        "out_weight": centred(arg_keys[9], (D, D), (D // 64) ** -0.5, 1.75, ((0, 2),)),
        "norm2_gain": jnp.clip(1.0 + 0.1 * jax.random.normal(arg_keys[10], (D,), jnp.float32), 0.5, 1.5),
        "norm2_shift": centred(arg_keys[11], (D,), 0.2, 1.0, (), jnp.float32),
        "up_weight": centred(arg_keys[12], (D, FF), D ** -0.5, 0.21875, ((1, 2),)),
        "down_weight": centred(arg_keys[13], (FF, D), FF ** -0.5, 0.109375, ((0, 2),)),
        "cotangent": centred(arg_keys[14], (TOKENS, D), 1.0, 6.0, ((0, 16),)),
    }


@jax.custom_vjp
def low(v):
    return lax.optimization_barrier(v.astype(jnp.bfloat16)).astype(jnp.float32)

@jax.custom_vjp
def low_back(v):
    return v

def low_keep(v):
    return (low(v), None)

def low_pass(kept, grad):
    return (grad,)

def back_keep(v):
    return (v, None)

def back_low(kept, grad):
    return (low(grad),)
low.defvjp(low_keep, low_pass)
low_back.defvjp(back_keep, back_low)
eps_norm = 1e-05
neg_fill = -1e+30
precise = lax.Precision.HIGHEST

def matmul(left_op, right_op):
    return jnp.dot(left_op, right_op, precision=precise)

def normalize(values_in, norm_gain, norm_shift):
    average = lax.optimization_barrier(jnp.mean(values_in, axis=-1, keepdims=True))
    centered = values_in - average
    variance = lax.optimization_barrier(jnp.mean(centered * centered, axis=-1, keepdims=True))
    return centered * lax.rsqrt(variance + eps_norm) * norm_gain + norm_shift

def attend_sequence(packed):
    seq_query, seq_keys, seq_values = packed
    length = seq_query.shape[0]
    score_scale = HEAD_DIM ** (-0.5)
    scores = low_back(jnp.einsum('qhd,khd->hqk', seq_query, seq_keys, precision=precise) * score_scale)
    positions = jnp.arange(length)
    masked = jnp.where(positions[None, None, :] <= positions[None, :, None], scores, neg_fill)
    weights_low = low(jax.nn.softmax(masked, axis=-1))
    return jnp.einsum('hqk,khd->qhd', weights_low, seq_values, precision=precise)

def layer(params, block_in, block_first, skip_map):
    norm1_gain, norm1_shift, query_weight, key_weight, value_weight, out_weight, norm2_gain, norm2_shift, up_weight, down_weight = params
    block_rows = block_in.shape[0]
    normed_one = low(normalize(block_in, norm1_gain, norm1_shift))
    queries = low(low_back(matmul(normed_one, query_weight)))
    keys_all = low(low_back(matmul(normed_one, key_weight)))
    fresh_values = low(low_back(matmul(normed_one, value_weight)))
    slot_select = (skip_map[:, None] == jnp.arange(SKIP_HEADS)[None, :]).astype(jnp.float32)
    picked = jnp.einsum('tjd,ij->tid', block_first.reshape(block_rows, SKIP_HEADS, HEAD_DIM), slot_select, precision=precise)
    group_shape = (block_rows, N_TENSOR, SKIP_HEADS // N_TENSOR, HEAD_DIM)
    values = jnp.concatenate([fresh_values.reshape(group_shape), picked.reshape(group_shape)], axis=2)
    seq_shape = (block_rows // SEQ_LEN, SEQ_LEN, HEADS, HEAD_DIM)
    attended = lax.map(jax.checkpoint(attend_sequence), (queries.reshape(seq_shape), keys_all.reshape(seq_shape), values.reshape(seq_shape)))
    attended = low(low_back(attended.reshape(block_rows, D)))
    mixed = block_in + low_back(matmul(attended, out_weight))
    normed_two = low(normalize(mixed, norm2_gain, norm2_shift))
    upper = low_back(matmul(normed_two, up_weight))
    activ = low(jax.nn.gelu(upper, approximate=True))
    return mixed + low_back(matmul(activ, down_weight))

def reference(tokens, first_values, seq_count, skip_map, norm1_gain, norm1_shift, query_weight, key_weight, value_weight, out_weight, norm2_gain, norm2_shift, up_weight, down_weight, cotangent):
    params = tuple((operand.astype(jnp.float32) for operand in (norm1_gain, norm1_shift, query_weight, key_weight, value_weight, out_weight, norm2_gain, norm2_shift, up_weight, down_weight)))
    rows_dev = SEQ_DEV * SEQ_LEN
    inputs = tokens.astype(jnp.float32).reshape(N_DP, rows_dev, D)
    firsts = first_values.astype(jnp.float32).reshape(N_DP, rows_dev, SKIP_HEADS * HEAD_DIM)
    cotangents = cotangent.astype(jnp.float32).reshape(N_DP, rows_dev, D)
    slot_rows = jnp.arange(rows_dev) // SEQ_LEN
    live_rows = (slot_rows[None, :] < seq_count[:, None]).astype(jnp.float32)

    def apply_layer(params_in, block_in, block_first):
        return layer(params_in, block_in, block_first, skip_map)

    def one_device(totals, stacked):
        block_in, block_first, block_cot, block_live = stacked
        outcome, pullback = jax.vjp(apply_layer, params, block_in, block_first)
        param_grads, grad_in, grad_first = pullback(block_cot * block_live[:, None])
        totals = jax.tree.map(lambda total_now, added: total_now + added, totals, param_grads)
        return (totals, (outcome, grad_in, grad_first))
    zero_grads = jax.tree.map(jnp.zeros_like, params)
    totals, (outcome, grad_in, grad_first) = lax.scan(one_device, zero_grads, (inputs, firsts, cotangents, live_rows))
    return (outcome.reshape(TOKENS, D), grad_in.reshape(TOKENS, D), grad_first.reshape(TOKENS, SKIP_HEADS * HEAD_DIM), totals[0], totals[1], totals[2], totals[3], totals[4], totals[5], totals[6], totals[7], totals[8], totals[9])
```

```python
import jax
import jax.numpy as jnp
from jax import lax
from jax.sharding import PartitionSpec as P

HEAD_DIM = 64
SEQ_LEN = 1024
SKIP_HEADS = 6


eps_norm = 1e-05
neg_fill = -1e30
precise = lax.Precision.HIGHEST


def normalize(values_in, norm_gain, norm_shift):
    average = jnp.mean(values_in, axis=-1, keepdims=True)
    centered = values_in - average
    variance = jnp.mean(centered * centered, axis=-1, keepdims=True)
    return centered * lax.rsqrt(variance + eps_norm) * norm_gain + norm_shift


def smooth_gate(upper):
    return jax.nn.gelu(upper, approximate=True)


def causal_scores(query_block, seq_keys, first_row):
    block_rows = query_block.shape[0]
    length = seq_keys.shape[0]
    score_scale = query_block.shape[2] ** (-0.5)
    scores = (
        jnp.einsum("qhd,khd->hqk", query_block, seq_keys, preferred_element_type=jnp.float32)
        * score_scale
    )
    query_pos = first_row + lax.iota(jnp.int32, block_rows)
    key_pos = lax.iota(jnp.int32, length)
    return jnp.where(key_pos[None, None, :] <= query_pos[None, :, None], scores, neg_fill)


def attend_forward(queries, keys_low, values):

    def one_sequence(packed):
        seq_query, seq_keys, seq_values = packed
        length = seq_query.shape[0]
        block_rows = min(512, length)
        count_blocks = length // block_rows
        query_blocks = seq_query.reshape((count_blocks, block_rows) + seq_query.shape[1:])
        block_starts = lax.iota(jnp.int32, count_blocks) * block_rows

        def one_block(block_pair):
            query_block, first_row = block_pair
            masked = causal_scores(query_block, seq_keys, first_row)
            row_peak = jnp.max(masked, axis=-1)
            expo_terms = jnp.exp(masked - row_peak[..., None])
            row_total = jnp.sum(expo_terms, axis=-1)
            weights_low = (expo_terms / row_total[..., None]).astype(jnp.bfloat16)
            mixed_rows = jnp.einsum(
                "hqk,khd->qhd", weights_low, seq_values, preferred_element_type=jnp.float32
            )
            return (mixed_rows.astype(jnp.bfloat16), row_peak, row_total)

        attended, peaks_all, totals_all = lax.map(one_block, (query_blocks, block_starts))
        return (attended.reshape(seq_query.shape), peaks_all, totals_all)

    return lax.map(one_sequence, (queries, keys_low, values))


def attend_backward(queries, keys_low, values, grad_heads, peaks_all, totals_all):

    def one_sequence(packed):
        seq_query, seq_keys, seq_values, seq_grad, seq_peaks, seq_totals = packed
        length, head_count, head_width = seq_query.shape
        block_rows = min(512, length)
        count_blocks = length // block_rows
        block_shape = (count_blocks, block_rows, head_count, head_width)
        score_scale = head_width ** (-0.5)
        block_starts = lax.iota(jnp.int32, count_blocks) * block_rows

        def one_block(carry, block_pack):
            key_acc, value_acc = carry
            query_block, grad_block, row_peak, row_total, first_row = block_pack
            masked = causal_scores(query_block, seq_keys, first_row)
            soft_full = jnp.exp(masked - row_peak[..., None]) / row_total[..., None]
            weights_low = soft_full.astype(jnp.bfloat16)
            value_acc = value_acc + jnp.einsum(
                "hqk,qhd->khd", weights_low, grad_block, preferred_element_type=jnp.float32
            )
            grad_weights = jnp.einsum(
                "qhd,khd->hqk", grad_block, seq_values, preferred_element_type=jnp.float32
            )
            row_dot = jnp.sum(soft_full * grad_weights, axis=-1, keepdims=True)
            score_grad = (soft_full * (grad_weights - row_dot)).astype(jnp.bfloat16)
            query_grad = (
                jnp.einsum("hqk,khd->qhd", score_grad, seq_keys, preferred_element_type=jnp.float32)
                * score_scale
            )
            key_acc = (
                key_acc
                + jnp.einsum(
                    "hqk,qhd->khd", score_grad, query_block, preferred_element_type=jnp.float32
                )
                * score_scale
            )
            return ((key_acc, value_acc), query_grad.astype(jnp.bfloat16))

        zeros_acc = jnp.zeros((length, head_count, head_width), jnp.float32)
        (key_acc, value_acc), query_grads = lax.scan(
            one_block,
            (zeros_acc, zeros_acc),
            (
                seq_query.reshape(block_shape),
                seq_grad.reshape(block_shape),
                seq_peaks,
                seq_totals,
                block_starts,
            ),
        )
        return (query_grads.reshape(seq_query.shape), key_acc.astype(jnp.bfloat16), value_acc)

    return lax.map(one_sequence, (queries, keys_low, values, grad_heads, peaks_all, totals_all))


def on_device(
    tokens,
    first_values,
    seq_count,
    skip_map,
    norm1_gain,
    norm1_shift,
    query_weight,
    key_weight,
    value_weight,
    out_weight,
    norm2_gain,
    norm2_shift,
    up_weight,
    down_weight,
    cotangent,
):
    rows_dev = tokens.shape[0]
    head_count = query_weight.shape[1] // HEAD_DIM
    fresh_count = value_weight.shape[1] // HEAD_DIM
    seq_shape = (rows_dev // SEQ_LEN, SEQ_LEN, head_count, HEAD_DIM)
    inputs = tokens.astype(jnp.float32)
    normed_one, pull_one = jax.vjp(normalize, inputs, norm1_gain, norm1_shift)
    normed_low = normed_one.astype(jnp.bfloat16)
    queries = jnp.dot(normed_low, query_weight, preferred_element_type=jnp.float32).astype(
        jnp.bfloat16
    )
    keys_low = jnp.dot(normed_low, key_weight, preferred_element_type=jnp.float32).astype(
        jnp.bfloat16
    )
    fresh_values = jnp.dot(normed_low, value_weight, preferred_element_type=jnp.float32).astype(
        jnp.bfloat16
    )
    slot_select = skip_map[:, None] == lax.iota(jnp.int32, SKIP_HEADS)[None, :]
    picked = jnp.einsum(
        "tjd,ij->tid",
        first_values.reshape(rows_dev, SKIP_HEADS, HEAD_DIM),
        slot_select.astype(jnp.bfloat16),
        preferred_element_type=jnp.float32,
    ).astype(jnp.bfloat16)
    values = jnp.concatenate(
        [fresh_values.reshape(rows_dev, fresh_count, HEAD_DIM), picked], axis=1
    )
    query_seq = queries.reshape(seq_shape)
    key_seq = keys_low.reshape(seq_shape)
    value_seq = values.reshape(seq_shape)
    attended, peaks_all, totals_all = attend_forward(query_seq, key_seq, value_seq)
    attended_low = attended.reshape(rows_dev, head_count * HEAD_DIM)
    attn_part = jnp.dot(attended_low, out_weight, preferred_element_type=jnp.float32)
    mixed = inputs + lax.psum(attn_part, "tensor")
    normed_two, pull_two = jax.vjp(normalize, mixed, norm2_gain, norm2_shift)
    normed_two_low = normed_two.astype(jnp.bfloat16)
    upper = jnp.dot(normed_two_low, up_weight, preferred_element_type=jnp.float32)
    activ, gate_pull = jax.vjp(smooth_gate, upper)
    activ_low = activ.astype(jnp.bfloat16)
    down_part = jnp.dot(activ_low, down_weight, preferred_element_type=jnp.float32)
    layer_out = mixed + lax.psum(down_part, "tensor")
    slot_rows = lax.iota(jnp.int32, rows_dev) // SEQ_LEN
    live_rows = (slot_rows < seq_count[0]).astype(jnp.float32)
    grad_out = cotangent.astype(jnp.float32) * live_rows[:, None]
    grad_low = grad_out.astype(jnp.bfloat16)
    down_grad = jnp.einsum("rf,rd->df", activ_low, grad_low, preferred_element_type=jnp.float32)
    grad_activ = jnp.dot(grad_low, down_weight.T, preferred_element_type=jnp.float32)
    grad_upper = gate_pull(grad_activ)[0].astype(jnp.bfloat16)
    up_grad = jnp.einsum(
        "rd,rf->df", normed_two_low, grad_upper, preferred_element_type=jnp.float32
    )
    two_part = jnp.dot(grad_upper, up_weight.T, preferred_element_type=jnp.float32)
    grad_two = lax.psum(two_part, "tensor")
    grad_mixed_norm, gain2_grad, shift2_grad = pull_two(grad_two)
    grad_mixed = grad_out + grad_mixed_norm
    grad_attn_low = grad_mixed.astype(jnp.bfloat16)
    out_grad = jnp.einsum(
        "rh,rd->dh", attended_low, grad_attn_low, preferred_element_type=jnp.float32
    )
    grad_heads = jnp.dot(grad_attn_low, out_weight.T, preferred_element_type=jnp.float32).astype(
        jnp.bfloat16
    )
    query_grads, key_grads, value_grads = attend_backward(
        query_seq, key_seq, value_seq, grad_heads.reshape(seq_shape), peaks_all, totals_all
    )
    query_low = query_grads.reshape(rows_dev, head_count * HEAD_DIM)
    key_low = key_grads.reshape(rows_dev, head_count * HEAD_DIM)
    value_rows = value_grads.reshape(rows_dev, head_count, HEAD_DIM)
    fresh_low = (
        value_rows[:, :fresh_count].astype(jnp.bfloat16).reshape(rows_dev, fresh_count * HEAD_DIM)
    )
    skip_rows = value_rows[:, fresh_count:]
    first_part = jnp.einsum(
        "tid,ij->tjd", skip_rows, slot_select.astype(jnp.float32), precision=precise
    ).reshape(rows_dev, SKIP_HEADS * HEAD_DIM)
    query_grad = jnp.einsum("rd,rh->dh", normed_low, query_low, preferred_element_type=jnp.float32)
    key_grad = jnp.einsum("rd,rh->dh", normed_low, key_low, preferred_element_type=jnp.float32)
    value_grad = jnp.einsum("rd,rh->dh", normed_low, fresh_low, preferred_element_type=jnp.float32)
    one_part = (
        jnp.dot(query_low, query_weight.T, preferred_element_type=jnp.float32)
        + jnp.dot(key_low, key_weight.T, preferred_element_type=jnp.float32)
        + jnp.dot(fresh_low, value_weight.T, preferred_element_type=jnp.float32)
    )
    grad_one = lax.psum(one_part, "tensor")
    first_grad = lax.psum_scatter(first_part, "tensor", scatter_dimension=1, tiled=True)
    grad_in_norm, gain1_grad, shift1_grad = pull_one(grad_one)
    input_grad = grad_mixed + grad_in_norm
    columns = [query_grad, key_grad, value_grad, out_grad, up_grad, down_grad]
    widths = [part.shape[1] for part in columns]
    vectors = jnp.stack([gain1_grad, shift1_grad, gain2_grad, shift2_grad], axis=1)
    vectors = jnp.pad(vectors, ((0, 0), (0, 124)))
    packed = jnp.concatenate(columns + [vectors], axis=1)
    summed = lax.psum_scatter(packed, "dp", scatter_dimension=0, tiled=True)
    pieces, start = [], 0
    for width in widths:
        pieces.append(summed[:, start : start + width])
        start += width
    query_total, key_total, value_total, out_rows, up_total, down_rows = pieces
    out_total, down_total = out_rows.T, down_rows.T
    gain1_total, shift1_total, gain2_total, shift2_total = (summed[:, start + n] for n in range(4))
    return (
        layer_out,
        input_grad,
        first_grad,
        gain1_total,
        shift1_total,
        query_total,
        key_total,
        value_total,
        out_total,
        gain2_total,
        shift2_total,
        up_total,
        down_total,
    )


def solution(mesh):
    placed = (
        P("dp", None),
        P("dp", None),
        P("dp"),
        P("tensor"),
        P(),
        P(),
        P(None, "tensor"),
        P(None, "tensor"),
        P(None, "tensor"),
        P("tensor", None),
        P(),
        P(),
        P(None, "tensor"),
        P("tensor", None),
        P("dp", None),
    )
    return jax.shard_map(
        on_device,
        mesh=mesh,
        in_specs=placed,
        out_specs=(
            P("dp", None),
            P("dp", None),
            P("dp", "tensor"),
            P("dp"),
            P("dp"),
            P("dp", "tensor"),
            P("dp", "tensor"),
            P("dp", "tensor"),
            P("tensor", "dp"),
            P("dp"),
            P("dp"),
            P("dp", "tensor"),
            P("tensor", "dp"),
        ),
        check_vma=False,
    )
```

```python
import functools

import jax
import jax.numpy as jnp
from jax import lax
from jax.experimental import pallas as pl
from jax.experimental.pallas import tpu as pltpu
from jax.sharding import PartitionSpec as P

HEAD_DIM = 64
SEQ_LEN = 1024
BLOCK = 256
PAIR = 2 * HEAD_DIM
EPS = 1e-05
FILL = -1e30
VMEM_BYTES = 60 * 1024 * 1024

F32 = jnp.float32
BF16 = jnp.bfloat16


def dot_nn(left, right):
    return lax.dot_general(left, right, (((1,), (0,)), ((), ())), preferred_element_type=F32)


def dot_nt(left, right):
    return lax.dot_general(left, right, (((1,), (1,)), ((), ())), preferred_element_type=F32)


def norm_stats(values_in):
    average = jnp.mean(values_in, axis=-1, keepdims=True)
    centered = values_in - average
    variance = jnp.mean(centered * centered, axis=-1, keepdims=True)
    factor = lax.rsqrt(variance + EPS)
    return centered * factor, factor


def norm_backward(grad, normed, factor, gain):
    scaled = grad * gain
    mean_plain = jnp.mean(scaled, axis=-1, keepdims=True)
    mean_cross = jnp.mean(scaled * normed, axis=-1, keepdims=True)
    return factor * (scaled - mean_plain - normed * mean_cross)


def head_masks(rows):
    lanes = lax.broadcasted_iota(jnp.int32, (rows, PAIR), 1)
    return lanes < HEAD_DIM


def split_heads(pair_rows):
    first = head_masks(pair_rows.shape[0])
    zero = jnp.zeros_like(pair_rows)
    return jnp.where(first, pair_rows, zero), jnp.where(first, zero, pair_rows)


def front_kernel(
    scal,
    x_ref,
    fv_ref,
    gain_ref,
    shift_ref,
    wq_own,
    wk_own,
    wv_own,
    wq_peer,
    wk_peer,
    wv_peer,
    sel_ref,
    n1_ref,
    q_ref,
    k_ref,
    v_ref,
    att_ref,
    lse_ref,
    w_scr,
    lse_scr,
):
    step = pl.program_id(0)
    length = x_ref.shape[0]
    blocks = length // BLOCK
    half = pl.num_programs(0) // 2

    @pl.when(step == 0)
    def _():
        lse_scr[...] = jnp.zeros_like(lse_scr)

        def one(row, carry):
            rows = pl.ds(row * BLOCK, BLOCK)
            normed, _ = norm_stats(x_ref[rows, :].astype(F32))
            n1_ref[rows, :] = (normed * gain_ref[...] + shift_ref[...]).astype(BF16)
            return carry

        lax.fori_loop(0, blocks, one, 0)

    @pl.when(step < half)
    def _():
        w_scr[:, 0:PAIR] = wq_own[...]
        w_scr[:, PAIR : 2 * PAIR] = wk_own[...]
        w_scr[:, 2 * PAIR : 3 * PAIR] = wv_own[...]

    @pl.when(step >= half)
    def _():
        w_scr[:, 0:PAIR] = wq_peer[...].astype(BF16)
        w_scr[:, PAIR : 2 * PAIR] = wk_peer[...].astype(BF16)
        w_scr[:, 2 * PAIR : 3 * PAIR] = wv_peer[...].astype(BF16)

    for block in range(blocks):
        rows = slice(block * BLOCK, (block + 1) * BLOCK)
        fused = dot_nn(n1_ref[rows, :], w_scr[...])
        picked = dot_nn(fv_ref[rows, :], sel_ref[...])
        q_ref[rows, :] = (fused[:, 0:PAIR].astype(BF16).astype(F32) * HEAD_DIM**-0.5).astype(BF16)
        k_ref[rows, :] = fused[:, PAIR : 2 * PAIR].astype(BF16)
        v_ref[rows, :] = (fused[:, 2 * PAIR :] + picked).astype(BF16)

    lane = lax.broadcasted_iota(jnp.int32, (BLOCK, PAIR), 1)
    row_pos = lax.broadcasted_iota(jnp.int32, (BLOCK, BLOCK), 0)
    col_pos = lax.broadcasted_iota(jnp.int32, (BLOCK, BLOCK), 1)
    seen = col_pos <= row_pos
    for block in range(blocks):
        lo, hi = block * BLOCK, (block + 1) * BLOCK
        queries = split_heads(q_ref[lo:hi, :])
        total = jnp.zeros((BLOCK, PAIR), F32)
        lse_tile = lse_scr[lo:hi, :]
        for head in range(2):
            diag = jnp.where(seen, dot_nt(queries[head], k_ref[lo:hi, :]), FILL)
            peak = jnp.max(diag, axis=-1, keepdims=True)
            if block:
                early = dot_nt(queries[head], k_ref[0:lo, :])
                peak = jnp.maximum(peak, jnp.max(early, axis=-1, keepdims=True))
            diag = jnp.exp(diag - peak)
            mass = jnp.sum(diag, axis=-1, keepdims=True)
            if block:
                early = jnp.exp(early - peak)
                mass = mass + jnp.sum(early, axis=-1, keepdims=True)
            inverse = 1.0 / mass
            total = total + dot_nn((diag * inverse).astype(BF16), split_heads(v_ref[lo:hi, :])[head])
            if block:
                total = total + dot_nn(
                    (early * inverse).astype(BF16), split_heads(v_ref[0:lo, :])[head]
                )
            lse_tile = jnp.where(lane == 2 * step + head, peak + jnp.log(mass), lse_tile)
        att_ref[lo:hi, :] = total.astype(BF16)
        lse_scr[lo:hi, :] = lse_tile

    @pl.when(step == pl.num_programs(0) - 1)
    def _():
        for block in range(blocks):
            lo, hi = block * BLOCK, (block + 1) * BLOCK
            lse_ref[:, lo:hi] = jnp.transpose(lse_scr[lo:hi, :])[0 : lse_ref.shape[0], :]


def front(scal, tokens, first_values, gain, shift, own, peer, select):
    width = tokens.shape[1]
    own_width = own[0].shape[1]
    heads_width = 2 * own_width
    half = own_width // PAIR
    fv_width = first_values.shape[1]
    row_block = lambda i, s: (s[0], 0)
    whole = lambda i, s: (0, 0)
    own_block = pl.BlockSpec((width, PAIR), lambda i, s: (0, jnp.minimum(i, half - 1)))
    peer_block = pl.BlockSpec((width, PAIR), lambda i, s: (0, jnp.maximum(i - half, 0)))
    pair_block = pl.BlockSpec((SEQ_LEN, PAIR), lambda i, s: (0, i))
    pair_out = jax.ShapeDtypeStruct((SEQ_LEN, heads_width), BF16)
    return pl.pallas_call(
        front_kernel,
        grid_spec=pltpu.PrefetchScalarGridSpec(
            num_scalar_prefetch=1,
            grid=(2 * half,),
            in_specs=[
                pl.BlockSpec((SEQ_LEN, width), row_block),
                pl.BlockSpec((SEQ_LEN, fv_width), row_block),
                pl.BlockSpec((1, width), whole),
                pl.BlockSpec((1, width), whole),
                own_block,
                own_block,
                own_block,
                peer_block,
                peer_block,
                peer_block,
                pl.BlockSpec((fv_width, PAIR), lambda i, s: (0, i)),
            ],
            out_specs=[
                pl.BlockSpec((SEQ_LEN, width), whole),
                pair_block,
                pair_block,
                pair_block,
                pair_block,
                pl.BlockSpec((16, SEQ_LEN), whole),
            ],
            scratch_shapes=[
                pltpu.VMEM((width, 3 * PAIR), BF16),
                pltpu.VMEM((SEQ_LEN, PAIR), F32),
            ],
        ),
        out_shape=[
            jax.ShapeDtypeStruct((SEQ_LEN, width), BF16),
            pair_out,
            pair_out,
            pair_out,
            pair_out,
            jax.ShapeDtypeStruct((16, SEQ_LEN), F32),
        ],
        compiler_params=pltpu.CompilerParams(vmem_limit_bytes=VMEM_BYTES),
        name="front",
    )(scal, tokens, first_values, gain, shift, *own, *peer, select)


def gelu_pair(upper):
    scale = (2.0 / jnp.pi) ** 0.5
    square = upper * upper
    inner = upper * (scale + (scale * 0.044715) * square)
    tanh = jnp.tanh(inner)
    cdf = 0.5 + 0.5 * tanh
    slope = cdf + 0.5 * upper * (1.0 - tanh * tanh) * (scale + (3.0 * scale * 0.044715) * square)
    return upper * cdf, slope


def middle_kernel(
    scal,
    x_ref,
    att_ref,
    cot_ref,
    gain_ref,
    shift_ref,
    wo_own,
    wo_peer,
    up_own,
    down_own,
    up_peer,
    down_peer,
    layer_ref,
    gmix_ref,
    gheads_ref,
    og_own,
    og_peer,
    ug_own,
    dg_own,
    ug_peer,
    dg_peer,
    vec_ref,
    mixed_scr,
    two_scr,
    low_scr,
    two_t,
    low_t,
    act_scr,
    gup_scr,
    gtwo_scr,
    up_scr,
    down_scr,
    wo_scr,
):
    step = pl.program_id(0)
    length, width = x_ref.shape
    blocks = length // BLOCK
    own_width = wo_own.shape[0]

    @pl.when(step == 0)
    def _():
        wo_scr[0:own_width, :] = wo_own[...]
        wo_scr[own_width:, :] = wo_peer[...].astype(BF16)
        live = jnp.where(scal[1] > 0, 1.0, 0.0).astype(F32)
        for block in range(blocks):
            rows = slice(block * BLOCK, (block + 1) * BLOCK)
            mixed = x_ref[rows, :].astype(F32) + dot_nn(att_ref[rows, :], wo_scr[...])
            mixed_scr[rows, :] = mixed
            normed, _ = norm_stats(mixed)
            two = (normed * gain_ref[...] + shift_ref[...]).astype(BF16)
            two_scr[rows, :] = two
            two_t[:, rows] = jnp.transpose(two)
            low = (cot_ref[rows, :].astype(F32) * live).astype(BF16)
            low_scr[rows, :] = low
            low_t[:, rows] = jnp.transpose(low)
            layer_ref[rows, :] = mixed
            gtwo_scr[rows, :] = jnp.zeros_like(mixed)

    @pl.when(step % 2 == 0)
    def _():
        up_scr[...] = up_peer[...].astype(BF16)
        down_scr[...] = down_peer[...].astype(BF16)

    @pl.when(step % 2 == 1)
    def _():
        up_scr[...] = up_own[...]
        down_scr[...] = down_own[...]

    for block in range(blocks):
        rows = slice(block * BLOCK, (block + 1) * BLOCK)
        upper = dot_nn(two_scr[rows, :], up_scr[...])
        active, slope = gelu_pair(upper)
        active = active.astype(BF16)
        act_scr[rows, :] = active
        layer_ref[rows, :] += dot_nn(active, down_scr[...])
        grad_upper = (dot_nt(low_scr[rows, :], down_scr[...]) * slope).astype(BF16)
        gup_scr[rows, :] = grad_upper
        gtwo_scr[rows, :] += dot_nt(grad_upper, up_scr[...])

    down_grad = dot_nn(low_t[...], act_scr[...])
    up_grad = dot_nn(two_t[...], gup_scr[...])

    @pl.when(step % 2 == 0)
    def _():
        dg_peer[...] = down_grad
        ug_peer[...] = up_grad

    @pl.when(step % 2 == 1)
    def _():
        dg_own[...] = down_grad
        ug_own[...] = up_grad

    @pl.when(step == pl.num_programs(0) - 1)
    def _():
        gain_sum = jnp.zeros((1, width), F32)
        shift_sum = jnp.zeros((1, width), F32)
        for block in range(blocks):
            rows = slice(block * BLOCK, (block + 1) * BLOCK)
            normed, factor = norm_stats(mixed_scr[rows, :])
            grad_two = gtwo_scr[rows, :]
            gain_sum += jnp.sum(grad_two * normed, axis=0, keepdims=True)
            shift_sum += jnp.sum(grad_two, axis=0, keepdims=True)
            grad_mixed = low_scr[rows, :].astype(F32) + norm_backward(
                grad_two, normed, factor, gain_ref[...]
            )
            gmix_ref[rows, :] = grad_mixed
            grad_attn = grad_mixed.astype(BF16)
            low_t[:, rows] = jnp.transpose(grad_attn)
            gheads_ref[rows, :] = dot_nt(grad_attn, wo_scr[...]).astype(BF16)
        vec_ref[...] = jnp.zeros_like(vec_ref)
        vec_ref[0:1, :] = gain_sum
        vec_ref[1:2, :] = shift_sum
        og_own[...] = dot_nn(low_t[...], att_ref[:, 0:own_width])
        og_peer[...] = dot_nn(low_t[...], att_ref[:, own_width:])


def middle(scal, tokens, attended, cotangent, gain, shift, out_own, out_peer, ups, downs):
    width = tokens.shape[1]
    own_ff = ups[0].shape[1]
    own_width = out_own.shape[0]
    ff_block = 512
    steps = 2 * (own_ff // ff_block)
    row_block = pl.BlockSpec((SEQ_LEN, width), lambda i, s: (s[0], 0))
    fixed = lambda shape: pl.BlockSpec(shape, lambda i, s: (0, 0))
    up_block = pl.BlockSpec((width, ff_block), lambda i, s: (0, i // 2))
    down_block = pl.BlockSpec((ff_block, width), lambda i, s: (i // 2, 0))
    seq_f32 = jax.ShapeDtypeStruct((SEQ_LEN, width), F32)
    grad_f32 = jax.ShapeDtypeStruct((width, own_ff), F32)
    out_f32 = jax.ShapeDtypeStruct((width, own_width), F32)
    return pl.pallas_call(
        middle_kernel,
        grid_spec=pltpu.PrefetchScalarGridSpec(
            num_scalar_prefetch=1,
            grid=(steps,),
            in_specs=[
                row_block,
                fixed((SEQ_LEN, width)),
                row_block,
                fixed((1, width)),
                fixed((1, width)),
                fixed((own_width, width)),
                fixed((own_width, width)),
                up_block,
                down_block,
                up_block,
                down_block,
            ],
            out_specs=[
                fixed((SEQ_LEN, width)),
                fixed((SEQ_LEN, width)),
                fixed((SEQ_LEN, width)),
                fixed((width, own_width)),
                fixed((width, own_width)),
                up_block,
                up_block,
                up_block,
                up_block,
                fixed((8, width)),
            ],
            scratch_shapes=[
                pltpu.VMEM((SEQ_LEN, width), F32),
                pltpu.VMEM((SEQ_LEN, width), BF16),
                pltpu.VMEM((SEQ_LEN, width), BF16),
                pltpu.VMEM((width, SEQ_LEN), BF16),
                pltpu.VMEM((width, SEQ_LEN), BF16),
                pltpu.VMEM((SEQ_LEN, ff_block), BF16),
                pltpu.VMEM((SEQ_LEN, ff_block), BF16),
                pltpu.VMEM((SEQ_LEN, width), F32),
                pltpu.VMEM((width, ff_block), BF16),
                pltpu.VMEM((ff_block, width), BF16),
                pltpu.VMEM((2 * own_width, width), BF16),
            ],
        ),
        out_shape=[
            seq_f32,
            seq_f32,
            jax.ShapeDtypeStruct((SEQ_LEN, 2 * own_width), BF16),
            out_f32,
            out_f32,
            grad_f32,
            grad_f32,
            grad_f32,
            grad_f32,
            jax.ShapeDtypeStruct((8, width), F32),
        ],
        compiler_params=pltpu.CompilerParams(vmem_limit_bytes=VMEM_BYTES),
        name="middle",
    )(scal, tokens, attended, cotangent, gain, shift, out_own, out_peer, *ups, *downs)


def back_kernel(
    scal,
    x_ref,
    n1_ref,
    q_ref,
    k_ref,
    v_ref,
    att_ref,
    gheads_ref,
    lse_ref,
    gmix_ref,
    gain_ref,
    wq_own,
    wk_own,
    wv_own,
    wq_peer,
    wk_peer,
    wv_peer,
    sel_ref,
    gin_ref,
    fvg_ref,
    grads_ref,
    vec_ref,
    n1_t,
    w_scr,
    dk_acc,
    dv_acc,
    dq_t,
    stack_scr,
    one_acc,
    fv_acc,
):
    step = pl.program_id(0)
    length, width = x_ref.shape
    blocks = length // BLOCK
    half = pl.num_programs(0) // 2

    @pl.when(step == 0)
    def _():
        for block in range(blocks):
            rows = slice(block * BLOCK, (block + 1) * BLOCK)
            n1_t[:, rows] = jnp.transpose(n1_ref[rows, :])
        one_acc[...] = jnp.zeros_like(one_acc)
        fv_acc[...] = jnp.zeros_like(fv_acc)

    @pl.when(step < half)
    def _():
        w_scr[:, 0:PAIR] = wq_own[...]
        w_scr[:, PAIR : 2 * PAIR] = wk_own[...]
        w_scr[:, 2 * PAIR : 3 * PAIR] = wv_own[...]

    @pl.when(step >= half)
    def _():
        w_scr[:, 0:PAIR] = wq_peer[...].astype(BF16)
        w_scr[:, PAIR : 2 * PAIR] = wk_peer[...].astype(BF16)
        w_scr[:, 2 * PAIR : 3 * PAIR] = wv_peer[...].astype(BF16)

    k_t = jnp.transpose(k_ref[...])
    prod_t = jnp.transpose(gheads_ref[...].astype(F32) * att_ref[...].astype(F32))
    lse_pair = lse_ref[0]
    row_pos = lax.broadcasted_iota(jnp.int32, (BLOCK, BLOCK), 0)
    col_pos = lax.broadcasted_iota(jnp.int32, (BLOCK, BLOCK), 1)
    seen = row_pos <= col_pos
    for block in range(blocks):
        cols = slice(block * BLOCK, (block + 1) * BLOCK)
        queries = split_heads(q_ref[cols, :])
        grads = split_heads(gheads_ref[cols, :])
        for head in range(2):
            part = slice(head * HEAD_DIM, (head + 1) * HEAD_DIM)
            delta = jnp.sum(prod_t[part, cols], axis=0, keepdims=True)
            lse = lse_pair[head : head + 1, cols]
            dq = jnp.zeros((HEAD_DIM, BLOCK), F32)
            for source in range(block + 1):
                rows = slice(source * BLOCK, (source + 1) * BLOCK)
                soft = jnp.exp(dot_nt(k_ref[rows, :], queries[head]) - lse)
                if source == block:
                    soft = jnp.where(seen, soft, 0.0)
                dsoft = dot_nt(v_ref[rows, :], grads[head])
                dscore = (soft * (dsoft - delta)).astype(BF16)
                dv = dot_nn(soft.astype(BF16), grads[head])
                dk = dot_nn(dscore, queries[head])
                if head == 0 and source == block:
                    dv_acc[rows, :] = dv
                    dk_acc[rows, :] = dk
                else:
                    dv_acc[rows, :] += dv
                    dk_acc[rows, :] += dk
                dq = dq + dot_nn(k_t[part, rows], dscore)
            dq_t[part, cols] = dq

    lane = lax.broadcasted_iota(jnp.int32, (BLOCK, PAIR), 1)
    for block in range(blocks):
        rows = slice(block * BLOCK, (block + 1) * BLOCK)
        stack_scr[rows, 0:PAIR] = (jnp.transpose(dq_t[:, rows]) * HEAD_DIM**-0.5).astype(BF16)
        stack_scr[rows, PAIR : 2 * PAIR] = dk_acc[rows, :].astype(BF16)
        dv = dv_acc[rows, :]
        stack_scr[rows, 2 * PAIR : 3 * PAIR] = dv.astype(BF16)
        high = dv.astype(BF16)
        low = (dv - high.astype(F32)).astype(BF16)
        fv_acc[rows, :] += dot_nt(high, sel_ref[...]) + dot_nt(low, sel_ref[...])
        one_acc[rows, :] += dot_nt(stack_scr[rows, :], w_scr[...])
    grads_ref[...] = dot_nn(n1_t[...], stack_scr[...])

    @pl.when(step == pl.num_programs(0) - 1)
    def _():
        gain_sum = jnp.zeros((1, width), F32)
        shift_sum = jnp.zeros((1, width), F32)
        for block in range(blocks):
            rows = slice(block * BLOCK, (block + 1) * BLOCK)
            normed, factor = norm_stats(x_ref[rows, :].astype(F32))
            grad_one = one_acc[rows, :]
            gain_sum += jnp.sum(grad_one * normed, axis=0, keepdims=True)
            shift_sum += jnp.sum(grad_one, axis=0, keepdims=True)
            gin_ref[rows, :] = gmix_ref[rows, :] + norm_backward(
                grad_one, normed, factor, gain_ref[...]
            )
            fvg_ref[rows, :] = fv_acc[rows, :]
        vec_ref[...] = jnp.zeros_like(vec_ref)
        vec_ref[0:1, :] = gain_sum
        vec_ref[1:2, :] = shift_sum


def back(scal, tokens, n1, q, k, v, attended, grad_heads, lse, grad_mixed, gain, own, peer, select):
    width = tokens.shape[1]
    own_width = own[0].shape[1]
    half = own_width // PAIR
    fv_width = select.shape[0]
    row_block = pl.BlockSpec((SEQ_LEN, width), lambda i, s: (s[0], 0))
    fixed = lambda shape: pl.BlockSpec(shape, lambda i, s: (0, 0))
    own_block = pl.BlockSpec((width, PAIR), lambda i, s: (0, jnp.minimum(i, half - 1)))
    peer_block = pl.BlockSpec((width, PAIR), lambda i, s: (0, jnp.maximum(i - half, 0)))
    pair_block = pl.BlockSpec((SEQ_LEN, PAIR), lambda i, s: (0, i))
    return pl.pallas_call(
        back_kernel,
        grid_spec=pltpu.PrefetchScalarGridSpec(
            num_scalar_prefetch=1,
            grid=(2 * half,),
            in_specs=[
                row_block,
                fixed((SEQ_LEN, width)),
                pair_block,
                pair_block,
                pair_block,
                pair_block,
                pair_block,
                pl.BlockSpec((1, 2, SEQ_LEN), lambda i, s: (i, 0, 0)),
                fixed((SEQ_LEN, width)),
                fixed((1, width)),
                own_block,
                own_block,
                own_block,
                peer_block,
                peer_block,
                peer_block,
                pl.BlockSpec((fv_width, PAIR), lambda i, s: (0, i)),
            ],
            out_specs=[
                fixed((SEQ_LEN, width)),
                fixed((SEQ_LEN, fv_width)),
                pl.BlockSpec((width, 3 * PAIR), lambda i, s: (0, i)),
                fixed((8, width)),
            ],
            scratch_shapes=[
                pltpu.VMEM((width, SEQ_LEN), BF16),
                pltpu.VMEM((width, 3 * PAIR), BF16),
                pltpu.VMEM((SEQ_LEN, PAIR), F32),
                pltpu.VMEM((SEQ_LEN, PAIR), F32),
                pltpu.VMEM((PAIR, SEQ_LEN), F32),
                pltpu.VMEM((SEQ_LEN, 3 * PAIR), BF16),
                pltpu.VMEM((SEQ_LEN, width), F32),
                pltpu.VMEM((SEQ_LEN, fv_width), F32),
            ],
        ),
        out_shape=[
            jax.ShapeDtypeStruct((SEQ_LEN, width), F32),
            jax.ShapeDtypeStruct((SEQ_LEN, fv_width), F32),
            jax.ShapeDtypeStruct((width, 6 * own_width), F32),
            jax.ShapeDtypeStruct((8, width), F32),
        ],
        compiler_params=pltpu.CompilerParams(vmem_limit_bytes=VMEM_BYTES),
        name="back",
    )(
        scal,
        tokens,
        n1,
        q,
        k,
        v,
        attended,
        grad_heads,
        lse,
        grad_mixed,
        gain,
        *own,
        *peer,
        select,
    )


def swap(value):
    return lax.ppermute(value, "tensor", [(0, 1), (1, 0)])


def on_device(
    tokens,
    first_values,
    seq_count,
    skip_map,
    norm1_gain,
    norm1_shift,
    query_weight,
    key_weight,
    value_weight,
    out_weight,
    norm2_gain,
    norm2_shift,
    up_weight,
    down_weight,
    cotangent,
):
    core = lax.axis_index("tensor")
    width = tokens.shape[1]
    own_width = query_weight.shape[1]
    fresh_width = value_weight.shape[1]
    skip_width = own_width - fresh_width
    fv_width = first_values.shape[1]
    half = own_width // PAIR
    scal = jnp.stack([core, (core < seq_count[0]).astype(jnp.int32)])

    value_padded = jnp.pad(value_weight, ((0, 0), (0, skip_width)))
    own = (query_weight, key_weight, value_padded)
    peer = tuple(swap(w.astype(F32)) for w in own)
    out_peer = swap(out_weight.astype(F32))
    up_peer = swap(up_weight.astype(F32))
    down_peer = swap(down_weight.astype(F32))

    maps = jnp.concatenate([skip_map, swap(skip_map)])
    target = jnp.repeat(maps, HEAD_DIM) * HEAD_DIM + jnp.tile(
        jnp.arange(HEAD_DIM), 2 * skip_width // HEAD_DIM
    )
    target = target.reshape(2, skip_width)
    target = jnp.concatenate([jnp.full((2, fresh_width), -1, jnp.int32), target], axis=1)
    select = (jnp.arange(fv_width)[:, None] == target.reshape(1, 2 * own_width)).astype(BF16)

    gain1, shift1 = norm1_gain[None, :], norm1_shift[None, :]
    gain2, shift2 = norm2_gain[None, :], norm2_shift[None, :]
    n1, q, k, v, attended, lse = front(
        scal, tokens, first_values, gain1, shift1, own, peer, select
    )
    lse = lse[0 : 4 * half].reshape(2 * half, 2, SEQ_LEN)
    (
        layer_rows,
        grad_mixed,
        grad_heads,
        og_own,
        og_peer,
        ug_own,
        dg_own,
        ug_peer,
        dg_peer,
        vec2,
    ) = middle(
        scal,
        tokens,
        attended,
        cotangent,
        gain2,
        shift2,
        out_weight,
        out_peer,
        (up_weight, down_weight),
        (up_peer, down_peer),
    )
    in_rows, fv_rows, proj_grads, vec1 = back(
        scal,
        tokens,
        n1,
        q,
        k,
        v,
        attended,
        grad_heads,
        lse,
        grad_mixed,
        gain1,
        own,
        peer,
        select,
    )
    vectors = jnp.pad(jnp.concatenate([vec1[0:2], vec2[0:2]]).T, ((0, 0), (0, 124)))
    proj_own, proj_peer = proj_grads[:, : 3 * own_width], proj_grads[:, 3 * own_width :]
    packed_own = jnp.concatenate([proj_own, og_own, ug_own, dg_own, vectors], axis=1)
    packed_peer = jnp.concatenate([proj_peer, og_peer, ug_peer, dg_peer, vectors], axis=1)
    packed = packed_own + swap(packed_peer)
    summed = lax.psum_scatter(packed, "dp", scatter_dimension=0, tiled=True)

    proj = summed[:, : 3 * own_width].reshape(-1, half, 3, PAIR)
    query_total = proj[:, :, 0].reshape(-1, own_width)
    key_total = proj[:, :, 1].reshape(-1, own_width)
    value_total = proj[:, :, 2].reshape(-1, own_width)[:, :fresh_width]
    start = 3 * own_width
    out_total = summed[:, start : start + own_width].T
    start += own_width
    ff = up_weight.shape[1]
    up_total = summed[:, start : start + ff]
    down_total = summed[:, start + ff : start + 2 * ff].T
    start += 2 * ff
    gain1_total, shift1_total, gain2_total, shift2_total = (summed[:, start + n] for n in range(4))

    def both(rows):
        other = swap(rows)
        return jnp.where(
            core == 0, jnp.concatenate([rows, other]), jnp.concatenate([other, rows])
        )

    layer_out = both(layer_rows)
    input_grad = both(in_rows)
    side = fv_width // 2
    left, right = fv_rows[:, :side], fv_rows[:, side:]
    keep = jnp.where(core == 0, left, right)
    other = swap(jnp.where(core == 0, right, left))
    first_grad = jnp.where(
        core == 0, jnp.concatenate([keep, other]), jnp.concatenate([other, keep])
    )
    return (
        layer_out,
        input_grad,
        first_grad,
        gain1_total,
        shift1_total,
        query_total,
        key_total,
        value_total,
        out_total,
        gain2_total,
        shift2_total,
        up_total,
        down_total,
    )


def solution(mesh):
    placed = (
        P("dp", None),
        P("dp", None),
        P("dp"),
        P("tensor"),
        P(),
        P(),
        P(None, "tensor"),
        P(None, "tensor"),
        P(None, "tensor"),
        P("tensor", None),
        P(),
        P(),
        P(None, "tensor"),
        P("tensor", None),
        P("dp", None),
    )
    return jax.shard_map(
        on_device,
        mesh=mesh,
        in_specs=placed,
        out_specs=(
            P("dp", None),
            P("dp", None),
            P("dp", "tensor"),
            P("dp"),
            P("dp"),
            P("dp", "tensor"),
            P("dp", "tensor"),
            P("dp", "tensor"),
            P("tensor", "dp"),
            P("dp"),
            P("dp"),
            P("dp", "tensor"),
            P("tensor", "dp"),
        ),
        check_vma=False,
    )
```

```python
import functools

import jax
import jax.numpy as jnp
from jax import lax
from jax.experimental import pallas as pl
from jax.experimental.pallas import tpu as pltpu
from jax.sharding import PartitionSpec as P

HEAD_DIM = 64
SEQ_LEN = 1024
BLOCK = 256
PAIR = 2 * HEAD_DIM
EPS = 1e-05
FILL = -1e30
VMEM_BYTES = 60 * 1024 * 1024

F32 = jnp.float32
BF16 = jnp.bfloat16


def dot_nn(left, right):
    return lax.dot_general(left, right, (((1,), (0,)), ((), ())), preferred_element_type=F32)


def dot_nt(left, right):
    return lax.dot_general(left, right, (((1,), (1,)), ((), ())), preferred_element_type=F32)


def norm_stats(values_in):
    average = jnp.mean(values_in, axis=-1, keepdims=True)
    centered = values_in - average
    variance = jnp.mean(centered * centered, axis=-1, keepdims=True)
    factor = lax.rsqrt(variance + EPS)
    return centered * factor, factor


def norm_backward(grad, normed, factor, gain):
    scaled = grad * gain
    mean_plain = jnp.mean(scaled, axis=-1, keepdims=True)
    mean_cross = jnp.mean(scaled * normed, axis=-1, keepdims=True)
    return factor * (scaled - mean_plain - normed * mean_cross)


def head_masks(rows):
    lanes = lax.broadcasted_iota(jnp.int32, (rows, PAIR), 1)
    return lanes < HEAD_DIM


def split_heads(pair_rows):
    first = head_masks(pair_rows.shape[0])
    zero = jnp.zeros_like(pair_rows)
    return jnp.where(first, pair_rows, zero), jnp.where(first, zero, pair_rows)


MESH = pl.DeviceIdType.MESH


def params(collective_id):
    return pltpu.CompilerParams(
        vmem_limit_bytes=VMEM_BYTES, collective_id=collective_id, has_side_effects=True
    )


def fixed(shape):
    zeros = (0,) * len(shape)
    return pl.BlockSpec(shape, lambda i: zeros, pipeline_mode=pl.Buffered(1))


ANY = pl.BlockSpec(memory_space=pl.ANY)
SMEM = pl.BlockSpec(memory_space=pltpu.SMEM)


def ring_of(dp_size, width):
    rows = width // dp_size
    return dp_size % 8 == 0 and width % dp_size == 0 and rows % 8 == 0


def place(ring, width, dp_size, columns):
    if not ring:
        return (width, columns)
    return (dp_size // 4, 2, 2, width // dp_size, columns)


class Link:
    def __init__(self, dp_size):
        self.dp = lax.axis_index("dp")
        self.core = lax.axis_index("tensor")
        self.depth = dp_size // 4
        self.x = lax.rem(self.dp, 2)
        self.y = lax.rem(lax.div(self.dp, 2), 2)
        self.z = lax.div(self.dp, 4)
        self.peer = {"tensor": 1 - self.core}
        self.x_side = {"dp": self.dp + 1 - 2 * self.x}
        self.y_side = {"dp": self.dp + 2 - 4 * self.y}

    def z_place(self, hop):
        return lax.rem(self.z + hop, self.depth)

    def z_side(self, hop):
        return {"dp": 4 * self.z_place(hop) + lax.rem(self.dp, 4)}

    def meet(self, partners):
        barrier = pltpu.get_barrier_semaphore()
        for partner in partners:
            pl.semaphore_signal(barrier, inc=1, device_id=partner, device_id_type=MESH)
        pl.semaphore_wait(barrier, len(partners))


def remote(source, target, sems, index, device):
    send, recv = sems
    return pltpu.make_async_remote_copy(
        src_ref=source,
        dst_ref=target,
        send_sem=send.at[index],
        recv_sem=recv.at[index],
        device_id=device,
        device_id_type=MESH,
    )


def first_hop(link, source, landing, sems, base):
    low = link.depth // 2
    return [
        remote(
            source.at[0:low, :, 1 - link.x], landing.at[0], sems, base, link.x_side
        ),
        remote(
            source.at[low : 2 * low, 1 - link.y],
            landing.at[1],
            sems,
            base + 1,
            link.y_side,
        ),
    ]


def second_hop(link, source, landing, sems, base):
    low = link.depth // 2
    return [
        remote(
            source.at[0, :, 1 - link.y],
            landing.at[0:low],
            sems,
            base,
            link.y_side,
        ),
        remote(
            source.at[1, :, 1 - link.x],
            landing.at[low : 2 * low],
            sems,
            base + 1,
            link.x_side,
        ),
    ]


def last_hop(link, source, landing, sems, base):
    return [
        remote(
            source.at[link.z_place(hop)],
            landing.at[hop - 1],
            sems,
            base + hop - 1,
            link.z_side(hop),
        )
        for hop in range(1, link.depth)
    ]


def go(copies):
    for copy in copies:
        copy.start()


def finish(copies):
    for copy in copies:
        copy.wait()


def merge_first(link, whole, landing):
    low = link.depth // 2
    for row in range(low):
        for other in range(2):
            landing[0, row, other] += whole[row, other, link.x]
            landing[1, row, other] += whole[low + row, link.y, other]


def merge_second(link, landed, landing):
    low = link.depth // 2
    for row in range(low):
        landing[row] += landed[0, row, link.y]
        landing[low + row] += landed[1, row, link.x]


def total_last(own, landing):
    total = own
    for hop in range(landing.shape[0]):
        total = total + landing[hop]
    return total


def front_kernel(
    dp_size,
    tokens,
    first_values,
    skip_map,
    gain_ref,
    shift_ref,
    wq_ref,
    wk_ref,
    wv_ref,
    out_w,
    up_w,
    down_w,
    n1_ref,
    q_ref,
    k_ref,
    v_ref,
    att_ref,
    lse_ref,
    w_ref,
    sel_ref,
    out_peer,
    up_peer,
    down_peer,
    x_scr,
    fv_scr,
    proj_own,
    proj_send,
    proj_recv,
    sel_send,
    sel_recv,
    out_low,
    up_low,
    down_low,
    out_send,
    up_send,
    down_send,
    lse_scr,
    local_sem,
    send_sem,
    recv_sem,
):
    step = pl.program_id(0)
    length, width = x_scr.shape
    blocks = length // BLOCK
    half = pl.num_programs(0) // 2
    own_width = wq_ref.shape[1]
    fresh_width = wv_ref.shape[1]
    fv_width = fv_scr.shape[1]
    link = Link(dp_size)
    sems = (send_sem, recv_sem)
    rows_here = pl.ds(link.core * length, length)
    local = [
        pltpu.make_async_copy(tokens.at[rows_here], x_scr, local_sem.at[0]),
        pltpu.make_async_copy(first_values.at[rows_here], fv_scr, local_sem.at[1]),
        pltpu.make_async_copy(up_w, up_low, local_sem.at[2]),
        pltpu.make_async_copy(down_w, down_low, local_sem.at[3]),
        pltpu.make_async_copy(out_w, out_low, local_sem.at[4]),
    ]
    early = [
        remote(proj_send, proj_recv, sems, 0, link.peer),
        remote(sel_send, sel_recv, sems, 1, link.peer),
    ]
    late = [
        remote(up_send, up_peer, sems, 2, link.peer),
        remote(down_send, down_peer, sems, 3, link.peer),
        remote(out_send, out_peer, sems, 4, link.peer),
    ]

    @pl.when(step == 0)
    def _():
        go(local)
        proj_own[0] = wq_ref[...]
        proj_own[1] = wk_ref[...]
        proj_own[2] = jnp.zeros_like(wq_ref)
        proj_own[2, :, 0:fresh_width] = wv_ref[...]
        proj_send[...] = proj_own[...].astype(F32)
        row = lax.broadcasted_iota(jnp.int32, (fv_width, own_width), 0)
        col = lax.broadcasted_iota(jnp.int32, (fv_width, own_width), 1)
        slots = (own_width - fresh_width) // HEAD_DIM
        target = jnp.full((fv_width, own_width), -1, jnp.int32)
        for slot in range(slots):
            start = fresh_width + slot * HEAD_DIM
            inside = jnp.logical_and(col >= start, col < start + HEAD_DIM)
            target = jnp.where(inside, skip_map[slot] * HEAD_DIM + col - start, target)
        chosen = jnp.where(row == target, 1.0, 0.0).astype(F32)
        sel_send[...] = chosen
        sel_ref[:, 0:own_width] = chosen.astype(BF16)
        link.meet([link.peer])
        go(early)
        lse_scr[...] = jnp.zeros_like(lse_scr)
        local[0].wait()
        local[1].wait()

        def one(block, carry):
            rows = pl.ds(block * BLOCK, BLOCK)
            normed, _ = norm_stats(x_scr[rows, :].astype(F32))
            n1_ref[rows, :] = (normed * gain_ref[...] + shift_ref[...]).astype(BF16)
            return carry

        lax.fori_loop(0, blocks, one, 0)

    @pl.when(step == half)
    def _():
        finish(early)
        sel_ref[:, own_width:] = sel_recv[...].astype(BF16)

    @pl.when(step < half)
    def _():
        cols = pl.ds(pl.multiple_of(step * PAIR, PAIR), PAIR)
        for part in range(3):
            w_ref[:, part * PAIR : (part + 1) * PAIR] = proj_own[part, :, cols]

    @pl.when(step >= half)
    def _():
        cols = pl.ds(pl.multiple_of((step - half) * PAIR, PAIR), PAIR)
        for part in range(3):
            w_ref[:, part * PAIR : (part + 1) * PAIR] = proj_recv[part, :, cols].astype(BF16)

    sel_cols = pl.ds(pl.multiple_of(step * PAIR, PAIR), PAIR)
    for block in range(blocks):
        rows = slice(block * BLOCK, (block + 1) * BLOCK)
        fused = dot_nn(n1_ref[rows, :], w_ref[...])
        picked = dot_nn(fv_scr[rows, :], sel_ref[:, sel_cols])
        q_ref[rows, :] = (fused[:, 0:PAIR].astype(BF16).astype(F32) * HEAD_DIM**-0.5).astype(BF16)
        k_ref[rows, :] = fused[:, PAIR : 2 * PAIR].astype(BF16)
        v_ref[rows, :] = (fused[:, 2 * PAIR :] + picked).astype(BF16)

    lane = lax.broadcasted_iota(jnp.int32, (BLOCK, PAIR), 1)
    row_pos = lax.broadcasted_iota(jnp.int32, (BLOCK, BLOCK), 0)
    col_pos = lax.broadcasted_iota(jnp.int32, (BLOCK, BLOCK), 1)
    seen = col_pos <= row_pos
    for block in range(blocks):
        lo, hi = block * BLOCK, (block + 1) * BLOCK
        queries = split_heads(q_ref[lo:hi, :])
        total = jnp.zeros((BLOCK, PAIR), F32)
        lse_tile = lse_scr[lo:hi, :]
        for head in range(2):
            diag = jnp.where(seen, dot_nt(queries[head], k_ref[lo:hi, :]), FILL)
            peak = jnp.max(diag, axis=-1, keepdims=True)
            if block:
                past = dot_nt(queries[head], k_ref[0:lo, :])
                peak = jnp.maximum(peak, jnp.max(past, axis=-1, keepdims=True))
            diag = jnp.exp(diag - peak)
            mass = jnp.sum(diag, axis=-1, keepdims=True)
            if block:
                past = jnp.exp(past - peak)
                mass = mass + jnp.sum(past, axis=-1, keepdims=True)
            inverse = 1.0 / mass
            total = total + dot_nn((diag * inverse).astype(BF16), split_heads(v_ref[lo:hi, :])[head])
            if block:
                total = total + dot_nn(
                    (past * inverse).astype(BF16), split_heads(v_ref[0:lo, :])[head]
                )
            lse_tile = jnp.where(lane == 2 * step + head, peak + jnp.log(mass), lse_tile)
        att_ref[lo:hi, :] = total.astype(BF16)
        lse_scr[lo:hi, :] = lse_tile

    @pl.when(step == 0)
    def _():
        for copy in local[2:]:
            copy.wait()
        up_send[...] = up_low[...].astype(F32)
        down_send[...] = down_low[...].astype(F32)
        out_send[...] = out_low[...].astype(F32)
        go(late)

    @pl.when(step == pl.num_programs(0) - 1)
    def _():
        for block in range(blocks):
            lo, hi = block * BLOCK, (block + 1) * BLOCK
            lse_ref[:, lo:hi] = jnp.transpose(lse_scr[lo:hi, :])[0 : lse_ref.shape[0], :]
        finish(late)


def front(dp_size, tokens, first_values, skip_map, gain, shift, wq, wk, wv, out_w, up_w, down_w):
    width = tokens.shape[1]
    own_width = wq.shape[1]
    half = own_width // PAIR
    fv_width = first_values.shape[1]
    pair_block = pl.BlockSpec((SEQ_LEN, PAIR), lambda i: (0, i))
    pair_out = jax.ShapeDtypeStruct((SEQ_LEN, 2 * own_width), BF16)
    return pl.pallas_call(
        functools.partial(front_kernel, dp_size),
        grid=(2 * half,),
        in_specs=[
            ANY,
            ANY,
            SMEM,
            fixed((1, width)),
            fixed((1, width)),
            fixed(wq.shape),
            fixed(wk.shape),
            fixed(wv.shape),
            ANY,
            ANY,
            ANY,
        ],
        out_specs=[
            fixed((SEQ_LEN, width)),
            pair_block,
            pair_block,
            pair_block,
            pair_block,
            fixed((16, SEQ_LEN)),
            pl.BlockSpec((width, 3 * PAIR), lambda i: (0, i)),
            fixed((fv_width, 2 * own_width)),
            ANY,
            ANY,
            ANY,
        ],
        scratch_shapes=[
            pltpu.VMEM((SEQ_LEN, width), BF16),
            pltpu.VMEM((SEQ_LEN, fv_width), BF16),
            pltpu.VMEM((3, width, own_width), BF16),
            pltpu.VMEM((3, width, own_width), F32),
            pltpu.VMEM((3, width, own_width), F32),
            pltpu.VMEM((fv_width, own_width), F32),
            pltpu.VMEM((fv_width, own_width), F32),
            pltpu.VMEM(out_w.shape, BF16),
            pltpu.VMEM(up_w.shape, BF16),
            pltpu.VMEM(down_w.shape, BF16),
            pltpu.VMEM(out_w.shape, F32),
            pltpu.VMEM(up_w.shape, F32),
            pltpu.VMEM(down_w.shape, F32),
            pltpu.VMEM((SEQ_LEN, PAIR), F32),
            pltpu.SemaphoreType.DMA((5,)),
            pltpu.SemaphoreType.DMA((5,)),
            pltpu.SemaphoreType.DMA((5,)),
        ],
        out_shape=[
            jax.ShapeDtypeStruct((SEQ_LEN, width), BF16),
            pair_out,
            pair_out,
            pair_out,
            pair_out,
            jax.ShapeDtypeStruct((16, SEQ_LEN), F32),
            jax.ShapeDtypeStruct((width, 6 * own_width), BF16),
            jax.ShapeDtypeStruct((fv_width, 2 * own_width), BF16),
            jax.ShapeDtypeStruct(out_w.shape, F32),
            jax.ShapeDtypeStruct(up_w.shape, F32),
            jax.ShapeDtypeStruct(down_w.shape, F32),
        ],
        compiler_params=params(0),
        name="front",
    )(tokens, first_values, skip_map, gain, shift, wq, wk, wv, out_w, up_w, down_w)


def gelu_pair(upper):
    scale = (2.0 / jnp.pi) ** 0.5
    square = upper * upper
    inner = upper * (scale + (scale * 0.044715) * square)
    tanh = jnp.tanh(inner)
    cdf = 0.5 + 0.5 * tanh
    slope = cdf + 0.5 * upper * (1.0 - tanh * tanh) * (scale + (3.0 * scale * 0.044715) * square)
    return upper * cdf, slope


def middle_kernel(
    dp_size,
    ring,
    tokens,
    att_ref,
    cotangent,
    seq_count,
    gain_ref,
    shift_ref,
    wo_own,
    wo_peer,
    up_own,
    down_own,
    up_peer,
    down_peer,
    layer_out,
    gmix_out,
    gheads_ref,
    og_own,
    og_peer,
    vec_ref,
    exports,
    mixed_scr,
    layer_scr,
    gtwo_scr,
    two_scr,
    low_scr,
    two_t,
    low_t,
    act_scr,
    gup_scr,
    up_scr,
    down_scr,
    wo_scr,
    post_scr,
    grad_scr,
    hop1_scr,
    hop2_scr,
    local_sem,
    send_sem,
    recv_sem,
):
    step = pl.program_id(0)
    steps = pl.num_programs(0)
    length, width = mixed_scr.shape
    blocks = length // BLOCK
    own_width = wo_own.shape[0]
    ff_block = up_own.shape[1]
    chunks = grad_scr.shape[0]
    link = Link(dp_size)
    sems = (send_sem, recv_sem)
    rows_here = pl.ds(link.core * length, length)
    x_ref = gheads_ref
    loads = [
        pltpu.make_async_copy(tokens.at[rows_here], x_ref, local_sem.at[0]),
        pltpu.make_async_copy(cotangent.at[rows_here], low_scr, local_sem.at[1]),
    ]
    layer_local = pltpu.make_async_copy(layer_scr, layer_out.at[rows_here], local_sem.at[2])
    layer_send = remote(layer_scr, layer_out.at[rows_here], sems, 0, link.peer)
    swaps = [
        remote(post_scr, grad_scr.at[chunk], sems, 1 + chunk, link.peer) for chunk in range(chunks)
    ]
    if ring:
        base = 1 + chunks
        one = [
            first_hop(link, grad_scr.at[chunk], hop1_scr.at[chunk], sems, base + 2 * chunk)
            for chunk in range(2)
        ]
        two = second_hop(link, hop1_scr.at[0], hop2_scr, sems, base + 4)

    @pl.when(step == 0)
    def _():
        go(loads)
        wo_scr[0:own_width, :] = wo_own[...]
        wo_scr[own_width:, :] = wo_peer[...].astype(BF16)
        partners = [link.peer]
        if ring:
            partners += [link.x_side, link.y_side]
        link.meet(partners)
        finish(loads)
        live = jnp.where(link.core < seq_count[0], 1.0, 0.0).astype(F32)
        for block in range(blocks):
            rows = slice(block * BLOCK, (block + 1) * BLOCK)
            mixed = x_ref[rows, :].astype(F32) + dot_nn(att_ref[rows, :], wo_scr[...])
            mixed_scr[rows, :] = mixed
            normed, _ = norm_stats(mixed)
            two_low = (normed * gain_ref[...] + shift_ref[...]).astype(BF16)
            two_scr[rows, :] = two_low
            two_t[:, rows] = jnp.transpose(two_low)
            low = (low_scr[rows, :].astype(F32) * live).astype(BF16)
            low_scr[rows, :] = low
            low_t[:, rows] = jnp.transpose(low)
            layer_scr[rows, :] = mixed
            gtwo_scr[rows, :] = jnp.zeros_like(mixed)

    @pl.when(step % 2 == 0)
    def _():
        up_scr[...] = up_peer[...].astype(BF16)
        down_scr[...] = down_peer[...].astype(BF16)

    @pl.when(step % 2 == 1)
    def _():
        up_scr[...] = up_own[...]
        down_scr[...] = down_own[...]

    for block in range(blocks):
        rows = slice(block * BLOCK, (block + 1) * BLOCK)
        upper = dot_nn(two_scr[rows, :], up_scr[...])
        active, slope = gelu_pair(upper)
        active = active.astype(BF16)
        act_scr[rows, :] = active
        layer_scr[rows, :] += dot_nn(active, down_scr[...])
        grad_upper = (dot_nt(low_scr[rows, :], down_scr[...]) * slope).astype(BF16)
        gup_scr[rows, :] = grad_upper
        gtwo_scr[rows, :] += dot_nt(grad_upper, up_scr[...])

    block_shape = grad_scr.shape[1:-1] + (ff_block,)
    for chunk in range(chunks):

        @pl.when(step == 2 * chunk)
        def _():
            if chunk:
                swaps[chunk - 1].wait_send()
            post_scr[..., 0:ff_block] = dot_nn(low_t[...], act_scr[...]).reshape(block_shape)
            post_scr[..., ff_block:] = dot_nn(two_t[...], gup_scr[...]).reshape(block_shape)
            swaps[chunk].start()

        @pl.when(step == 2 * chunk + 1)
        def _():
            swaps[chunk].wait_recv()
            grad_scr[chunk, ..., 0:ff_block] += dot_nn(low_t[...], act_scr[...]).reshape(
                block_shape
            )
            grad_scr[chunk, ..., ff_block:] += dot_nn(two_t[...], gup_scr[...]).reshape(
                block_shape
            )
            if ring and chunk < 2:
                go(one[chunk])
            if ring and chunk == 1:
                finish(one[0])
                merge_first(link, grad_scr.at[0], hop1_scr.at[0])
                go(two)
            if chunk == chunks - 1:
                swaps[chunk].wait_send()

    @pl.when(step == steps - 1)
    def _():
        layer_local.start()
        layer_send.start()
        if not ring:
            outs = [
                pltpu.make_async_copy(grad_scr, exports[0], local_sem.at[3]),
            ]
            go(outs)
        else:
            outs = [
                pltpu.make_async_copy(grad_scr.at[chunks - 1], exports[2], local_sem.at[3]),
                pltpu.make_async_copy(hop1_scr.at[1], exports[1], local_sem.at[4]),
                pltpu.make_async_copy(hop2_scr, exports[0], local_sem.at[5]),
            ]
            outs[0].start()
        gain_sum = jnp.zeros((1, width), F32)
        shift_sum = jnp.zeros((1, width), F32)
        for block in range(blocks):
            rows = slice(block * BLOCK, (block + 1) * BLOCK)
            normed, factor = norm_stats(mixed_scr[rows, :])
            grad_two = gtwo_scr[rows, :]
            gain_sum += jnp.sum(grad_two * normed, axis=0, keepdims=True)
            shift_sum += jnp.sum(grad_two, axis=0, keepdims=True)
            grad_mixed = low_scr[rows, :].astype(F32) + norm_backward(
                grad_two, normed, factor, gain_ref[...]
            )
            mixed_scr[rows, :] = grad_mixed
            grad_attn = grad_mixed.astype(BF16)
            low_t[:, rows] = jnp.transpose(grad_attn)
            gheads_ref[rows, :] = dot_nt(grad_attn, wo_scr[...]).astype(BF16)
        gmix_copy = pltpu.make_async_copy(mixed_scr, gmix_out, local_sem.at[6])
        gmix_copy.start()
        vec_ref[...] = jnp.zeros_like(vec_ref)
        vec_ref[0:1, :] = gain_sum
        vec_ref[1:2, :] = shift_sum
        og_own[...] = dot_nn(low_t[...], att_ref[:, 0:own_width]).reshape(og_own.shape)
        og_peer[...] = dot_nn(low_t[...], att_ref[:, own_width:]).reshape(og_peer.shape)
        if ring:
            finish(two)
            merge_second(link, hop1_scr.at[0], hop2_scr)
            outs[2].start()
            finish(one[1])
            merge_first(link, grad_scr.at[1], hop1_scr.at[1])
            outs[1].start()
        finish(outs)
        gmix_copy.wait()
        layer_local.wait()
        layer_send.wait()


def middle(
    dp_size, ring, tokens, attended, cotangent, seq_count, gain, shift, wo_own, wo_peer, own, peer
):
    width = tokens.shape[1]
    own_ff = own[0].shape[1]
    own_width = wo_own.shape[0]
    chunks = 3
    ff_block = own_ff // chunks
    up_block = pl.BlockSpec((width, ff_block), lambda i: (0, i // 2))
    down_block = pl.BlockSpec((ff_block, width), lambda i: (i // 2, 0))
    grad_shape = place(ring, width, dp_size, 2 * ff_block)
    og_shape = place(ring, width, dp_size, own_width)
    if ring:
        depth, rows = dp_size // 4, width // dp_size
        hop1_shape = (2, 2, depth // 2, 2, rows, 2 * ff_block)
        hop2_shape = (depth, rows, 2 * ff_block)
        export_shapes = [hop2_shape, hop1_shape[1:], grad_shape]
    else:
        hop1_shape = hop2_shape = (8, 128)
        export_shapes = [(chunks,) + grad_shape]

    def body(*refs):
        fixed_outs = 18
        exports = refs[fixed_outs : fixed_outs + len(export_shapes)]
        rest = refs[fixed_outs + len(export_shapes) :]
        middle_kernel(dp_size, ring, *refs[:fixed_outs], exports, *rest)

    return pl.pallas_call(
        body,
        grid=(2 * chunks,),
        in_specs=[
            ANY,
            fixed((SEQ_LEN, 2 * own_width)),
            ANY,
            SMEM,
            fixed((1, width)),
            fixed((1, width)),
            fixed((own_width, width)),
            fixed((own_width, width)),
            up_block,
            down_block,
            up_block,
            down_block,
        ],
        out_specs=[
            ANY,
            ANY,
            fixed((SEQ_LEN, 2 * own_width)),
            fixed(og_shape),
            fixed(og_shape),
            fixed((8, width)),
        ]
        + [ANY] * len(export_shapes),
        scratch_shapes=[
            pltpu.VMEM((SEQ_LEN, width), F32),
            pltpu.VMEM((SEQ_LEN, width), F32),
            pltpu.VMEM((SEQ_LEN, width), F32),
            pltpu.VMEM((SEQ_LEN, width), BF16),
            pltpu.VMEM((SEQ_LEN, width), BF16),
            pltpu.VMEM((width, SEQ_LEN), BF16),
            pltpu.VMEM((width, SEQ_LEN), BF16),
            pltpu.VMEM((SEQ_LEN, ff_block), BF16),
            pltpu.VMEM((SEQ_LEN, ff_block), BF16),
            pltpu.VMEM((width, ff_block), BF16),
            pltpu.VMEM((ff_block, width), BF16),
            pltpu.VMEM((2 * own_width, width), BF16),
            pltpu.VMEM(grad_shape, F32),
            pltpu.VMEM((chunks,) + grad_shape, F32),
            pltpu.VMEM(hop1_shape, F32),
            pltpu.VMEM(hop2_shape, F32),
            pltpu.SemaphoreType.DMA((7,)),
            pltpu.SemaphoreType.DMA((7 + chunks,)),
            pltpu.SemaphoreType.DMA((7 + chunks,)),
        ],
        out_shape=[
            jax.ShapeDtypeStruct((2 * SEQ_LEN, width), F32),
            jax.ShapeDtypeStruct((SEQ_LEN, width), F32),
            jax.ShapeDtypeStruct((SEQ_LEN, 2 * own_width), BF16),
            jax.ShapeDtypeStruct(og_shape, F32),
            jax.ShapeDtypeStruct(og_shape, F32),
            jax.ShapeDtypeStruct((8, width), F32),
        ]
        + [jax.ShapeDtypeStruct(shape, F32) for shape in export_shapes],
        compiler_params=params(1),
        name="middle",
    )(tokens, attended, cotangent, seq_count, gain, shift, wo_own, wo_peer, *own, *peer)


HOPS = 7


class Chunk:
    def __init__(self, link, sems, base, whole=None, hop1=None, hop2=None, hop3=None):
        self.link, self.whole, self.hop1, self.hop2, self.hop3 = link, whole, hop1, hop2, hop3
        self.sems, self.base = sems, base

    def one(self, source=None):
        source = self.whole if source is None else source
        return first_hop(self.link, source, self.hop1, self.sems, self.base)

    def two(self, source=None):
        source = self.hop1 if source is None else source
        return second_hop(self.link, source, self.hop2, self.sems, self.base + 2)

    def three(self, source=None):
        source = self.hop2 if source is None else source
        return last_hop(self.link, source, self.hop3, self.sems, self.base + 4)

    def from_one(self):
        finish(self.one())
        merge_first(self.link, self.whole, self.hop1)
        go(self.two())

    def from_two(self):
        finish(self.two())
        merge_second(self.link, self.hop1, self.hop2)
        go(self.three())

    def from_three(self):
        finish(self.three())
        return total_last(self.hop2[self.link.z], self.hop3)


def back_kernel(
    dp_size,
    ring,
    counts,
    *refs,
):
    n_in, n_out = counts
    (
        tokens,
        n1_ref,
        q_ref,
        k_ref,
        v_ref,
        att_ref,
        gheads_ref,
        lse_ref,
        gmix,
        gain_ref,
        w_ref,
        sel_ref,
        og_own,
        og_peer,
        vec2_ref,
    ) = refs[:15]
    exports = refs[15:n_in]
    in_grad, first_grad = refs[n_in : n_in + 2]
    outs = refs[n_in + 2 : n_in + n_out]
    scratch = refs[n_in + n_out :]
    (
        x_scr,
        gmix_scr,
        n1_t,
        dk_acc,
        dv_acc,
        dq_t,
        stack_scr,
        one_acc,
        fv_acc,
        fv_send,
        fv_keep,
        post_scr,
        grad_scr,
        out_scr,
        local_sem,
        send_sem,
        recv_sem,
    ) = scratch[:17]
    ring_scr = scratch[17:]
    step = pl.program_id(0)
    steps = pl.num_programs(0)
    length, width = x_scr.shape
    blocks = length // BLOCK
    link = Link(dp_size)
    sems = (send_sem, recv_sem)
    rows_here = pl.ds(link.core * length, length)
    chunks = grad_scr.shape[0]
    side = fv_send.shape[1]
    loads = [
        pltpu.make_async_copy(tokens.at[rows_here], x_scr, local_sem.at[0]),
        pltpu.make_async_copy(gmix, gmix_scr, local_sem.at[1]),
        pltpu.make_async_copy(og_own, out_scr.at[0], local_sem.at[2]),
    ]
    out_swap = remote(og_peer, out_scr.at[1], sems, 0, link.peer)
    swaps = [
        remote(post_scr, grad_scr.at[chunk], sems, 1 + chunk, link.peer) for chunk in range(chunks)
    ]
    base = 1 + chunks
    in_send = remote(one_acc, in_grad.at[rows_here], sems, base, link.peer)
    in_local = pltpu.make_async_copy(one_acc, in_grad.at[rows_here], local_sem.at[3])
    first_send = remote(fv_send, first_grad.at[rows_here], sems, base + 1, link.peer)
    first_local = pltpu.make_async_copy(fv_keep, first_grad.at[rows_here], local_sem.at[7])
    base += 2
    if ring:
        (
            c0_own,
            c0_hop3,
            c1_own,
            c1_hop2,
            c1_hop3,
            c2_whole,
            c2_hop1,
            c2_hop2,
            c2_hop3,
            o_hop1,
            o_hop2,
            o_hop3,
            p_hop1,
            p_hop2,
            p_hop3,
            v_whole,
            v_recv,
            v_hop1,
            v_hop2,
            v_hop3,
            v_send,
        ) = ring_scr
        c0 = Chunk(link, sems, base, hop3=c0_hop3)
        c1 = Chunk(link, sems, base + HOPS, hop1=c1_own, hop2=c1_hop2, hop3=c1_hop3)
        c2 = Chunk(link, sems, base + 2 * HOPS, c2_whole, c2_hop1, c2_hop2, c2_hop3)
        out = Chunk(link, sems, base + 3 * HOPS, out_scr.at[0], o_hop1, o_hop2, o_hop3)
        proj = [
            Chunk(
                link,
                sems,
                base + (4 + chunk) * HOPS,
                grad_scr.at[chunk],
                p_hop1.at[chunk],
                p_hop2.at[chunk],
                p_hop3.at[chunk],
            )
            for chunk in range(chunks)
        ]
        vec = Chunk(link, sems, base + (4 + chunks) * HOPS, v_whole, v_hop1, v_hop2, v_hop3)
        vec_swap = remote(v_send, v_recv, sems, base + (5 + chunks) * HOPS, link.peer)
        ring_loads = [
            pltpu.make_async_copy(exports[0].at[link.z], c0_own, local_sem.at[4]),
            pltpu.make_async_copy(exports[1], c1_own, local_sem.at[5]),
            pltpu.make_async_copy(exports[2], c2_whole, local_sem.at[6]),
        ]

    @pl.when(step == 0)
    def _():
        partners = [link.peer]
        if ring:
            partners += [link.x_side, link.y_side]
            partners += [link.z_side(hop) for hop in range(1, link.depth)]
        link.meet(partners)
        if ring:
            go(c1.two(exports[1]))
            go(c2.one(exports[2]))
            go(c0.three(exports[0]))
        out_swap.start()
        go(loads)
        if ring:
            go(ring_loads)
        for block in range(blocks):
            rows = slice(block * BLOCK, (block + 1) * BLOCK)
            n1_t[:, rows] = jnp.transpose(n1_ref[rows, :])
        one_acc[...] = jnp.zeros_like(one_acc)
        fv_acc[...] = jnp.zeros_like(fv_acc)

    k_t = jnp.transpose(k_ref[...])
    prod_t = jnp.transpose(gheads_ref[...].astype(F32) * att_ref[...].astype(F32))
    lse_pair = lse_ref[0]
    row_pos = lax.broadcasted_iota(jnp.int32, (BLOCK, BLOCK), 0)
    col_pos = lax.broadcasted_iota(jnp.int32, (BLOCK, BLOCK), 1)
    seen = row_pos <= col_pos
    for block in range(blocks):
        cols = slice(block * BLOCK, (block + 1) * BLOCK)
        queries = split_heads(q_ref[cols, :])
        grads = split_heads(gheads_ref[cols, :])
        for head in range(2):
            part = slice(head * HEAD_DIM, (head + 1) * HEAD_DIM)
            delta = jnp.sum(prod_t[part, cols], axis=0, keepdims=True)
            lse = lse_pair[head : head + 1, cols]
            dq = jnp.zeros((HEAD_DIM, BLOCK), F32)
            for source in range(block + 1):
                rows = slice(source * BLOCK, (source + 1) * BLOCK)
                soft = jnp.exp(dot_nt(k_ref[rows, :], queries[head]) - lse)
                if source == block:
                    soft = jnp.where(seen, soft, 0.0)
                dsoft = dot_nt(v_ref[rows, :], grads[head])
                dscore = (soft * (dsoft - delta)).astype(BF16)
                dv = dot_nn(soft.astype(BF16), grads[head])
                dk = dot_nn(dscore, queries[head])
                if head == 0 and source == block:
                    dv_acc[rows, :] = dv
                    dk_acc[rows, :] = dk
                else:
                    dv_acc[rows, :] += dv
                    dk_acc[rows, :] += dk
                dq = dq + dot_nn(k_t[part, rows], dscore)
            dq_t[part, cols] = dq

    for block in range(blocks):
        rows = slice(block * BLOCK, (block + 1) * BLOCK)
        stack_scr[rows, 0:PAIR] = (jnp.transpose(dq_t[:, rows]) * HEAD_DIM**-0.5).astype(BF16)
        stack_scr[rows, PAIR : 2 * PAIR] = dk_acc[rows, :].astype(BF16)
        dv = dv_acc[rows, :]
        stack_scr[rows, 2 * PAIR : 3 * PAIR] = dv.astype(BF16)
        high = dv.astype(BF16)
        low = (dv - high.astype(F32)).astype(BF16)
        fv_acc[rows, :] += dot_nt(high, sel_ref[...]) + dot_nt(low, sel_ref[...])
        one_acc[rows, :] += dot_nt(stack_scr[rows, :], w_ref[...])

    grad_shape = grad_scr.shape[1:]
    for chunk in range(chunks):

        @pl.when(step == 2 * chunk)
        def _():
            if chunk:
                swaps[chunk - 1].wait_send()
            post_scr[...] = dot_nn(n1_t[...], stack_scr[...]).reshape(grad_shape)
            swaps[chunk].start()

        @pl.when(step == 2 * chunk + 1)
        def _():
            swaps[chunk].wait_recv()
            grad_scr[chunk] += dot_nn(n1_t[...], stack_scr[...]).reshape(grad_shape)
            if ring:
                go(proj[chunk].one())
            if chunk == chunks - 1:
                swaps[chunk].wait_send()

    @pl.when(step == 0)
    def _():
        out_swap.wait()
        finish(loads)
        out_scr[0] += out_scr[1]
        if ring:
            finish(ring_loads)
            go(out.one())

    if ring:

        @pl.when(step == 1)
        def _():
            finish(c1.two(exports[1]))
            merge_second(link, c1_own, c1_hop2)
            go(c1.three())
            finish(c2.one(exports[2]))
            merge_first(link, c2_whole, c2_hop1)
            go(c2.two())

        @pl.when(step == 2)
        def _():
            out.from_one()

        @pl.when(step == 3)
        def _():
            c2.from_two()

        @pl.when(step == 4)
        def _():
            proj[0].from_one()
            out.from_two()

    @pl.when(step == steps - 1)
    def _():
        if ring:
            proj[1].from_one()
            proj[0].from_two()
        gain_sum = jnp.zeros((1, width), F32)
        shift_sum = jnp.zeros((1, width), F32)
        for block in range(blocks):
            rows = slice(block * BLOCK, (block + 1) * BLOCK)
            normed, factor = norm_stats(x_scr[rows, :].astype(F32))
            grad_one = one_acc[rows, :]
            gain_sum += jnp.sum(grad_one * normed, axis=0, keepdims=True)
            shift_sum += jnp.sum(grad_one, axis=0, keepdims=True)
            one_acc[rows, :] = gmix_scr[rows, :] + norm_backward(
                grad_one, normed, factor, gain_ref[...]
            )
        in_local.start()
        in_send.start()
        left, right = fv_acc[:, 0:side], fv_acc[:, side:]
        fv_send[...] = jnp.where(link.core == 0, right, left)
        fv_keep[...] = jnp.where(link.core == 0, left, right)
        first_send.start()
        first_local.start()
        vectors = jnp.concatenate(
            [gain_sum, shift_sum, vec2_ref[0:2, :], jnp.zeros((4, width), F32)], axis=0
        )
        if ring:
            ffn_up, ffn_down, q_out, k_out, v_out, o_out, vec_out = outs
            rows_dev = width // dp_size
            depth = dp_size // 4
            v_send[...] = jnp.zeros_like(v_send)
            for block in range(dp_size):
                v_send[block // 4, (block // 2) % 2, block % 2, :, 0:rows_dev] = vectors[
                    :, block * rows_dev : (block + 1) * rows_dev
                ]
            vec_swap.start()
            vec_swap.wait()
            v_whole[...] = v_send[...] + v_recv[...]
            go(vec.one())
            proj[1].from_two()
            proj[2].from_one()
            vec.from_one()
            ff_block = ffn_up.shape[1] // 3

            def put_ffn(index, total):
                ffn_down[index * ff_block : (index + 1) * ff_block, :] = jnp.transpose(
                    total[:, 0:ff_block]
                )
                ffn_up[:, index * ff_block : (index + 1) * ff_block] = total[:, ff_block:]

            def put_proj(index, total):
                cols = slice(index * PAIR, (index + 1) * PAIR)
                q_out[:, cols] = total[:, 0:PAIR]
                k_out[:, cols] = total[:, PAIR : 2 * PAIR]
                v_out[:, cols] = total[:, 2 * PAIR :]

            finish(c0.three(exports[0]))
            put_ffn(0, total_last(c0_own[...], c0_hop3))
            put_ffn(1, c1.from_three())
            put_ffn(2, c2.from_three())
            o_out[...] = jnp.transpose(out.from_three())
            put_proj(0, proj[0].from_three())
            proj[2].from_two()
            vec.from_two()
            put_proj(1, proj[1].from_three())
            put_proj(2, proj[2].from_three())
            vec_out[...] = vec.from_three()
        else:
            proj_out, o_out, vec_out = outs
            vec_out[...] = vectors
            store = pltpu.make_async_copy(grad_scr, proj_out, local_sem.at[4])
            store_out = pltpu.make_async_copy(out_scr.at[0], o_out, local_sem.at[5])
            go([store, store_out])
            finish([store, store_out])
        in_local.wait()
        in_send.wait()
        first_local.wait()
        first_send.wait()


def back(
    dp_size,
    ring,
    tokens,
    n1,
    q,
    k,
    v,
    attended,
    grad_heads,
    lse,
    grad_mixed,
    gain,
    weights,
    select,
    og_own,
    og_peer,
    vec2,
    exports,
    fresh_width,
    own_ff,
):
    width = tokens.shape[1]
    own_width = og_own.shape[-1]
    half = own_width // PAIR
    fv_width = select.shape[0]
    side = fv_width // 2
    pair_of = lambda i: lax.rem(i + 1, 2) * half + lax.div(i, 2)
    pair_block = pl.BlockSpec((SEQ_LEN, PAIR), lambda i: (0, pair_of(i)))
    grad_shape = place(ring, width, dp_size, 3 * PAIR)
    og_shape = place(ring, width, dp_size, own_width)
    scratch = [
        pltpu.VMEM((SEQ_LEN, width), BF16),
        pltpu.VMEM((SEQ_LEN, width), F32),
        pltpu.VMEM((width, SEQ_LEN), BF16),
        pltpu.VMEM((SEQ_LEN, PAIR), F32),
        pltpu.VMEM((SEQ_LEN, PAIR), F32),
        pltpu.VMEM((PAIR, SEQ_LEN), F32),
        pltpu.VMEM((SEQ_LEN, 3 * PAIR), BF16),
        pltpu.VMEM((SEQ_LEN, width), F32),
        pltpu.VMEM((SEQ_LEN, fv_width), F32),
        pltpu.VMEM((SEQ_LEN, side), F32),
        pltpu.VMEM((SEQ_LEN, side), F32),
        pltpu.VMEM(grad_shape, F32),
        pltpu.VMEM((half,) + grad_shape, F32),
        pltpu.VMEM((2,) + og_shape, F32),
        pltpu.SemaphoreType.DMA((8,)),
    ]
    n_sems = 3 + half + (1 + (5 + half) * HOPS if ring else 0)
    scratch += [pltpu.SemaphoreType.DMA((n_sems,))] * 2
    if ring:
        depth, rows = dp_size // 4, width // dp_size

        def hops(columns, first, height=rows):
            shapes = [
                (2, depth // 2, 2, height, columns),
                (depth, height, columns),
                (depth - 1, height, columns),
            ]
            return [pltpu.VMEM(shape, F32) for shape in shapes[first:]]

        ff = 2 * own_ff // 3
        scratch += [pltpu.VMEM((rows, ff), F32)] + hops(ff, 2)
        scratch += [pltpu.VMEM((2, depth // 2, 2, rows, ff), F32)] + hops(ff, 1)
        scratch += [pltpu.VMEM(place(ring, width, dp_size, ff), F32)] + hops(ff, 0)
        scratch += hops(own_width, 0)
        scratch += [
            pltpu.VMEM((half, 2, depth // 2, 2, rows, 3 * PAIR), F32),
            pltpu.VMEM((half, depth, rows, 3 * PAIR), F32),
            pltpu.VMEM((half, depth - 1, rows, 3 * PAIR), F32),
        ]
        vec_whole = pltpu.VMEM((depth, 2, 2, 8, PAIR), F32)
        scratch += [vec_whole, vec_whole] + hops(PAIR, 0, 8) + [vec_whole]
        totals = [
            (rows, own_ff),
            (own_ff, rows),
            (rows, own_width),
            (rows, own_width),
            (rows, own_width),
            (own_width, rows),
            (8, PAIR),
        ]
        total_specs = [fixed(shape) for shape in totals]
    else:
        totals = [(half,) + grad_shape, og_shape, (8, width)]
        total_specs = [ANY, ANY, fixed((8, width))]
    used = list(exports) if ring else []
    in_specs = [
        ANY,
        fixed((SEQ_LEN, width)),
        pair_block,
        pair_block,
        pair_block,
        pair_block,
        pair_block,
        pl.BlockSpec((1, 2, SEQ_LEN), lambda i: (pair_of(i), 0, 0)),
        ANY,
        fixed((1, width)),
        pl.BlockSpec((width, 3 * PAIR), lambda i: (0, pair_of(i))),
        pl.BlockSpec((fv_width, PAIR), lambda i: (0, pair_of(i))),
        ANY,
        ANY,
        fixed((8, width)),
    ] + [ANY] * len(used)
    return pl.pallas_call(
        functools.partial(back_kernel, dp_size, ring, (len(in_specs), 2 + len(totals))),
        grid=(2 * half,),
        in_specs=in_specs,
        out_specs=[ANY, ANY] + total_specs,
        scratch_shapes=scratch,
        out_shape=[
            jax.ShapeDtypeStruct((2 * SEQ_LEN, width), F32),
            jax.ShapeDtypeStruct((2 * SEQ_LEN, side), F32),
        ]
        + [jax.ShapeDtypeStruct(shape, F32) for shape in totals],
        compiler_params=params(2),
        name="back",
    )(
        tokens,
        n1,
        q,
        k,
        v,
        attended,
        grad_heads,
        lse,
        grad_mixed,
        gain,
        weights,
        select,
        og_own,
        og_peer,
        vec2,
        *used,
    )


def on_device(
    dp_size,
    tokens,
    first_values,
    seq_count,
    skip_map,
    norm1_gain,
    norm1_shift,
    query_weight,
    key_weight,
    value_weight,
    out_weight,
    norm2_gain,
    norm2_shift,
    up_weight,
    down_weight,
    cotangent,
):
    width = tokens.shape[1]
    own_width = query_weight.shape[1]
    fresh_width = value_weight.shape[1]
    own_ff = up_weight.shape[1]
    half = own_width // PAIR
    ring = ring_of(dp_size, width)
    gain1, shift1 = norm1_gain[None, :], norm1_shift[None, :]
    gain2, shift2 = norm2_gain[None, :], norm2_shift[None, :]
    n1, q, k, v, attended, lse, weights, select, out_peer, up_peer, down_peer = front(
        dp_size,
        tokens,
        first_values,
        skip_map,
        gain1,
        shift1,
        query_weight,
        key_weight,
        value_weight,
        out_weight,
        up_weight,
        down_weight,
    )
    lse = lse[0 : 4 * half].reshape(2 * half, 2, SEQ_LEN)
    layer_out, grad_mixed, grad_heads, og_own, og_peer, vec2, *exports = middle(
        dp_size,
        ring,
        tokens,
        attended,
        cotangent,
        seq_count,
        gain2,
        shift2,
        out_weight,
        out_peer,
        (up_weight, down_weight),
        (up_peer, down_peer),
    )
    input_grad, first_grad, *totals = back(
        dp_size,
        ring,
        tokens,
        n1,
        q,
        k,
        v,
        attended,
        grad_heads,
        lse,
        grad_mixed,
        gain1,
        weights,
        select,
        og_own,
        og_peer,
        vec2,
        exports,
        fresh_width,
        own_ff,
    )
    if ring:
        up_total, down_total, query_total, key_total, value_total, out_total, vectors = totals
        rows = width // dp_size
        value_total = value_total[:, :fresh_width]
        gain1_total, shift1_total, gain2_total, shift2_total = (vectors[n, :rows] for n in range(4))
    else:
        proj, out_grad, vectors = totals
        ff_block = own_ff // exports[0].shape[0]
        vectors = vectors + lax.ppermute(vectors, "tensor", [(0, 1), (1, 0)])
        columns = [proj[n] for n in range(half)] + [out_grad]
        columns += [part for part in exports[0]]
        packed = jnp.concatenate(columns + [jnp.pad(vectors.T, ((0, 0), (0, 120)))], axis=1)
        summed = lax.psum_scatter(packed, "dp", scatter_dimension=0, tiled=True)
        heads = summed[:, : 3 * own_width].reshape(-1, half, 3, PAIR)
        query_total, key_total, value_total = (
            heads[:, :, n].reshape(-1, own_width) for n in range(3)
        )
        value_total = value_total[:, :fresh_width]
        start = 3 * own_width
        out_total = summed[:, start : start + own_width].T
        start += own_width
        pairs = summed[:, start : start + 2 * own_ff].reshape(-1, own_ff // ff_block, 2, ff_block)
        down_total = pairs[:, :, 0].reshape(-1, own_ff).T
        up_total = pairs[:, :, 1].reshape(-1, own_ff)
        start += 2 * own_ff
        gain1_total, shift1_total, gain2_total, shift2_total = (
            summed[:, start + n] for n in range(4)
        )
    return (
        layer_out,
        input_grad,
        first_grad,
        gain1_total,
        shift1_total,
        query_total,
        key_total,
        value_total,
        out_total,
        gain2_total,
        shift2_total,
        up_total,
        down_total,
    )


def solution(mesh):
    placed = (
        P("dp", None),
        P("dp", None),
        P("dp"),
        P("tensor"),
        P(),
        P(),
        P(None, "tensor"),
        P(None, "tensor"),
        P(None, "tensor"),
        P("tensor", None),
        P(),
        P(),
        P(None, "tensor"),
        P("tensor", None),
        P("dp", None),
    )
    return jax.shard_map(
        functools.partial(on_device, mesh.shape["dp"]),
        mesh=mesh,
        in_specs=placed,
        out_specs=(
            P("dp", None),
            P("dp", None),
            P("dp", "tensor"),
            P("dp"),
            P("dp"),
            P("dp", "tensor"),
            P("dp", "tensor"),
            P("dp", "tensor"),
            P("tensor", "dp"),
            P("dp"),
            P("dp"),
            P("dp", "tensor"),
            P("tensor", "dp"),
        ),
        check_vma=False,
    )
```

```python
import functools

import jax
import jax.numpy as jnp
from jax import lax
from jax.experimental import pallas as pl
from jax.experimental.pallas import tpu as pltpu
from jax.sharding import PartitionSpec as P

HEAD_DIM = 64
SEQ_LEN = 1024
BLOCK = 256
PAIR = 2 * HEAD_DIM
EPS = 1e-05
FILL = -1e30
VMEM_BYTES = 60 * 1024 * 1024

F32 = jnp.float32
BF16 = jnp.bfloat16


def dot_nn(left, right):
    return lax.dot_general(left, right, (((1,), (0,)), ((), ())), preferred_element_type=F32)


def dot_nt(left, right):
    return lax.dot_general(left, right, (((1,), (1,)), ((), ())), preferred_element_type=F32)


def norm_stats(values_in):
    average = jnp.mean(values_in, axis=-1, keepdims=True)
    centered = values_in - average
    variance = jnp.mean(centered * centered, axis=-1, keepdims=True)
    factor = lax.rsqrt(variance + EPS)
    return centered * factor, factor


def norm_backward(grad, normed, factor, gain):
    scaled = grad * gain
    mean_plain = jnp.mean(scaled, axis=-1, keepdims=True)
    mean_cross = jnp.mean(scaled * normed, axis=-1, keepdims=True)
    return factor * (scaled - mean_plain - normed * mean_cross)


def each(count, body):
    lax.fori_loop(0, count, lambda index, carry: (body(index), carry)[1], 0)


def row_block(index):
    return pl.ds(pl.multiple_of(index * BLOCK, BLOCK), BLOCK)


def recast(source, target, rows=64):
    def one(index):
        part = pl.ds(pl.multiple_of(index * rows, rows), rows)
        target[part, :] = source[part, :].astype(target.dtype)

    each(source.shape[0] // rows, one)


def head_masks(rows):
    lanes = lax.broadcasted_iota(jnp.int32, (rows, PAIR), 1)
    return lanes < HEAD_DIM


def split_heads(pair_rows):
    first = head_masks(pair_rows.shape[0])
    zero = jnp.zeros_like(pair_rows)
    return jnp.where(first, pair_rows, zero), jnp.where(first, zero, pair_rows)


MESH = pl.DeviceIdType.MESH


def params(collective_id):
    return pltpu.CompilerParams(
        vmem_limit_bytes=VMEM_BYTES, collective_id=collective_id, has_side_effects=True
    )


def fixed(shape):
    zeros = (0,) * len(shape)
    return pl.BlockSpec(shape, lambda i: zeros, pipeline_mode=pl.Buffered(1))


ANY = pl.BlockSpec(memory_space=pl.ANY)
SMEM = pl.BlockSpec(memory_space=pltpu.SMEM)


def ring_of(dp_size, width):
    rows = width // dp_size
    return dp_size % 8 == 0 and width % dp_size == 0 and rows % 8 == 0


def place(ring, width, dp_size, columns):
    if not ring:
        return (width, columns)
    return (dp_size // 4, 2, 2, width // dp_size, columns)


class Link:
    def __init__(self, dp_size):
        self.dp = lax.axis_index("dp")
        self.core = lax.axis_index("tensor")
        self.depth = dp_size // 4
        self.x = lax.rem(self.dp, 2)
        self.y = lax.rem(lax.div(self.dp, 2), 2)
        self.z = lax.div(self.dp, 4)
        self.peer = {"tensor": 1 - self.core}
        self.x_side = {"dp": self.dp + 1 - 2 * self.x}
        self.y_side = {"dp": self.dp + 2 - 4 * self.y}

    def z_place(self, hop):
        return lax.rem(self.z + hop, self.depth)

    def z_side(self, hop):
        return {"dp": 4 * self.z_place(hop) + lax.rem(self.dp, 4)}

    def meet(self, partners):
        barrier = pltpu.get_barrier_semaphore()
        for partner in partners:
            pl.semaphore_signal(barrier, inc=1, device_id=partner, device_id_type=MESH)
        pl.semaphore_wait(barrier, len(partners))


def remote(source, target, sems, index, device):
    send, recv = sems
    return pltpu.make_async_remote_copy(
        src_ref=source,
        dst_ref=target,
        send_sem=send.at[index],
        recv_sem=recv.at[index],
        device_id=device,
        device_id_type=MESH,
    )


def first_hop(link, source, landing, sems, base):
    low = link.depth // 2
    return [
        remote(
            source.at[0:low, :, 1 - link.x], landing.at[0], sems, base, link.x_side
        ),
        remote(
            source.at[low : 2 * low, 1 - link.y],
            landing.at[1],
            sems,
            base + 1,
            link.y_side,
        ),
    ]


def second_hop(link, source, landing, sems, base):
    low = link.depth // 2
    return [
        remote(
            source.at[0, :, 1 - link.y],
            landing.at[0:low],
            sems,
            base,
            link.y_side,
        ),
        remote(
            source.at[1, :, 1 - link.x],
            landing.at[low : 2 * low],
            sems,
            base + 1,
            link.x_side,
        ),
    ]


def last_hop(link, source, landing, sems, base):
    return [
        remote(
            source.at[link.z_place(hop)],
            landing.at[hop - 1],
            sems,
            base + hop - 1,
            link.z_side(hop),
        )
        for hop in range(1, link.depth)
    ]


def go(copies):
    for copy in copies:
        copy.start()


def finish(copies):
    for copy in copies:
        copy.wait()


def merge_first(link, whole, landing):
    low = link.depth // 2

    def one(row):
        for other in range(2):
            landing[0, row, other] += whole[row, other, link.x]
            landing[1, row, other] += whole[low + row, link.y, other]

    each(low, one)


def merge_second(link, landed, landing):
    low = link.depth // 2

    def one(row):
        landing[row] += landed[0, row, link.y]
        landing[low + row] += landed[1, row, link.x]

    each(low, one)


def total_last(own, landing):
    total = own
    for hop in range(landing.shape[0]):
        total = total + landing[hop]
    return total


HOPS = 7


class Chunk:
    def __init__(self, link, sems, base, whole=None, hop1=None, hop2=None, hop3=None):
        self.link, self.whole, self.hop1, self.hop2, self.hop3 = link, whole, hop1, hop2, hop3
        self.sems, self.base = sems, base
        self.sources = [whole, hop1, hop2]

    def hop(self, number):
        source = self.sources[number - 1]
        if number == 1:
            return first_hop(self.link, source, self.hop1, self.sems, self.base)
        if number == 2:
            return second_hop(self.link, source, self.hop2, self.sems, self.base + 2)
        return last_hop(self.link, source, self.hop3, self.sems, self.base + 4)

    def start(self, number):
        go(self.hop(number))

    def land(self, number):
        finish(self.hop(number))
        if number == 1:
            merge_first(self.link, self.whole, self.hop1)
        elif number == 2:
            merge_second(self.link, self.hop1, self.hop2)

    def total(self):
        finish(self.hop(3))
        return total_last(self.hop2[self.link.z], self.hop3)


class DeepChunk:
    def __init__(self, link, sems, base, whole, hop1, summed, source, hop2, hop3):
        self.link, self.whole, self.hop1, self.hop2, self.hop3 = link, whole, hop1, hop2, hop3
        self.summed, self.source = summed, source
        self.sems, self.base = sems, base

    def hop(self, number):
        link, sems, base = self.link, self.sems, self.base
        if number == 1:
            return last_hop(link, self.whole, self.hop1, sems, base)
        side = self.hop3.shape[-1]
        left, right = pl.ds(0, side), pl.ds(side, side)
        if number == 2:
            base += link.depth - 1
            summed = self.source
            return [
                remote(
                    summed.at[:, 1 - link.x, :, left], self.hop2.at[0], sems, base, link.x_side
                ),
                remote(
                    summed.at[1 - link.y, :, :, right], self.hop2.at[1], sems, base + 1, link.y_side
                ),
            ]
        base += link.depth + 1
        return [
            remote(self.hop2.at[0, 1 - link.y], self.hop3.at[0], sems, base, link.y_side),
            remote(self.hop2.at[1, 1 - link.x], self.hop3.at[1], sems, base + 1, link.x_side),
        ]

    def start(self, number):
        go(self.hop(number))

    def land(self, number):
        link = self.link
        finish(self.hop(number))
        if number == 1:

            def one(row):
                for other in range(2):
                    total = self.whole[link.z, row, other]
                    for hop in range(self.hop1.shape[0]):
                        total = total + self.hop1[hop, row, other]
                    self.summed[row, other] = total

            each(2, one)
        else:
            side = self.hop3.shape[-1]
            for other in range(2):
                self.hop2[0, other] += self.summed[other, link.x, :, 0:side]
                self.hop2[1, other] += self.summed[link.y, other, :, side:]

    def total(self):
        finish(self.hop(3))
        return jnp.concatenate(
            [self.hop2[0, self.link.y] + self.hop3[0], self.hop2[1, self.link.x] + self.hop3[1]],
            axis=-1,
        )


def front_kernel(
    dp_size,
    tokens,
    first_values,
    skip_map,
    gain_ref,
    shift_ref,
    wq_ref,
    wk_ref,
    wv_ref,
    out_w,
    up_w,
    down_w,
    n1_ref,
    q_ref,
    k_ref,
    v_ref,
    att_ref,
    lse_ref,
    w_ref,
    sel_ref,
    out_peer,
    up_peer,
    down_peer,
    x_scr,
    fv_scr,
    proj_own,
    proj_send,
    proj_recv,
    sel_send,
    sel_recv,
    out_low,
    up_low,
    down_low,
    out_send,
    up_send,
    down_send,
    out_recv,
    up_recv,
    down_recv,
    lse_scr,
    local_sem,
    send_sem,
    recv_sem,
):
    step = pl.program_id(0)
    length, width = x_scr.shape
    blocks = length // BLOCK
    half = pl.num_programs(0) // 2
    own_width = wq_ref.shape[1]
    fresh_width = wv_ref.shape[0]
    fv_width = fv_scr.shape[1]
    link = Link(dp_size)
    sems = (send_sem, recv_sem)
    rows_here = pl.ds(link.core * length, length)
    local = [
        pltpu.make_async_copy(tokens.at[rows_here], x_scr, local_sem.at[0]),
        pltpu.make_async_copy(first_values.at[rows_here], fv_scr, local_sem.at[1]),
        pltpu.make_async_copy(up_w, up_low, local_sem.at[2]),
        pltpu.make_async_copy(down_w, down_low, local_sem.at[3]),
        pltpu.make_async_copy(out_w, out_low, local_sem.at[4]),
    ]
    early = [
        remote(proj_send, proj_recv, sems, 0, link.peer),
        remote(sel_send, sel_recv, sems, 1, link.peer),
    ]
    late = [
        remote(up_send, up_recv, sems, 2, link.peer),
        remote(down_send, down_recv, sems, 3, link.peer),
        remote(out_send, out_recv, sems, 4, link.peer),
    ]
    landed = [
        (late[0], up_recv, up_low, pltpu.make_async_copy(up_low, up_peer, local_sem.at[2])),
        (late[1], down_recv, down_low, pltpu.make_async_copy(down_low, down_peer, local_sem.at[3])),
        (late[2], out_recv, out_low, pltpu.make_async_copy(out_low, out_peer, local_sem.at[4])),
    ]

    @pl.when(step == 0)
    def _():
        go(local)
        proj_own[2, :, 0:fresh_width] = jnp.transpose(wv_ref[...])
        proj_own[2, :, fresh_width:] = jnp.zeros((width, own_width - fresh_width), BF16)
        for part, source in enumerate((wq_ref, wk_ref)):
            recast(source, proj_own.at[part])
        for part in range(3):
            recast(proj_own.at[part], proj_send.at[part])
        row = lax.broadcasted_iota(jnp.int32, (fv_width, own_width), 0)
        col = lax.broadcasted_iota(jnp.int32, (fv_width, own_width), 1)
        slots = (own_width - fresh_width) // HEAD_DIM
        target = jnp.full((fv_width, own_width), -1, jnp.int32)
        for slot in range(slots):
            start = fresh_width + slot * HEAD_DIM
            inside = jnp.logical_and(col >= start, col < start + HEAD_DIM)
            target = jnp.where(inside, skip_map[slot] * HEAD_DIM + col - start, target)
        chosen = jnp.where(row == target, 1.0, 0.0).astype(F32)
        sel_send[...] = chosen
        sel_ref[:, 0:own_width] = chosen.astype(BF16)
        link.meet([link.peer])
        go(early)
        lse_scr[...] = jnp.zeros_like(lse_scr)
        local[0].wait()
        local[1].wait()

        def one(block, carry):
            rows = pl.ds(block * BLOCK, BLOCK)
            normed, _ = norm_stats(x_scr[rows, :].astype(F32))
            n1_ref[rows, :] = (normed * gain_ref[...] + shift_ref[...]).astype(BF16)
            return carry

        lax.fori_loop(0, blocks, one, 0)

    @pl.when(step == half)
    def _():
        finish(early)
        sel_ref[:, own_width:] = sel_recv[...].astype(BF16)

    @pl.when(step < half)
    def _():
        cols = pl.ds(pl.multiple_of(step * PAIR, PAIR), PAIR)
        for part in range(3):
            w_ref[:, part * PAIR : (part + 1) * PAIR] = proj_own[part, :, cols]

    @pl.when(step >= half)
    def _():
        cols = pl.ds(pl.multiple_of((step - half) * PAIR, PAIR), PAIR)
        for part in range(3):
            w_ref[:, part * PAIR : (part + 1) * PAIR] = proj_recv[part, :, cols].astype(BF16)

    sel_cols = pl.ds(pl.multiple_of(step * PAIR, PAIR), PAIR)
    for block in range(blocks):
        rows = slice(block * BLOCK, (block + 1) * BLOCK)
        fused = dot_nn(n1_ref[rows, :], w_ref[...])
        picked = dot_nn(fv_scr[rows, :], sel_ref[:, sel_cols])
        q_ref[rows, :] = (fused[:, 0:PAIR].astype(BF16).astype(F32) * HEAD_DIM**-0.5).astype(BF16)
        k_ref[rows, :] = fused[:, PAIR : 2 * PAIR].astype(BF16)
        v_ref[rows, :] = (fused[:, 2 * PAIR :] + picked).astype(BF16)

    lane = lax.broadcasted_iota(jnp.int32, (BLOCK, PAIR), 1)
    row_pos = lax.broadcasted_iota(jnp.int32, (BLOCK, BLOCK), 0)
    col_pos = lax.broadcasted_iota(jnp.int32, (BLOCK, BLOCK), 1)
    seen = col_pos <= row_pos
    for block in range(blocks):
        lo, hi = block * BLOCK, (block + 1) * BLOCK
        queries = split_heads(q_ref[lo:hi, :])
        total = jnp.zeros((BLOCK, PAIR), F32)
        lse_tile = lse_scr[lo:hi, :]
        for head in range(2):
            diag = jnp.where(seen, dot_nt(queries[head], k_ref[lo:hi, :]), FILL)
            peak = jnp.max(diag, axis=-1, keepdims=True)
            if block:
                past = dot_nt(queries[head], k_ref[0:lo, :])
                peak = jnp.maximum(peak, jnp.max(past, axis=-1, keepdims=True))
            diag = jnp.exp(diag - peak)
            mass = jnp.sum(diag, axis=-1, keepdims=True)
            if block:
                past = jnp.exp(past - peak)
                mass = mass + jnp.sum(past, axis=-1, keepdims=True)
            inverse = 1.0 / mass
            total = total + dot_nn((diag * inverse).astype(BF16), split_heads(v_ref[lo:hi, :])[head])
            if block:
                total = total + dot_nn(
                    (past * inverse).astype(BF16), split_heads(v_ref[0:lo, :])[head]
                )
            lse_tile = jnp.where(lane == 2 * step + head, peak + jnp.log(mass), lse_tile)
        att_ref[lo:hi, :] = total.astype(BF16)
        lse_scr[lo:hi, :] = lse_tile

    @pl.when(step == 0)
    def _():
        for copy in local[2:]:
            copy.wait()
        recast(up_low, up_send)
        recast(down_low, down_send)
        recast(out_low, out_send)
        go(late)

    @pl.when(step == pl.num_programs(0) - 2)
    def _():
        for copy, recv, low, store in landed:
            copy.wait()
            recast(recv, low)
            store.start()

    @pl.when(step == pl.num_programs(0) - 1)
    def _():
        for block in range(blocks):
            lo, hi = block * BLOCK, (block + 1) * BLOCK
            turned = jnp.transpose(lse_scr[lo:hi, :])
            for pair in range(lse_ref.shape[0]):
                lse_ref[pair, 0:2, lo:hi] = turned[2 * pair : 2 * pair + 2, :]
        for _, _, _, store in landed:
            store.wait()


def front(dp_size, tokens, first_values, skip_map, gain, shift, wq, wk, wv, out_w, up_w, down_w):
    width = tokens.shape[1]
    own_width = wq.shape[1]
    half = own_width // PAIR
    fv_width = first_values.shape[1]
    pair_block = pl.BlockSpec((SEQ_LEN, PAIR), lambda i: (0, i))
    pair_out = jax.ShapeDtypeStruct((SEQ_LEN, 2 * own_width), BF16)
    return pl.pallas_call(
        functools.partial(front_kernel, dp_size),
        grid=(2 * half,),
        in_specs=[
            ANY,
            ANY,
            SMEM,
            fixed((1, width)),
            fixed((1, width)),
            fixed(wq.shape),
            fixed(wk.shape),
            fixed(wv.shape),
            ANY,
            ANY,
            ANY,
        ],
        out_specs=[
            fixed((SEQ_LEN, width)),
            pair_block,
            pair_block,
            pair_block,
            pair_block,
            fixed((2 * half, 8, SEQ_LEN)),
            pl.BlockSpec((width, 3 * PAIR), lambda i: (0, i)),
            fixed((fv_width, 2 * own_width)),
            ANY,
            ANY,
            ANY,
        ],
        scratch_shapes=[
            pltpu.VMEM((SEQ_LEN, width), BF16),
            pltpu.VMEM((SEQ_LEN, fv_width), BF16),
            pltpu.VMEM((3, width, own_width), BF16),
            pltpu.VMEM((3, width, own_width), F32),
            pltpu.VMEM((3, width, own_width), F32),
            pltpu.VMEM((fv_width, own_width), F32),
            pltpu.VMEM((fv_width, own_width), F32),
            pltpu.VMEM(out_w.shape, BF16),
            pltpu.VMEM(up_w.shape, BF16),
            pltpu.VMEM(down_w.shape, BF16),
            pltpu.VMEM(out_w.shape, F32),
            pltpu.VMEM(up_w.shape, F32),
            pltpu.VMEM(down_w.shape, F32),
            pltpu.VMEM(out_w.shape, F32),
            pltpu.VMEM(up_w.shape, F32),
            pltpu.VMEM(down_w.shape, F32),
            pltpu.VMEM((SEQ_LEN, PAIR), F32),
            pltpu.SemaphoreType.DMA((5,)),
            pltpu.SemaphoreType.DMA((5,)),
            pltpu.SemaphoreType.DMA((5,)),
        ],
        out_shape=[
            jax.ShapeDtypeStruct((SEQ_LEN, width), BF16),
            pair_out,
            pair_out,
            pair_out,
            pair_out,
            jax.ShapeDtypeStruct((2 * half, 8, SEQ_LEN), F32),
            jax.ShapeDtypeStruct((width, 6 * own_width), BF16),
            jax.ShapeDtypeStruct((fv_width, 2 * own_width), BF16),
            jax.ShapeDtypeStruct(out_w.shape, BF16),
            jax.ShapeDtypeStruct(up_w.shape, BF16),
            jax.ShapeDtypeStruct(down_w.shape, BF16),
        ],
        compiler_params=params(0),
        name="front",
    )(tokens, first_values, skip_map, gain, shift, wq, wk, wv, out_w, up_w, down_w)


def gelu_pair(upper):
    scale = (2.0 / jnp.pi) ** 0.5
    square = upper * upper
    inner = upper * (scale + (scale * 0.044715) * square)
    tanh = jnp.tanh(inner)
    cdf = 0.5 + 0.5 * tanh
    slope = cdf + 0.5 * upper * (1.0 - tanh * tanh) * (scale + (3.0 * scale * 0.044715) * square)
    return upper * cdf, slope


def middle_kernel(dp_size, ring, n_exports, *refs):
    (
        tokens,
        att_ref,
        cotangent,
        seq_count,
        gain_ref,
        shift_ref,
        wo_own,
        wo_peer,
        up_own,
        down_own,
        up_peer,
        down_peer,
        layer_out,
        gmix_out,
        gheads_ref,
        og_own,
        og_peer,
        vec_ref,
    ) = refs[:18]
    exports = refs[18 : 18 + n_exports]
    (
        mixed_scr,
        stage_scr,
        two_scr,
        low_scr,
        two_t,
        low_t,
        act_scr,
        gup_scr,
        up_scr,
        down_scr,
        wo_scr,
        post_scr,
        grad_scr,
        local_sem,
        send_sem,
        recv_sem,
    ) = refs[18 + n_exports : 34 + n_exports]
    ring_scr = refs[34 + n_exports :]
    step = pl.program_id(0)
    steps = pl.num_programs(0)
    length, width = mixed_scr.shape
    blocks = length // BLOCK
    own_width = wo_own.shape[0]
    own_ff = up_own.shape[1]
    chunks = grad_scr.shape[0]
    ff_block = own_ff // chunks
    link = Link(dp_size)
    sems = (send_sem, recv_sem)
    rows_here = pl.ds(link.core * length, length)
    x_ref = gheads_ref
    loads = [
        pltpu.make_async_copy(tokens.at[rows_here], x_ref, local_sem.at[0]),
        pltpu.make_async_copy(wo_own, wo_scr.at[pl.ds(0, own_width)], local_sem.at[1]),
        pltpu.make_async_copy(wo_peer, wo_scr.at[pl.ds(own_width, own_width)], local_sem.at[2]),
        pltpu.make_async_copy(cotangent.at[rows_here], low_scr, local_sem.at[3]),
    ]
    weight_loads = [
        pltpu.make_async_copy(up_own, up_scr.at[:, pl.ds(0, own_ff)], local_sem.at[4]),
        pltpu.make_async_copy(up_peer, up_scr.at[:, pl.ds(own_ff, own_ff)], local_sem.at[5]),
        pltpu.make_async_copy(down_own, down_scr.at[pl.ds(0, own_ff)], local_sem.at[6]),
        pltpu.make_async_copy(down_peer, down_scr.at[pl.ds(own_ff, own_ff)], local_sem.at[7]),
    ]
    gmix_copy = pltpu.make_async_copy(mixed_scr, gmix_out, local_sem.at[8])

    def layer_copies(block):
        rows = pl.ds(link.core * length + block * BLOCK, BLOCK)
        return [
            pltpu.make_async_copy(
                stage_scr.at[lax.rem(block, 2)], layer_out.at[rows], local_sem.at[9 + block]
            ),
            remote(stage_scr.at[lax.rem(block, 2)], layer_out.at[rows], sems, block, link.peer),
        ]


    def swap(chunk):
        return remote(
            post_scr.at[lax.rem(chunk, 2)], grad_scr.at[chunk], sems, blocks + chunk, link.peer
        )

    flows = {}
    if ring:
        base = blocks + chunks
        hop1, hop2, deep1 = ring_scr
        for slot, chunk in enumerate((0, 2, 3, 5)):
            flows[chunk] = Chunk(
                link,
                sems,
                base + HOPS * chunk,
                grad_scr.at[chunk],
                hop1.at[slot],
                None if chunk else hop2,
            )
        flows[1] = DeepChunk(
            link, sems, base + HOPS, grad_scr.at[1], deep1, deep1.at[0], None, None, None
        )

    def run(events):
        for chunk, number in events:
            if ring:
                if number > 1:
                    flows[chunk].land(number - 1)
                flows[chunk].start(number)

    @pl.when(step == 0)
    def _():
        go(loads)
        go(weight_loads)
        partners = [link.peer]
        if ring:
            partners += [link.x_side, link.y_side]
            partners += [link.z_side(hop) for hop in range(1, link.depth)]
        link.meet(partners)
        finish(loads)
        live = jnp.where(link.core < seq_count[0], 1.0, 0.0).astype(F32)

        def enter(block):
            rows = row_block(block)
            mixed = x_ref[rows, :].astype(F32) + dot_nn(att_ref[rows, :], wo_scr[...])
            mixed_scr[rows, :] = mixed
            normed, _ = norm_stats(mixed)
            two_low = (normed * gain_ref[...] + shift_ref[...]).astype(BF16)
            two_scr[rows, :] = two_low
            two_t[:, rows] = jnp.transpose(two_low)
            low = (low_scr[rows, :].astype(F32) * live).astype(BF16)
            low_scr[rows, :] = low
            low_t[:, rows] = jnp.transpose(low)

        each(blocks, enter)
        finish(weight_loads)

    last = lax.div(step, steps - 1)
    mine = (1 - lax.rem(step, 2)) * lax.div(step + steps - 1, steps) + last
    mine_index = lax.div(step - 1 + lax.div(steps - step, steps), 2)
    post_index = lax.div(step + 1, 2)
    turn = mine * mine_index + (1 - mine) * (chunks + post_index)
    slot = 2 * mine + (1 - mine) * lax.rem(post_index, 2)
    cols = pl.ds(pl.multiple_of(turn * ff_block, ff_block), ff_block)
    for block in range(blocks):
        rows = slice(block * BLOCK, (block + 1) * BLOCK)
        upper = dot_nn(two_scr[rows, :], up_scr[:, cols])
        active, slope = gelu_pair(upper)
        act_scr[rows, cols] = active.astype(BF16)
        grad_active = dot_nt(low_scr[rows, :], down_scr[cols, :])
        gup_scr[rows, cols] = (grad_active * slope).astype(BF16)

    block_shape = grad_scr.shape[1:-1] + (ff_block,)
    @pl.when(jnp.logical_and(mine == 0, post_index > 1))
    def _():
        swap(post_index - 2).wait_send()

    post_scr[slot, ..., 0:ff_block] = dot_nn(low_t[...], act_scr[:, cols]).reshape(block_shape)
    post_scr[slot, ..., ff_block:] = dot_nn(two_t[...], gup_scr[:, cols]).reshape(block_shape)

    @pl.when(mine == 0)
    def _():
        swap(post_index).start()

    @pl.when(mine == 1)
    def _():
        swap(mine_index).wait_recv()
        grad_scr[mine_index] += post_scr[2]

    if ring:
        for when, events in {
            2: [(0, 1)],
            4: [(1, 1)],
            6: [(2, 1)],
            7: [(0, 2)],
            8: [(3, 1)],
        }.items():

            @pl.when(step == when)
            def _():
                run(events)

    @pl.when(step == steps - 1)
    def _():
        swap(chunks - 2).wait_send()
        swap(chunks - 1).wait_send()
        if not ring:
            whole_copy = pltpu.make_async_copy(grad_scr, exports[0], local_sem.at[13])
            whole_copy.start()

        def leave(block):
            rows = row_block(block)

            @pl.when(block > 1)
            def _():
                finish(layer_copies(block - 2))

            stage_scr[lax.rem(block, 2)] = mixed_scr[rows, :] + dot_nn(
                act_scr[rows, :], down_scr[...]
            )
            go(layer_copies(block))

        each(blocks, leave)
        run([(5, 1)])
        vec_ref[...] = jnp.zeros_like(vec_ref)

        def turn_back(block):
            rows = row_block(block)
            grad_two = dot_nt(gup_scr[rows, :], up_scr[...])
            normed, factor = norm_stats(mixed_scr[rows, :])
            vec_ref[0:1, :] += jnp.sum(grad_two * normed, axis=0, keepdims=True)
            vec_ref[1:2, :] += jnp.sum(grad_two, axis=0, keepdims=True)
            grad_mixed = low_scr[rows, :].astype(F32) + norm_backward(
                grad_two, normed, factor, gain_ref[...]
            )
            mixed_scr[rows, :] = grad_mixed
            grad_attn = grad_mixed.astype(BF16)
            low_t[:, rows] = jnp.transpose(grad_attn)
            gheads_ref[rows, :] = dot_nt(grad_attn, wo_scr[...]).astype(BF16)

        each(blocks, turn_back)
        gmix_copy.start()
        og_peer[...] = dot_nn(low_t[...], att_ref[:, own_width:]).reshape(og_peer.shape)
        og_own[...] = dot_nn(low_t[...], att_ref[:, 0:own_width]).reshape(og_own.shape)
        if ring:
            at_zero, at_one, at_two, at_deep = exports
            outs = [
                pltpu.make_async_copy(grad_scr.at[4], at_zero, local_sem.at[13]),
                pltpu.make_async_copy(hop1.at[pl.ds(1, 3)], at_one, local_sem.at[14]),
                pltpu.make_async_copy(hop2, at_two, local_sem.at[15]),
                pltpu.make_async_copy(deep1.at[0], at_deep, local_sem.at[16]),
            ]
            outs[0].start()
            flows[0].land(2)
            outs[2].start()
            flows[1].land(1)
            outs[3].start()
            flows[2].land(1)
            flows[3].land(1)
            flows[5].land(1)
            outs[1].start()
            finish(outs)
        else:
            whole_copy.wait()
        gmix_copy.wait()
        finish(layer_copies(blocks - 2))
        finish(layer_copies(blocks - 1))


def middle(
    dp_size, ring, tokens, attended, cotangent, seq_count, gain, shift, wo_own, wo_peer, own, peer
):
    width = tokens.shape[1]
    own_ff = own[0].shape[1]
    own_width = wo_own.shape[0]
    chunks = 6
    ff_block = own_ff // chunks
    grad_shape = place(ring, width, dp_size, 2 * ff_block)
    og_shape = place(ring, width, dp_size, own_width)
    scratch = []
    if ring:
        depth, rows = dp_size // 4, width // dp_size
        hop1 = (2, depth // 2, 2, rows, 2 * ff_block)
        hop2 = (depth, rows, 2 * ff_block)
        deep1 = (depth - 1, 2, 2, rows, 2 * ff_block)
        export_shapes = [grad_shape, (3,) + hop1, hop2, deep1[1:]]
        scratch = [
            pltpu.VMEM((4,) + hop1, F32),
            pltpu.VMEM(hop2, F32),
            pltpu.VMEM(deep1, F32),
        ]
    else:
        export_shapes = [(chunks,) + grad_shape]
    blocks = SEQ_LEN // BLOCK
    n_sems = blocks + chunks + HOPS * chunks
    return pl.pallas_call(
        functools.partial(middle_kernel, dp_size, ring, len(export_shapes)),
        grid=(2 * chunks,),
        in_specs=[
            ANY,
            fixed((SEQ_LEN, 2 * own_width)),
            ANY,
            SMEM,
            fixed((1, width)),
            fixed((1, width)),
            ANY,
            ANY,
            ANY,
            ANY,
            ANY,
            ANY,
        ],
        out_specs=[
            ANY,
            ANY,
            fixed((SEQ_LEN, 2 * own_width)),
            fixed(og_shape),
            fixed(og_shape),
            fixed((8, width)),
        ]
        + [ANY] * len(export_shapes),
        scratch_shapes=[
            pltpu.VMEM((SEQ_LEN, width), F32),
            pltpu.VMEM((2, BLOCK, width), F32),
            pltpu.VMEM((SEQ_LEN, width), BF16),
            pltpu.VMEM((SEQ_LEN, width), BF16),
            pltpu.VMEM((width, SEQ_LEN), BF16),
            pltpu.VMEM((width, SEQ_LEN), BF16),
            pltpu.VMEM((SEQ_LEN, 2 * own_ff), BF16),
            pltpu.VMEM((SEQ_LEN, 2 * own_ff), BF16),
            pltpu.VMEM((width, 2 * own_ff), BF16),
            pltpu.VMEM((2 * own_ff, width), BF16),
            pltpu.VMEM((2 * own_width, width), BF16),
            pltpu.VMEM((3,) + grad_shape, F32),
            pltpu.VMEM((chunks,) + grad_shape, F32),
            pltpu.SemaphoreType.DMA((17,)),
            pltpu.SemaphoreType.DMA((n_sems,)),
            pltpu.SemaphoreType.DMA((n_sems,)),
        ]
        + scratch,
        out_shape=[
            jax.ShapeDtypeStruct((2 * SEQ_LEN, width), F32),
            jax.ShapeDtypeStruct((SEQ_LEN, width), F32),
            jax.ShapeDtypeStruct((SEQ_LEN, 2 * own_width), BF16),
            jax.ShapeDtypeStruct(og_shape, F32),
            jax.ShapeDtypeStruct(og_shape, F32),
            jax.ShapeDtypeStruct((8, width), F32),
        ]
        + [jax.ShapeDtypeStruct(shape, F32) for shape in export_shapes],
        compiler_params=params(1),
        name="middle",
    )(tokens, attended, cotangent, seq_count, gain, shift, wo_own, wo_peer, *own, *peer)


def back_kernel(dp_size, ring, counts, *refs):
    n_in, n_out, fresh_width = counts
    (
        tokens,
        n1_ref,
        q_ref,
        k_ref,
        v_ref,
        att_ref,
        gheads_ref,
        lse_ref,
        gmix,
        gain_ref,
        w_ref,
        sel_ref,
        og_own,
        og_peer,
        vec2_ref,
    ) = refs[:15]
    exports = refs[15:n_in]
    in_grad, first_grad = refs[n_in : n_in + 2]
    outs = refs[n_in + 2 : n_in + n_out]
    scratch = refs[n_in + n_out :]
    (
        x_scr,
        gmix_scr,
        n1_t,
        dk_acc,
        dv_acc,
        dq_t,
        stack_scr,
        one_acc,
        fv_t,
        post_scr,
        out_scr,
        sums_scr,
        local_sem,
        send_sem,
        recv_sem,
    ) = scratch[:15]
    step = pl.program_id(0)
    steps = pl.num_programs(0)
    length, width = x_scr.shape
    blocks = length // BLOCK
    link = Link(dp_size)
    sems = (send_sem, recv_sem)
    rows_here = pl.ds(link.core * length, length)
    chunks = lse_ref.shape[0] * steps // 2
    grads = scratch[15 : 15 + chunks]
    ring_scr = list(scratch[15 + chunks :])
    side = fv_t.shape[0] // 2
    loads = [
        pltpu.make_async_copy(tokens.at[rows_here], x_scr, local_sem.at[0]),
        pltpu.make_async_copy(gmix, gmix_scr, local_sem.at[1]),
        pltpu.make_async_copy(og_own, out_scr.at[0], local_sem.at[2]),
    ]
    out_swap = remote(og_peer, out_scr.at[1], sems, 0, link.peer)
    swaps = [
        remote(
            post_scr.at[0, ..., pl.ds(0, grads[chunk].shape[-1])],
            grads[chunk],
            sems,
            1 + chunk,
            link.peer,
        )
        for chunk in range(chunks)
    ]
    base = 1 + chunks
    in_copies = [
        remote(one_acc, in_grad.at[rows_here], sems, base, link.peer),
        pltpu.make_async_copy(one_acc, in_grad.at[rows_here], local_sem.at[3]),
    ]
    seq_cols = pl.ds(pl.multiple_of(link.core * length, length), length)
    first_copies = [
        remote(
            fv_t.at[pl.ds((1 - link.core) * side, side)],
            first_grad.at[:, seq_cols],
            sems,
            base + 1,
            link.peer,
        ),
        pltpu.make_async_copy(
            fv_t.at[pl.ds(link.core * side, side)], first_grad.at[:, seq_cols], local_sem.at[4]
        ),
    ]
    base += 2
    flows = {}
    if ring:
        at_zero, at_one, at_two, at_deep = exports
        whole, hop1, hop2, hop3, deep, deep2, deep3 = ring_scr[:7]
        del ring_scr[:7]
        for slot, chunk in enumerate((0, 2, 3, 4, 5)):
            flows[chunk] = Chunk(
                link,
                sems,
                base + slot * HOPS,
                whole,
                None if chunk == 0 else hop1.at[slot - 1],
                hop2.at[slot],
                hop3.at[slot],
            )
        flows[0].sources[2] = at_two
        flows[2].sources[1] = at_one.at[0]
        flows[3].sources[1] = at_one.at[1]
        flows[4].sources[0] = at_zero
        flows[5].sources[1] = at_one.at[2]
        flows[1] = DeepChunk(
            link, sems, base + 5 * HOPS, None, None, deep, at_deep, deep2, deep3
        )
        ring_loads = [
            pltpu.make_async_copy(at_zero, whole, local_sem.at[5]),
            pltpu.make_async_copy(at_one.at[0], hop1.at[0], local_sem.at[6]),
            pltpu.make_async_copy(at_one.at[1], hop1.at[1], local_sem.at[7]),
            pltpu.make_async_copy(at_one.at[2], hop1.at[3], local_sem.at[8]),
            pltpu.make_async_copy(at_two, hop2.at[0], local_sem.at[9]),
            pltpu.make_async_copy(at_deep, deep, local_sem.at[10]),
        ]
        wholes = {"o": out_scr.at[0]}
        wholes.update({"p%d" % n: grads[n] for n in range(chunks)})
        place_in = base + 6 * HOPS
        for name, whole in wholes.items():
            flows[name] = Chunk(link, sems, place_in, whole, *ring_scr[:3])
            del ring_scr[:3]
            place_in += HOPS
        v_send, v_recv = ring_scr[:2]
        flows["v"] = Chunk(link, sems, place_in, v_recv, *ring_scr[2:5])
        vec_swap = remote(v_send, v_recv, sems, place_in + HOPS, link.peer)

    ready = [(1, 2), (2, 2)]

    def run(events):
        for name, number in events:
            if ring:
                if number > 1 and (name, number) not in ready:
                    flows[name].land(number - 1)
                flows[name].start(number)

    @pl.when(step == 0)
    def _():
        partners = [link.peer]
        if ring:
            partners += [link.x_side, link.y_side]
            partners += [link.z_side(hop) for hop in range(1, link.depth)]
        link.meet(partners)
        if ring:
            flows[3].start(2)
            flows[5].start(2)
            flows[0].start(3)
        out_swap.start()
        go(loads)
        if ring:
            go(ring_loads)
        for block in range(blocks):
            rows = slice(block * BLOCK, (block + 1) * BLOCK)
            n1_t[:, rows] = jnp.transpose(n1_ref[rows, :])
        one_acc[...] = jnp.zeros_like(one_acc)
        fv_t[...] = jnp.zeros_like(fv_t)

    k_t = jnp.transpose(k_ref[...])
    prod_t = jnp.transpose(gheads_ref[...].astype(F32) * att_ref[...].astype(F32))
    lse_pair = lse_ref[0]
    row_pos = lax.broadcasted_iota(jnp.int32, (BLOCK, BLOCK), 0)
    col_pos = lax.broadcasted_iota(jnp.int32, (BLOCK, BLOCK), 1)
    seen = row_pos <= col_pos
    for block in range(blocks):
        cols = slice(block * BLOCK, (block + 1) * BLOCK)
        queries = split_heads(q_ref[cols, :])
        heads_grad = split_heads(gheads_ref[cols, :])
        for head in range(2):
            part = slice(head * HEAD_DIM, (head + 1) * HEAD_DIM)
            delta = jnp.sum(prod_t[part, cols], axis=0, keepdims=True)
            lse = lse_pair[head : head + 1, cols]
            dq = jnp.zeros((HEAD_DIM, BLOCK), F32)
            for source in range(block + 1):
                rows = slice(source * BLOCK, (source + 1) * BLOCK)
                soft = jnp.exp(dot_nt(k_ref[rows, :], queries[head]) - lse)
                if source == block:
                    soft = jnp.where(seen, soft, 0.0)
                dsoft = dot_nt(v_ref[rows, :], heads_grad[head])
                dscore = (soft * (dsoft - delta)).astype(BF16)
                dv = dot_nn(soft.astype(BF16), heads_grad[head])
                dk = dot_nn(dscore, queries[head])
                if head == 0 and source == block:
                    dv_acc[rows, :] = dv
                    dk_acc[rows, :] = dk
                else:
                    dv_acc[rows, :] += dv
                    dk_acc[rows, :] += dk
                dq = dq + dot_nn(k_t[part, rows], dscore)
            dq_t[part, cols] = dq

    middle_events = {
        0: [(4, 1)],
        1: [(5, 3)],
        2: [(4, 2), (2, 3)],
        3: [("p0", 2)],
        4: [("p1", 1), ("p0", 3)],
        5: [("p1", 2)],
    }
    end_events = {
        0: [(2, 2), (3, 3)],
        1: [("p0", 1), (1, 2)],
        3: [("o", 1), (4, 3)],
        4: [("o", 2), (1, 3)],
        5: [("p2", 1), ("o", 3), ("p1", 3)],
    }
    if ring:
        for when, events in middle_events.items():

            @pl.when(step == when)
            def _():
                run(events)

        @pl.when(step == 0)
        def _():
            finish(ring_loads)

    for block in range(blocks):
        rows = slice(block * BLOCK, (block + 1) * BLOCK)
        stack_scr[rows, 0:PAIR] = (jnp.transpose(dq_t[:, rows]) * HEAD_DIM**-0.5).astype(BF16)
        stack_scr[rows, PAIR : 2 * PAIR] = dk_acc[rows, :].astype(BF16)
        dv = dv_acc[rows, :]
        stack_scr[rows, 2 * PAIR : 3 * PAIR] = dv.astype(BF16)
        one_acc[rows, :] += dot_nt(stack_scr[rows, :], w_ref[...])

    @pl.when(step >= 2 * (fresh_width // PAIR))
    def _():
        for block in range(blocks):
            rows = slice(block * BLOCK, (block + 1) * BLOCK)
            dv = dv_acc[rows, :]
            high = dv.astype(BF16)
            low = (dv - high.astype(F32)).astype(BF16)
            fv_t[:, rows] += dot_nt(sel_ref[...], high) + dot_nt(sel_ref[...], low)

    for chunk in range(1, chunks):

        @pl.when(step == 2 * chunk)
        def _():
            swaps[chunk - 1].wait_send()

    post_scr[lax.rem(step, 2)] = dot_nn(n1_t[...], stack_scr[...]).reshape(post_scr.shape[1:])
    for chunk in range(chunks):
        used = grads[chunk].shape[-1]

        @pl.when(step == 2 * chunk)
        def _():
            swaps[chunk].start()

        @pl.when(step == 2 * chunk + 1)
        def _():
            swaps[chunk].wait_recv()
            grads[chunk][...] += post_scr[1, ..., 0:used]
            if chunk == chunks - 1:
                swaps[chunk].wait_send()

    @pl.when(step == 0)
    def _():
        out_swap.wait()
        finish(loads)
        out_scr[0] += out_scr[1]

    if ring:
        for when, events in end_events.items():

            @pl.when(step == when)
            def _():
                run(events)

    @pl.when(step == steps - 1)
    def _():
        go(first_copies)
        sums_scr[...] = jnp.zeros_like(sums_scr)

        def leave(block):
            rows = row_block(block)
            normed, factor = norm_stats(x_scr[rows, :].astype(F32))
            grad_one = one_acc[rows, :]
            sums_scr[0:1, :] += jnp.sum(grad_one * normed, axis=0, keepdims=True)
            sums_scr[1:2, :] += jnp.sum(grad_one, axis=0, keepdims=True)
            one_acc[rows, :] = gmix_scr[rows, :] + norm_backward(
                grad_one, normed, factor, gain_ref[...]
            )

        each(blocks, leave)
        go(in_copies)
        vectors = jnp.concatenate(
            [sums_scr[0:2, :], vec2_ref[0:2, :], jnp.zeros((4, width), F32)], axis=0
        )
        if ring:
            up_out, down_out, q_out, k_out, v_out, o_out, vec_out = outs
            rows_dev = width // dp_size
            v_send[...] = jnp.zeros_like(v_send)
            for block in range(dp_size):
                v_send[block // 4, (block // 2) % 2, block % 2, :, 0:rows_dev] = vectors[
                    :, block * rows_dev : (block + 1) * rows_dev
                ]
            vec_swap.start()
            run([("p2", 2)])
            vec_swap.wait()
            v_recv[...] += v_send[...]
            run([("v", 1)])
            ff_block = up_out.shape[-1] // 6

            def put_ffn(index, total):
                cols = slice(index * ff_block, (index + 1) * ff_block)
                down_out[:, cols] = total[:, 0:ff_block]
                up_out[:, cols] = total[:, ff_block:]

            def put_proj(index, total):
                cols = slice(index * PAIR, (index + 1) * PAIR)
                q_out[:, cols] = total[:, 0:PAIR]
                k_out[:, cols] = total[:, PAIR : 2 * PAIR]
                if total.shape[1] > 2 * PAIR:
                    last = min((index + 1) * PAIR, fresh_width)
                    v_out[:, index * PAIR : last] = total[
                        :, 2 * PAIR : 2 * PAIR + last - index * PAIR
                    ]

            for chunk in range(6):
                put_ffn(chunk, flows[chunk].total())
            o_out[...] = flows["o"].total()
            run([("v", 2), ("p2", 3), ("v", 3)])
            put_proj(0, flows["p0"].total())
            put_proj(1, flows["p1"].total())
            put_proj(2, flows["p2"].total())
            vec_out[...] = flows["v"].total()
        else:
            vec_out = outs[-1]
            vec_out[...] = vectors
            stores = [
                pltpu.make_async_copy(grads[chunk], outs[chunk], local_sem.at[5 + chunk])
                for chunk in range(chunks)
            ]
            stores.append(pltpu.make_async_copy(out_scr.at[0], outs[chunks], local_sem.at[8]))
            go(stores)
            finish(stores)
        finish(in_copies)
        finish(first_copies)


def back(
    dp_size,
    ring,
    tokens,
    n1,
    q,
    k,
    v,
    attended,
    grad_heads,
    lse,
    grad_mixed,
    gain,
    weights,
    select,
    og_own,
    og_peer,
    vec2,
    exports,
    fresh_width,
    own_ff,
):
    width = tokens.shape[1]
    own_width = og_own.shape[-1]
    half = own_width // PAIR
    fv_width = select.shape[0]
    side = fv_width // 2
    pair_of = lambda i: lax.rem(i + 1, 2) * half + lax.div(i, 2)
    pair_block = pl.BlockSpec((SEQ_LEN, PAIR), lambda i: (0, pair_of(i)))
    used = [3 * PAIR if n * PAIR < fresh_width else 2 * PAIR for n in range(half)]
    grad_shapes = [place(ring, width, dp_size, columns) for columns in used]
    og_shape = place(ring, width, dp_size, own_width)
    scratch = [
        pltpu.VMEM((SEQ_LEN, width), BF16),
        pltpu.VMEM((SEQ_LEN, width), F32),
        pltpu.VMEM((width, SEQ_LEN), BF16),
        pltpu.VMEM((SEQ_LEN, PAIR), F32),
        pltpu.VMEM((SEQ_LEN, PAIR), F32),
        pltpu.VMEM((PAIR, SEQ_LEN), F32),
        pltpu.VMEM((SEQ_LEN, 3 * PAIR), BF16),
        pltpu.VMEM((SEQ_LEN, width), F32),
        pltpu.VMEM((fv_width, SEQ_LEN), F32),
        pltpu.VMEM((2,) + grad_shapes[0], F32),
        pltpu.VMEM((2,) + og_shape, F32),
        pltpu.VMEM((8, width), F32),
        pltpu.SemaphoreType.DMA((11,)),
    ]
    n_sems = 3 + half + (1 + (8 + half) * HOPS if ring else 0)
    scratch += [pltpu.SemaphoreType.DMA((n_sems,))] * 2
    scratch += [pltpu.VMEM(shape, F32) for shape in grad_shapes]
    if ring:
        depth, rows = dp_size // 4, width // dp_size

        def hops(columns, first, height=rows):
            shapes = [
                (2, depth // 2, 2, height, columns),
                (depth, height, columns),
                (depth - 1, height, columns),
            ]
            return [pltpu.VMEM(shape, F32) for shape in shapes[first:]]

        ff = exports[0].shape[-1]
        scratch += [
            pltpu.VMEM(place(ring, width, dp_size, ff), F32),
            pltpu.VMEM((4, 2, depth // 2, 2, rows, ff), F32),
            pltpu.VMEM((5, depth, rows, ff), F32),
            pltpu.VMEM((5, depth - 1, rows, ff), F32),
            pltpu.VMEM((2, 2, rows, ff), F32),
            pltpu.VMEM((2, 2, rows, ff // 2), F32),
            pltpu.VMEM((2, rows, ff // 2), F32),
        ]
        scratch += hops(own_width, 0)
        for columns in used:
            scratch += hops(columns, 0)
        vec_whole = pltpu.VMEM((depth, 2, 2, 8, PAIR), F32)
        scratch += [vec_whole, vec_whole] + hops(PAIR, 0, 8)
        totals = [
            (rows, own_ff),
            (rows, own_ff),
            (rows, own_width),
            (rows, own_width),
            (rows, fresh_width),
            (rows, own_width),
            (8, PAIR),
        ]
        total_specs = [fixed(shape) for shape in totals]
        export_args = list(exports)
        export_specs = [ANY] * len(export_args)
    else:
        totals = grad_shapes + [og_shape, (8, width)]
        total_specs = [ANY] * (half + 1) + [fixed((8, width))]
        export_args, export_specs = [], []
    in_specs = [
        ANY,
        fixed((SEQ_LEN, width)),
        pair_block,
        pair_block,
        pair_block,
        pair_block,
        pair_block,
        pl.BlockSpec((1, 8, SEQ_LEN), lambda i: (pair_of(i), 0, 0)),
        ANY,
        fixed((1, width)),
        pl.BlockSpec((width, 3 * PAIR), lambda i: (0, pair_of(i))),
        pl.BlockSpec((fv_width, PAIR), lambda i: (0, pair_of(i))),
        ANY,
        ANY,
        fixed((8, width)),
    ] + export_specs
    return pl.pallas_call(
        functools.partial(
            back_kernel, dp_size, ring, (len(in_specs), 2 + len(totals), fresh_width)
        ),
        grid=(2 * half,),
        in_specs=in_specs,
        out_specs=[ANY, ANY] + total_specs,
        scratch_shapes=scratch,
        out_shape=[
            jax.ShapeDtypeStruct((2 * SEQ_LEN, width), F32),
            jax.ShapeDtypeStruct((side, 2 * SEQ_LEN), F32),
        ]
        + [jax.ShapeDtypeStruct(shape, F32) for shape in totals],
        compiler_params=params(2),
        name="back",
    )(
        tokens,
        n1,
        q,
        k,
        v,
        attended,
        grad_heads,
        lse,
        grad_mixed,
        gain,
        weights,
        select,
        og_own,
        og_peer,
        vec2,
        *export_args,
    )


def on_device(
    dp_size,
    tokens,
    first_values,
    seq_count,
    skip_map,
    norm1_gain,
    norm1_shift,
    query_weight,
    key_weight,
    value_weight,
    out_weight,
    norm2_gain,
    norm2_shift,
    up_weight,
    down_weight,
    cotangent,
):
    width = tokens.shape[1]
    own_width = query_weight.shape[1]
    fresh_width = value_weight.shape[1]
    own_ff = up_weight.shape[1]
    ring = ring_of(dp_size, width)
    gain1, shift1 = norm1_gain[None, :], norm1_shift[None, :]
    gain2, shift2 = norm2_gain[None, :], norm2_shift[None, :]
    n1, q, k, v, attended, lse, weights, select, out_peer, up_peer, down_peer = front(
        dp_size,
        tokens,
        first_values,
        skip_map,
        gain1,
        shift1,
        query_weight,
        key_weight,
        value_weight.T,
        out_weight,
        up_weight,
        down_weight,
    )
    layer_out, grad_mixed, grad_heads, og_own, og_peer, vec2, *exports = middle(
        dp_size,
        ring,
        tokens,
        attended,
        cotangent,
        seq_count,
        gain2,
        shift2,
        out_weight,
        out_peer,
        (up_weight, down_weight),
        (up_peer, down_peer),
    )
    input_grad, first_grad, *totals = back(
        dp_size,
        ring,
        tokens,
        n1,
        q,
        k,
        v,
        attended,
        grad_heads,
        lse,
        grad_mixed,
        gain1,
        weights,
        select,
        og_own,
        og_peer,
        vec2,
        exports,
        fresh_width,
        own_ff,
    )
    first_grad = first_grad.T
    if ring:
        up_total, down_t, query_total, key_total, value_total, out_t, vectors = totals
        rows = width // dp_size
        down_total, out_total = down_t.T, out_t.T
        gain1_total, shift1_total, gain2_total, shift2_total = (vectors[n, :rows] for n in range(4))
    else:
        *proj, out_grad, vectors = totals
        chunks = exports[0].shape[0]
        ff_block = own_ff // chunks
        vectors = vectors + lax.ppermute(vectors, "tensor", [(0, 1), (1, 0)])
        columns = list(proj) + [out_grad] + [exports[0][n] for n in range(chunks)]
        packed = jnp.concatenate(columns + [jnp.pad(vectors.T, ((0, 0), (0, 120)))], axis=1)
        summed = lax.psum_scatter(packed, "dp", scatter_dimension=0, tiled=True)
        heads, start = [[], [], []], 0
        for part in proj:
            for n in range(part.shape[1] // PAIR):
                heads[n].append(summed[:, start : start + PAIR])
                start += PAIR
        query_total, key_total, value_total = (jnp.concatenate(part, axis=1) for part in heads)
        value_total = value_total[:, :fresh_width]
        out_total = summed[:, start : start + own_width].T
        start += own_width
        pairs = summed[:, start : start + 2 * own_ff].reshape(-1, chunks, 2, ff_block)
        down_total = pairs[:, :, 0].reshape(-1, own_ff).T
        up_total = pairs[:, :, 1].reshape(-1, own_ff)
        start += 2 * own_ff
        gain1_total, shift1_total, gain2_total, shift2_total = (
            summed[:, start + n] for n in range(4)
        )
    return (
        layer_out,
        input_grad,
        first_grad,
        gain1_total,
        shift1_total,
        query_total,
        key_total,
        value_total,
        out_total,
        gain2_total,
        shift2_total,
        up_total,
        down_total,
    )


def solution(mesh):
    placed = (
        P("dp", None),
        P("dp", None),
        P("dp"),
        P("tensor"),
        P(),
        P(),
        P(None, "tensor"),
        P(None, "tensor"),
        P(None, "tensor"),
        P("tensor", None),
        P(),
        P(),
        P(None, "tensor"),
        P("tensor", None),
        P("dp", None),
    )
    return jax.shard_map(
        functools.partial(on_device, mesh.shape["dp"]),
        mesh=mesh,
        in_specs=placed,
        out_specs=(
            P("dp", None),
            P("dp", None),
            P("dp", "tensor"),
            P("dp"),
            P("dp"),
            P("dp", "tensor"),
            P("dp", "tensor"),
            P("dp", "tensor"),
            P("tensor", "dp"),
            P("dp"),
            P("dp"),
            P("dp", "tensor"),
            P("tensor", "dp"),
        ),
        check_vma=False,
    )
```

```python
import functools

import jax
import jax.numpy as jnp
from jax import lax
from jax.experimental import pallas as pl
from jax.experimental.pallas import tpu as pltpu
from jax.sharding import PartitionSpec as P

HEAD_DIM = 64
SEQ_LEN = 1024
BLOCK = 256
PAIR = 2 * HEAD_DIM
EPS = 1e-05
FILL = -1e30

F32 = jnp.float32
BF16 = jnp.bfloat16


def dot_nn(left, right):
    return lax.dot_general(left, right, (((1,), (0,)), ((), ())), preferred_element_type=F32)


def dot_nt(left, right):
    return lax.dot_general(left, right, (((1,), (1,)), ((), ())), preferred_element_type=F32)


def norm_stats(values_in):
    average = jnp.mean(values_in, axis=-1, keepdims=True)
    centered = values_in - average
    variance = jnp.mean(centered * centered, axis=-1, keepdims=True)
    factor = lax.rsqrt(variance + EPS)
    return centered * factor, factor


def norm_backward(grad, normed, factor, gain):
    scaled = grad * gain
    mean_plain = jnp.mean(scaled, axis=-1, keepdims=True)
    mean_cross = jnp.mean(scaled * normed, axis=-1, keepdims=True)
    return factor * (scaled - mean_plain - normed * mean_cross)


def each(count, body):
    lax.fori_loop(0, count, lambda index, carry: (body(index), carry)[1], 0)


def row_block(index):
    return pl.ds(pl.multiple_of(index * BLOCK, BLOCK), BLOCK)


def recast(source, target, rows=64):
    def one(index):
        part = pl.ds(pl.multiple_of(index * rows, rows), rows)
        target[part, :] = source[part, :].astype(target.dtype)

    each(source.shape[0] // rows, one)


def head_masks(rows):
    lanes = lax.broadcasted_iota(jnp.int32, (rows, PAIR), 1)
    return lanes < HEAD_DIM


def split_heads(pair_rows):
    first = head_masks(pair_rows.shape[0])
    zero = jnp.zeros_like(pair_rows)
    return jnp.where(first, pair_rows, zero), jnp.where(first, zero, pair_rows)


MESH = pl.DeviceIdType.MESH


def params(collective_id, vmem_mib):
    return pltpu.CompilerParams(
        vmem_limit_bytes=vmem_mib * 1024 * 1024,
        collective_id=collective_id,
        has_side_effects=True,
    )


def fixed(shape):
    zeros = (0,) * len(shape)
    return pl.BlockSpec(shape, lambda i: zeros, pipeline_mode=pl.Buffered(1))


ANY = pl.BlockSpec(memory_space=pl.ANY)
SMEM = pl.BlockSpec(memory_space=pltpu.SMEM)


def ring_of(dp_size, width):
    rows = width // dp_size
    return dp_size % 8 == 0 and width % dp_size == 0 and rows % 8 == 0


def place(ring, width, dp_size, columns):
    if not ring:
        return (width, columns)
    return (dp_size // 4, 2, 2, width // dp_size, columns)


class Link:
    def __init__(self, dp_size):
        self.dp = lax.axis_index("dp")
        self.core = lax.axis_index("tensor")
        self.depth = dp_size // 4
        self.x = lax.rem(self.dp, 2)
        self.y = lax.rem(lax.div(self.dp, 2), 2)
        self.z = lax.div(self.dp, 4)
        self.peer = {"tensor": 1 - self.core}
        self.x_side = {"dp": self.dp + 1 - 2 * self.x}
        self.y_side = {"dp": self.dp + 2 - 4 * self.y}

    def z_place(self, hop):
        return lax.rem(self.z + hop, self.depth)

    def z_side(self, hop):
        return {"dp": 4 * self.z_place(hop) + lax.rem(self.dp, 4)}

    def greet(self, partners):
        barrier = pltpu.get_barrier_semaphore()
        for partner in partners:
            pl.semaphore_signal(barrier, inc=1, device_id=partner, device_id_type=MESH)

    def meet(self, partners):
        pl.semaphore_wait(pltpu.get_barrier_semaphore(), len(partners))


def remote(source, target, sems, index, device):
    send, recv = sems
    return pltpu.make_async_remote_copy(
        src_ref=source,
        dst_ref=target,
        send_sem=send.at[index],
        recv_sem=recv.at[index],
        device_id=device,
        device_id_type=MESH,
    )


def first_hop(link, source, landing, sems, base):
    low = link.depth // 2
    return [
        remote(
            source.at[0:low, :, 1 - link.x], landing.at[0], sems, base, link.x_side
        ),
        remote(
            source.at[low : 2 * low, 1 - link.y],
            landing.at[1],
            sems,
            base + 1,
            link.y_side,
        ),
    ]


def second_hop(link, source, landing, sems, base):
    low = link.depth // 2
    return [
        remote(
            source.at[0, :, 1 - link.y],
            landing.at[0:low],
            sems,
            base,
            link.y_side,
        ),
        remote(
            source.at[1, :, 1 - link.x],
            landing.at[low : 2 * low],
            sems,
            base + 1,
            link.x_side,
        ),
    ]


def last_hop(link, source, landing, sems, base):
    return [
        remote(
            source.at[link.z_place(hop)],
            landing.at[hop - 1],
            sems,
            base + hop - 1,
            link.z_side(hop),
        )
        for hop in range(1, link.depth)
    ]


def go(copies):
    for copy in copies:
        copy.start()


def finish(copies):
    for copy in copies:
        copy.wait()


def merge_first(link, whole, landing):
    low = link.depth // 2

    def one(row):
        for other in range(2):
            landing[0, row, other] += whole[row, other, link.x]
            landing[1, row, other] += whole[low + row, link.y, other]

    each(low, one)


def merge_second(link, landed, landing):
    low = link.depth // 2

    def one(row):
        landing[row] += landed[0, row, link.y]
        landing[low + row] += landed[1, row, link.x]

    each(low, one)


def total_last(own, landing):
    total = own
    for hop in range(landing.shape[0]):
        total = total + landing[hop]
    return total


HOPS = 7


class Chunk:
    def __init__(self, link, sems, base, whole=None, hop1=None, hop2=None, hop3=None):
        self.link, self.whole, self.hop1, self.hop2, self.hop3 = link, whole, hop1, hop2, hop3
        self.sems, self.base = sems, base
        self.sources = [whole, hop1, hop2]

    def hop(self, number):
        source = self.sources[number - 1]
        if number == 1:
            return first_hop(self.link, source, self.hop1, self.sems, self.base)
        if number == 2:
            return second_hop(self.link, source, self.hop2, self.sems, self.base + 2)
        return last_hop(self.link, source, self.hop3, self.sems, self.base + 4)

    def start(self, number):
        go(self.hop(number))

    def land(self, number):
        finish(self.hop(number))
        if number == 1:
            merge_first(self.link, self.whole, self.hop1)
        elif number == 2:
            merge_second(self.link, self.hop1, self.hop2)

    def total(self):
        finish(self.hop(3))
        return total_last(self.hop2[self.link.z], self.hop3)


class DeepChunk:
    def __init__(self, link, sems, base, whole, hop1, summed, source, hop2, hop3):
        self.link, self.whole, self.hop1, self.hop2, self.hop3 = link, whole, hop1, hop2, hop3
        self.summed, self.source = summed, source
        self.sems, self.base = sems, base

    def hop(self, number):
        link, sems, base = self.link, self.sems, self.base
        if number == 1:
            return last_hop(link, self.whole, self.hop1, sems, base)
        side = self.hop3.shape[-1]
        left, right = pl.ds(0, side), pl.ds(side, side)
        if number == 2:
            base += link.depth - 1
            summed = self.source
            return [
                remote(
                    summed.at[:, 1 - link.x, :, left], self.hop2.at[0], sems, base, link.x_side
                ),
                remote(
                    summed.at[1 - link.y, :, :, right], self.hop2.at[1], sems, base + 1, link.y_side
                ),
            ]
        base += link.depth + 1
        return [
            remote(self.hop2.at[0, 1 - link.y], self.hop3.at[0], sems, base, link.y_side),
            remote(self.hop2.at[1, 1 - link.x], self.hop3.at[1], sems, base + 1, link.x_side),
        ]

    def start(self, number):
        go(self.hop(number))

    def land(self, number):
        link = self.link
        finish(self.hop(number))
        if number == 1:

            def one(row):
                for other in range(2):
                    total = self.whole[link.z, row, other]
                    for hop in range(self.hop1.shape[0]):
                        total = total + self.hop1[hop, row, other]
                    self.summed[row, other] = total

            each(2, one)
        else:
            side = self.hop3.shape[-1]
            for other in range(2):
                self.hop2[0, other] += self.summed[other, link.x, :, 0:side]
                self.hop2[1, other] += self.summed[link.y, other, :, side:]

    def total(self):
        finish(self.hop(3))
        return jnp.concatenate(
            [self.hop2[0, self.link.y] + self.hop3[0], self.hop2[1, self.link.x] + self.hop3[1]],
            axis=-1,
        )


def front_kernel(
    dp_size,
    tokens,
    first_values,
    skip_map,
    gain_ref,
    shift_ref,
    wq_ref,
    wk_ref,
    wv_ref,
    out_w,
    up_w,
    down_w,
    n1_ref,
    q_ref,
    k_ref,
    v_ref,
    att_ref,
    lse_ref,
    w_ref,
    sel_ref,
    out_peer,
    up_peer,
    down_peer,
    x_scr,
    fv_scr,
    proj_own,
    proj_send,
    proj_recv,
    sel_send,
    sel_recv,
    out_low,
    up_low,
    down_low,
    out_send,
    up_send,
    down_send,
    out_recv,
    up_recv,
    down_recv,
    lse_scr,
    local_sem,
    send_sem,
    recv_sem,
):
    step = pl.program_id(0)
    length, width = x_scr.shape
    blocks = length // BLOCK
    half = pl.num_programs(0) // 2
    own_width = wq_ref.shape[1]
    fresh_width = wv_ref.shape[0]
    fv_width = fv_scr.shape[1]
    link = Link(dp_size)
    sems = (send_sem, recv_sem)
    rows_here = pl.ds(link.core * length, length)
    local = [
        pltpu.make_async_copy(tokens.at[rows_here], x_scr, local_sem.at[0]),
        pltpu.make_async_copy(first_values.at[rows_here], fv_scr, local_sem.at[1]),
        pltpu.make_async_copy(up_w, up_low, local_sem.at[2]),
        pltpu.make_async_copy(down_w, down_low, local_sem.at[3]),
        pltpu.make_async_copy(out_w, out_low, local_sem.at[4]),
    ]
    early = [
        remote(proj_send, proj_recv, sems, 0, link.peer),
        remote(sel_send, sel_recv, sems, 1, link.peer),
    ]
    late = [
        remote(up_send, up_recv, sems, 2, link.peer),
        remote(down_send, down_recv, sems, 3, link.peer),
        remote(out_send, out_recv, sems, 4, link.peer),
    ]
    landed = [
        (late[0], up_recv, up_low, pltpu.make_async_copy(up_low, up_peer, local_sem.at[2])),
        (late[1], down_recv, down_low, pltpu.make_async_copy(down_low, down_peer, local_sem.at[3])),
        (late[2], out_recv, out_low, pltpu.make_async_copy(out_low, out_peer, local_sem.at[4])),
    ]

    @pl.when(step == 0)
    def _():
        link.greet([link.peer])
        go(local)
        proj_own[2, :, 0:fresh_width] = jnp.transpose(wv_ref[...])
        proj_own[2, :, fresh_width:] = jnp.zeros((width, own_width - fresh_width), BF16)
        for part, source in enumerate((wq_ref, wk_ref)):
            recast(source, proj_own.at[part])
        for part in range(3):
            recast(proj_own.at[part], proj_send.at[part])
        row = lax.broadcasted_iota(jnp.int32, (fv_width, own_width), 0)
        col = lax.broadcasted_iota(jnp.int32, (fv_width, own_width), 1)
        slots = (own_width - fresh_width) // HEAD_DIM
        target = jnp.full((fv_width, own_width), -1, jnp.int32)
        for slot in range(slots):
            start = fresh_width + slot * HEAD_DIM
            inside = jnp.logical_and(col >= start, col < start + HEAD_DIM)
            target = jnp.where(inside, skip_map[slot] * HEAD_DIM + col - start, target)
        chosen = jnp.where(row == target, 1.0, 0.0).astype(F32)
        sel_send[...] = chosen
        sel_ref[:, 0:own_width] = chosen.astype(BF16)
        link.meet([link.peer])
        go(early)
        lse_scr[...] = jnp.zeros_like(lse_scr)
        local[0].wait()
        local[1].wait()

        def one(block, carry):
            rows = pl.ds(block * BLOCK, BLOCK)
            normed, _ = norm_stats(x_scr[rows, :].astype(F32))
            n1_ref[rows, :] = (normed * gain_ref[...][None, :] + shift_ref[...][None, :]).astype(BF16)
            return carry

        lax.fori_loop(0, blocks, one, 0)

    @pl.when(step == half)
    def _():
        finish(early)
        sel_ref[:, own_width:] = sel_recv[...].astype(BF16)

    @pl.when(step < half)
    def _():
        cols = pl.ds(pl.multiple_of(step * PAIR, PAIR), PAIR)
        for part in range(3):
            w_ref[:, part * PAIR : (part + 1) * PAIR] = proj_own[part, :, cols]

    @pl.when(step >= half)
    def _():
        cols = pl.ds(pl.multiple_of((step - half) * PAIR, PAIR), PAIR)
        for part in range(3):
            w_ref[:, part * PAIR : (part + 1) * PAIR] = proj_recv[part, :, cols].astype(BF16)

    sel_cols = pl.ds(pl.multiple_of(step * PAIR, PAIR), PAIR)
    for block in range(blocks):
        rows = slice(block * BLOCK, (block + 1) * BLOCK)
        fused = dot_nn(n1_ref[rows, :], w_ref[...])
        picked = dot_nn(fv_scr[rows, :], sel_ref[:, sel_cols])
        q_ref[rows, :] = (fused[:, 0:PAIR].astype(BF16).astype(F32) * HEAD_DIM**-0.5).astype(BF16)
        k_ref[rows, :] = fused[:, PAIR : 2 * PAIR].astype(BF16)
        v_ref[rows, :] = (fused[:, 2 * PAIR :] + picked).astype(BF16)

    lane = lax.broadcasted_iota(jnp.int32, (BLOCK, PAIR), 1)
    row_pos = lax.broadcasted_iota(jnp.int32, (BLOCK, BLOCK), 0)
    col_pos = lax.broadcasted_iota(jnp.int32, (BLOCK, BLOCK), 1)
    seen = col_pos <= row_pos
    items = [(block, head) for block in range(blocks) for head in range(2)]
    scores, weights, partial = {}, {}, {}

    def score(index):
        block, head = items[index]
        lo, hi = block * BLOCK, (block + 1) * BLOCK
        query = split_heads(q_ref[lo:hi, :])[head]
        diag = dot_nt(query, k_ref[lo:hi, :])
        scores[index] = (diag, dot_nt(query, k_ref[0:lo, :]) if block else None)

    def soften(index):
        block, head = items[index]
        lo, hi = block * BLOCK, (block + 1) * BLOCK
        diag, past = scores.pop(index)
        diag = jnp.where(seen, diag, FILL)
        peak = jnp.max(diag, axis=-1, keepdims=True)
        if block:
            peak = jnp.maximum(peak, jnp.max(past, axis=-1, keepdims=True))
        diag = jnp.exp(diag - peak)
        mass = jnp.sum(diag, axis=-1, keepdims=True)
        if block:
            past = jnp.exp(past - peak)
            mass = mass + jnp.sum(past, axis=-1, keepdims=True)
        inverse = 1.0 / mass
        weights[index] = (
            (diag * inverse).astype(BF16),
            (past * inverse).astype(BF16) if block else None,
        )
        lse_scr[lo:hi, :] = jnp.where(
            lane == 2 * step + head, peak + jnp.log(mass), lse_scr[lo:hi, :]
        )

    def attend(index):
        block, head = items[index]
        lo, hi = block * BLOCK, (block + 1) * BLOCK
        diag, past = weights.pop(index)
        total = dot_nn(diag, split_heads(v_ref[lo:hi, :])[head])
        if block:
            total = total + dot_nn(past, split_heads(v_ref[0:lo, :])[head])
        if head == 0:
            partial[block] = total
        else:
            att_ref[lo:hi, :] = (partial.pop(block) + total).astype(BF16)

    for index in range(len(items) + 2):
        if index < len(items):
            score(index)
        if 0 <= index - 1 < len(items):
            soften(index - 1)
        if index >= 2:
            attend(index - 2)

    @pl.when(step == 0)
    def _():
        for copy in local[2:]:
            copy.wait()
        recast(up_low, up_send)
        recast(down_low, down_send)
        recast(out_low, out_send)
        go(late)

    @pl.when(step == pl.num_programs(0) - 2)
    def _():
        for copy, recv, low, store in landed:
            copy.wait()
            recast(recv, low)
            store.start()

    @pl.when(step == pl.num_programs(0) - 1)
    def _():
        for block in range(blocks):
            lo, hi = block * BLOCK, (block + 1) * BLOCK
            turned = jnp.transpose(lse_scr[lo:hi, :])
            for pair in range(lse_ref.shape[0]):
                lse_ref[pair, 0:2, lo:hi] = turned[2 * pair : 2 * pair + 2, :]
        for _, _, _, store in landed:
            store.wait()


def front(dp_size, tokens, first_values, skip_map, gain, shift, wq, wk, wv, out_w, up_w, down_w):
    width = tokens.shape[1]
    own_width = wq.shape[1]
    half = own_width // PAIR
    fv_width = first_values.shape[1]
    pair_block = pl.BlockSpec((SEQ_LEN, PAIR), lambda i: (0, i))
    pair_out = jax.ShapeDtypeStruct((SEQ_LEN, 2 * own_width), BF16)
    return pl.pallas_call(
        functools.partial(front_kernel, dp_size),
        grid=(2 * half,),
        in_specs=[
            ANY,
            ANY,
            SMEM,
            fixed((width,)),
            fixed((width,)),
            fixed(wq.shape),
            fixed(wk.shape),
            fixed(wv.shape),
            ANY,
            ANY,
            ANY,
        ],
        out_specs=[
            fixed((SEQ_LEN, width)),
            pair_block,
            pair_block,
            pair_block,
            pair_block,
            fixed((2 * half, 8, SEQ_LEN)),
            pl.BlockSpec((width, 3 * PAIR), lambda i: (0, i)),
            fixed((fv_width, 2 * own_width)),
            ANY,
            ANY,
            ANY,
        ],
        scratch_shapes=[
            pltpu.VMEM((SEQ_LEN, width), BF16),
            pltpu.VMEM((SEQ_LEN, fv_width), BF16),
            pltpu.VMEM((3, width, own_width), BF16),
            pltpu.VMEM((3, width, own_width), F32),
            pltpu.VMEM((3, width, own_width), F32),
            pltpu.VMEM((fv_width, own_width), F32),
            pltpu.VMEM((fv_width, own_width), F32),
            pltpu.VMEM(out_w.shape, BF16),
            pltpu.VMEM(up_w.shape, BF16),
            pltpu.VMEM(down_w.shape, BF16),
            pltpu.VMEM(out_w.shape, F32),
            pltpu.VMEM(up_w.shape, F32),
            pltpu.VMEM(down_w.shape, F32),
            pltpu.VMEM(out_w.shape, F32),
            pltpu.VMEM(up_w.shape, F32),
            pltpu.VMEM(down_w.shape, F32),
            pltpu.VMEM((SEQ_LEN, PAIR), F32),
            pltpu.SemaphoreType.DMA((5,)),
            pltpu.SemaphoreType.DMA((5,)),
            pltpu.SemaphoreType.DMA((5,)),
        ],
        out_shape=[
            jax.ShapeDtypeStruct((SEQ_LEN, width), BF16),
            pair_out,
            pair_out,
            pair_out,
            pair_out,
            jax.ShapeDtypeStruct((2 * half, 8, SEQ_LEN), F32),
            jax.ShapeDtypeStruct((width, 6 * own_width), BF16),
            jax.ShapeDtypeStruct((fv_width, 2 * own_width), BF16),
            jax.ShapeDtypeStruct(out_w.shape, BF16),
            jax.ShapeDtypeStruct(up_w.shape, BF16),
            jax.ShapeDtypeStruct(down_w.shape, BF16),
        ],
        compiler_params=params(0, 60),
        name="front",
    )(tokens, first_values, skip_map, gain, shift, wq, wk, wv, out_w, up_w, down_w)


def gelu_pair(upper):
    scale = (2.0 / jnp.pi) ** 0.5
    square = upper * upper
    inner = upper * (scale + (scale * 0.044715) * square)
    tanh = jnp.tanh(inner)
    cdf = 0.5 + 0.5 * tanh
    slope = cdf + 0.5 * upper * (1.0 - tanh * tanh) * (scale + (3.0 * scale * 0.044715) * square)
    return upper * cdf, slope


def middle_kernel(dp_size, ring, n_exports, *refs):
    (
        tokens,
        att_ref,
        cotangent,
        seq_count,
        gain_ref,
        shift_ref,
        wo_own,
        wo_peer,
        up_own,
        down_own,
        up_peer,
        down_peer,
        layer_out,
        gmix_out,
        gheads_ref,
        og_own,
        og_peer,
        vec_ref,
    ) = refs[:18]
    exports = refs[18 : 18 + n_exports]
    (
        mixed_scr,
        stage_scr,
        two_scr,
        low_scr,
        two_t,
        low_t,
        act_scr,
        gup_scr,
        up_scr,
        down_scr,
        wo_scr,
        post_scr,
        grad_scr,
        local_sem,
        send_sem,
        recv_sem,
    ) = refs[18 + n_exports : 34 + n_exports]
    ring_scr = refs[34 + n_exports :]
    step = pl.program_id(0)
    steps = pl.num_programs(0)
    length, width = mixed_scr.shape
    blocks = length // BLOCK
    own_width = wo_own.shape[0]
    own_ff = up_own.shape[1]
    chunks = grad_scr.shape[0]
    ff_block = own_ff // chunks
    link = Link(dp_size)
    sems = (send_sem, recv_sem)
    rows_here = pl.ds(link.core * length, length)
    x_ref = gheads_ref
    loads = [
        pltpu.make_async_copy(tokens.at[rows_here], x_ref, local_sem.at[0]),
        pltpu.make_async_copy(wo_own, wo_scr.at[pl.ds(0, own_width)], local_sem.at[1]),
        pltpu.make_async_copy(wo_peer, wo_scr.at[pl.ds(own_width, own_width)], local_sem.at[2]),
        pltpu.make_async_copy(cotangent.at[rows_here], low_scr, local_sem.at[3]),
    ]
    weight_loads = [
        pltpu.make_async_copy(up_own, up_scr.at[:, pl.ds(0, own_ff)], local_sem.at[4]),
        pltpu.make_async_copy(up_peer, up_scr.at[:, pl.ds(own_ff, own_ff)], local_sem.at[5]),
        pltpu.make_async_copy(down_own, down_scr.at[pl.ds(0, own_ff)], local_sem.at[6]),
        pltpu.make_async_copy(down_peer, down_scr.at[pl.ds(own_ff, own_ff)], local_sem.at[7]),
    ]
    gmix_copy = pltpu.make_async_copy(mixed_scr, gmix_out, local_sem.at[8])

    def layer_copies(block):
        rows = pl.ds(link.core * length + block * BLOCK, BLOCK)
        return [
            pltpu.make_async_copy(
                stage_scr.at[lax.rem(block, 2)], layer_out.at[rows], local_sem.at[9 + block]
            ),
            remote(stage_scr.at[lax.rem(block, 2)], layer_out.at[rows], sems, block, link.peer),
        ]


    def swap(chunk):
        return remote(
            post_scr.at[lax.rem(chunk, 2)], grad_scr.at[chunk], sems, blocks + chunk, link.peer
        )

    flows = {}
    if ring:
        base = blocks + chunks
        hop1, hop2, deep1 = ring_scr
        for slot, chunk in enumerate((0, 2, 3, 5)):
            flows[chunk] = Chunk(
                link,
                sems,
                base + HOPS * chunk,
                grad_scr.at[chunk],
                hop1.at[slot],
                None if chunk else hop2,
            )
        flows[1] = DeepChunk(
            link, sems, base + HOPS, grad_scr.at[1], deep1, deep1.at[0], None, None, None
        )

    partners = [link.peer]
    if ring:
        partners += [link.x_side, link.y_side]
        partners += [link.z_side(hop) for hop in range(1, link.depth)]

    def run(events):
        for chunk, number in events:
            if ring:
                if number > 1:
                    flows[chunk].land(number - 1)
                flows[chunk].start(number)

    @pl.when(step == 0)
    def _():
        link.greet(partners)
        go(loads)
        go(weight_loads)
        finish(loads)
        live = jnp.where(link.core < seq_count[0], 1.0, 0.0).astype(F32)

        def enter(block):
            rows = row_block(block)
            mixed = x_ref[rows, :].astype(F32) + dot_nn(att_ref[rows, :], wo_scr[...])
            mixed_scr[rows, :] = mixed
            normed, _ = norm_stats(mixed)
            two_low = (normed * gain_ref[...][None, :] + shift_ref[...][None, :]).astype(BF16)
            two_scr[rows, :] = two_low
            two_t[:, rows] = jnp.transpose(two_low)
            low = (low_scr[rows, :].astype(F32) * live).astype(BF16)
            low_scr[rows, :] = low
            low_t[:, rows] = jnp.transpose(low)

        each(blocks, enter)
        finish(weight_loads)
        link.meet(partners)

    last = lax.div(step, steps - 1)
    mine = (1 - lax.rem(step, 2)) * lax.div(step + steps - 1, steps) + last
    mine_index = lax.div(step - 1 + lax.div(steps - step, steps), 2)
    post_index = lax.div(step + 1, 2)
    turn = mine * mine_index + (1 - mine) * (chunks + post_index)
    slot = 2 * mine + (1 - mine) * lax.rem(post_index, 2)
    cols = pl.ds(pl.multiple_of(turn * ff_block, ff_block), ff_block)
    for block in range(blocks):
        rows = slice(block * BLOCK, (block + 1) * BLOCK)
        upper = dot_nn(two_scr[rows, :], up_scr[:, cols])
        active, slope = gelu_pair(upper)
        act_scr[rows, cols] = active.astype(BF16)
        grad_active = dot_nt(low_scr[rows, :], down_scr[cols, :])
        gup_scr[rows, cols] = (grad_active * slope).astype(BF16)

    block_shape = grad_scr.shape[1:-1] + (ff_block,)
    @pl.when(jnp.logical_and(mine == 0, post_index > 1))
    def _():
        swap(post_index - 2).wait_send()

    post_scr[slot, ..., 0:ff_block] = dot_nn(low_t[...], act_scr[:, cols]).reshape(block_shape)
    post_scr[slot, ..., ff_block:] = dot_nn(two_t[...], gup_scr[:, cols]).reshape(block_shape)

    @pl.when(mine == 0)
    def _():
        swap(post_index).start()

    @pl.when(mine == 1)
    def _():
        swap(mine_index).wait_recv()
        grad_scr[mine_index] += post_scr[2]

    if ring:
        for when, events in {
            2: [(0, 1)],
            4: [(1, 1)],
            6: [(2, 1)],
            7: [(0, 2)],
            8: [(3, 1)],
        }.items():

            @pl.when(step == when)
            def _():
                run(events)

    @pl.when(step == steps - 1)
    def _():
        swap(chunks - 2).wait_send()
        swap(chunks - 1).wait_send()
        if not ring:
            whole_copy = pltpu.make_async_copy(grad_scr, exports[0], local_sem.at[13])
            whole_copy.start()

        def leave(block):
            rows = row_block(block)

            @pl.when(block > 1)
            def _():
                finish(layer_copies(block - 2))

            stage_scr[lax.rem(block, 2)] = mixed_scr[rows, :] + dot_nn(
                act_scr[rows, :], down_scr[...]
            )
            go(layer_copies(block))

        each(blocks, leave)
        run([(5, 1)])
        vec_ref[...] = jnp.zeros_like(vec_ref)

        def turn_back(block):
            rows = row_block(block)
            grad_two = dot_nt(gup_scr[rows, :], up_scr[...])
            normed, factor = norm_stats(mixed_scr[rows, :])
            vec_ref[0:1, :] += jnp.sum(grad_two * normed, axis=0, keepdims=True)
            vec_ref[1:2, :] += jnp.sum(grad_two, axis=0, keepdims=True)
            grad_mixed = low_scr[rows, :].astype(F32) + norm_backward(
                grad_two, normed, factor, gain_ref[...][None, :]
            )
            mixed_scr[rows, :] = grad_mixed
            grad_attn = grad_mixed.astype(BF16)
            low_t[:, rows] = jnp.transpose(grad_attn)
            gheads_ref[rows, :] = dot_nt(grad_attn, wo_scr[...]).astype(BF16)

        each(blocks, turn_back)
        gmix_copy.start()
        og_peer[...] = dot_nn(low_t[...], att_ref[:, own_width:]).reshape(og_peer.shape)
        og_own[...] = dot_nn(low_t[...], att_ref[:, 0:own_width]).reshape(og_own.shape)
        if ring:
            at_zero, at_one, at_two, at_deep = exports
            outs = [
                pltpu.make_async_copy(grad_scr.at[4], at_zero, local_sem.at[13]),
                pltpu.make_async_copy(hop1.at[pl.ds(1, 3)], at_one, local_sem.at[14]),
                pltpu.make_async_copy(hop2, at_two, local_sem.at[15]),
                pltpu.make_async_copy(deep1.at[0], at_deep, local_sem.at[16]),
            ]
            outs[0].start()
            flows[0].land(2)
            outs[2].start()
            flows[1].land(1)
            outs[3].start()
            flows[2].land(1)
            flows[3].land(1)
            flows[5].land(1)
            outs[1].start()
            finish(outs)
        else:
            whole_copy.wait()
        gmix_copy.wait()
        finish(layer_copies(blocks - 2))
        finish(layer_copies(blocks - 1))


def middle(
    dp_size, ring, tokens, attended, cotangent, seq_count, gain, shift, wo_own, wo_peer, own, peer
):
    width = tokens.shape[1]
    own_ff = own[0].shape[1]
    own_width = wo_own.shape[0]
    chunks = 6
    ff_block = own_ff // chunks
    grad_shape = place(ring, width, dp_size, 2 * ff_block)
    og_shape = place(ring, width, dp_size, own_width)
    scratch = []
    if ring:
        depth, rows = dp_size // 4, width // dp_size
        hop1 = (2, depth // 2, 2, rows, 2 * ff_block)
        hop2 = (depth, rows, 2 * ff_block)
        deep1 = (depth - 1, 2, 2, rows, 2 * ff_block)
        export_shapes = [grad_shape, (3,) + hop1, hop2, deep1[1:]]
        scratch = [
            pltpu.VMEM((4,) + hop1, F32),
            pltpu.VMEM(hop2, F32),
            pltpu.VMEM(deep1, F32),
        ]
    else:
        export_shapes = [(chunks,) + grad_shape]
    blocks = SEQ_LEN // BLOCK
    n_sems = blocks + chunks + HOPS * chunks
    return pl.pallas_call(
        functools.partial(middle_kernel, dp_size, ring, len(export_shapes)),
        grid=(2 * chunks,),
        in_specs=[
            ANY,
            fixed((SEQ_LEN, 2 * own_width)),
            ANY,
            SMEM,
            fixed((width,)),
            fixed((width,)),
            ANY,
            ANY,
            ANY,
            ANY,
            ANY,
            ANY,
        ],
        out_specs=[
            ANY,
            ANY,
            fixed((SEQ_LEN, 2 * own_width)),
            fixed(og_shape),
            fixed(og_shape),
            fixed((8, width)),
        ]
        + [ANY] * len(export_shapes),
        scratch_shapes=[
            pltpu.VMEM((SEQ_LEN, width), F32),
            pltpu.VMEM((2, BLOCK, width), F32),
            pltpu.VMEM((SEQ_LEN, width), BF16),
            pltpu.VMEM((SEQ_LEN, width), BF16),
            pltpu.VMEM((width, SEQ_LEN), BF16),
            pltpu.VMEM((width, SEQ_LEN), BF16),
            pltpu.VMEM((SEQ_LEN, 2 * own_ff), BF16),
            pltpu.VMEM((SEQ_LEN, 2 * own_ff), BF16),
            pltpu.VMEM((width, 2 * own_ff), BF16),
            pltpu.VMEM((2 * own_ff, width), BF16),
            pltpu.VMEM((2 * own_width, width), BF16),
            pltpu.VMEM((3,) + grad_shape, F32),
            pltpu.VMEM((chunks,) + grad_shape, F32),
            pltpu.SemaphoreType.DMA((17,)),
            pltpu.SemaphoreType.DMA((n_sems,)),
            pltpu.SemaphoreType.DMA((n_sems,)),
        ]
        + scratch,
        out_shape=[
            jax.ShapeDtypeStruct((2 * SEQ_LEN, width), F32),
            jax.ShapeDtypeStruct((SEQ_LEN, width), F32),
            jax.ShapeDtypeStruct((SEQ_LEN, 2 * own_width), BF16),
            jax.ShapeDtypeStruct(og_shape, F32),
            jax.ShapeDtypeStruct(og_shape, F32),
            jax.ShapeDtypeStruct((8, width), F32),
        ]
        + [jax.ShapeDtypeStruct(shape, F32) for shape in export_shapes],
        compiler_params=params(1, 60),
        name="middle",
    )(tokens, attended, cotangent, seq_count, gain, shift, wo_own, wo_peer, *own, *peer)


def back_kernel(dp_size, ring, counts, *refs):
    n_in, n_out, fresh_width = counts
    (
        tokens,
        n1_ref,
        q_ref,
        k_ref,
        v_ref,
        att_ref,
        gheads_ref,
        lse_ref,
        gmix,
        gain_ref,
        w_ref,
        sel_ref,
        og_own,
        og_peer,
        vec2_ref,
    ) = refs[:15]
    exports = refs[15:n_in]
    in_grad, first_grad = refs[n_in : n_in + 2]
    outs = refs[n_in + 2 : n_in + n_out]
    scratch = refs[n_in + n_out :]
    (
        x_scr,
        gmix_scr,
        n1_t,
        dk_acc,
        dv_acc,
        dq_t,
        stack_scr,
        one_acc,
        fv_t,
        post_scr,
        out_scr,
        sums_scr,
        local_sem,
        send_sem,
        recv_sem,
    ) = scratch[:15]
    step = pl.program_id(0)
    steps = pl.num_programs(0)
    length, width = x_scr.shape
    blocks = length // BLOCK
    link = Link(dp_size)
    sems = (send_sem, recv_sem)
    rows_here = pl.ds(link.core * length, length)
    chunks = lse_ref.shape[0] * steps // 2
    grads = scratch[15 : 15 + chunks]
    ring_scr = list(scratch[15 + chunks :])
    side = fv_t.shape[0] // 2
    loads = [
        pltpu.make_async_copy(tokens.at[rows_here], x_scr, local_sem.at[0]),
        pltpu.make_async_copy(gmix, gmix_scr, local_sem.at[1]),
        pltpu.make_async_copy(og_own, out_scr.at[0], local_sem.at[2]),
    ]
    out_swap = remote(og_peer, out_scr.at[1], sems, 0, link.peer)
    swaps = [
        remote(
            post_scr.at[0, ..., pl.ds(0, grads[chunk].shape[-1])],
            grads[chunk],
            sems,
            1 + chunk,
            link.peer,
        )
        for chunk in range(chunks)
    ]
    base = 1 + chunks
    in_copies = [
        remote(one_acc, in_grad.at[rows_here], sems, base, link.peer),
        pltpu.make_async_copy(one_acc, in_grad.at[rows_here], local_sem.at[3]),
    ]
    seq_cols = pl.ds(pl.multiple_of(link.core * length, length), length)
    first_copies = [
        remote(
            fv_t.at[pl.ds((1 - link.core) * side, side)],
            first_grad.at[:, seq_cols],
            sems,
            base + 1,
            link.peer,
        ),
        pltpu.make_async_copy(
            fv_t.at[pl.ds(link.core * side, side)], first_grad.at[:, seq_cols], local_sem.at[4]
        ),
    ]
    base += 2
    flows = {}
    if ring:
        at_zero, at_one, at_two, at_deep = exports
        whole, hop1, hop2, hop3, deep, deep2, deep3 = ring_scr[:7]
        del ring_scr[:7]
        for slot, chunk in enumerate((0, 2, 3, 4, 5)):
            flows[chunk] = Chunk(
                link,
                sems,
                base + slot * HOPS,
                whole,
                None if chunk == 0 else hop1.at[slot - 1],
                hop2.at[slot],
                hop3.at[slot],
            )
        flows[0].sources[2] = at_two
        flows[2].sources[1] = at_one.at[0]
        flows[3].sources[1] = at_one.at[1]
        flows[4].sources[0] = at_zero
        flows[5].sources[1] = at_one.at[2]
        flows[1] = DeepChunk(
            link, sems, base + 5 * HOPS, None, None, deep, at_deep, deep2, deep3
        )
        ring_loads = [
            pltpu.make_async_copy(at_zero, whole, local_sem.at[5]),
            pltpu.make_async_copy(at_one.at[0], hop1.at[0], local_sem.at[6]),
            pltpu.make_async_copy(at_one.at[1], hop1.at[1], local_sem.at[7]),
            pltpu.make_async_copy(at_one.at[2], hop1.at[3], local_sem.at[8]),
            pltpu.make_async_copy(at_two, hop2.at[0], local_sem.at[9]),
            pltpu.make_async_copy(at_deep, deep, local_sem.at[10]),
        ]
        wholes = {"o": out_scr.at[0]}
        wholes.update({"p%d" % n: grads[n] for n in range(chunks)})
        place_in = base + 6 * HOPS
        for name, whole in wholes.items():
            flows[name] = Chunk(link, sems, place_in, whole, *ring_scr[:3])
            del ring_scr[:3]
            place_in += HOPS
        v_send, v_recv = ring_scr[:2]
        flows["v"] = Chunk(link, sems, place_in, v_recv, *ring_scr[2:5])
        vec_swap = remote(v_send, v_recv, sems, place_in + HOPS, link.peer)

    ready = [(1, 2), (2, 2)]

    def run(events):
        for name, number in events:
            if ring:
                if number > 1 and (name, number) not in ready:
                    flows[name].land(number - 1)
                flows[name].start(number)

    @pl.when(step == 0)
    def _():
        partners = [link.peer]
        if ring:
            partners += [link.x_side, link.y_side]
            partners += [link.z_side(hop) for hop in range(1, link.depth)]
        link.greet(partners)
        link.meet(partners)
        if ring:
            flows[3].start(2)
            flows[5].start(2)
            flows[0].start(3)
        out_swap.start()
        go(loads)
        if ring:
            go(ring_loads)
        for block in range(blocks):
            rows = slice(block * BLOCK, (block + 1) * BLOCK)
            n1_t[:, rows] = jnp.transpose(n1_ref[rows, :])
        one_acc[...] = jnp.zeros_like(one_acc)
        fv_t[...] = jnp.zeros_like(fv_t)

    k_t = jnp.transpose(k_ref[...])
    prod_t = jnp.transpose(gheads_ref[...].astype(F32) * att_ref[...].astype(F32))
    lse_pair = lse_ref[0]
    row_pos = lax.broadcasted_iota(jnp.int32, (BLOCK, BLOCK), 0)
    col_pos = lax.broadcasted_iota(jnp.int32, (BLOCK, BLOCK), 1)
    seen = row_pos <= col_pos
    items = [
        (block, head, source)
        for block in range(blocks)
        for head in range(2)
        for source in range(block + 1)
    ]
    raw, soft_low, dq_sums = {}, {}, {}

    def part_of(ref, block, head):
        return split_heads(ref[block * BLOCK : (block + 1) * BLOCK, :])[head]

    def score(index):
        block, head, source = items[index]
        rows = slice(source * BLOCK, (source + 1) * BLOCK)
        raw[index] = (
            dot_nt(k_ref[rows, :], part_of(q_ref, block, head)),
            dot_nt(v_ref[rows, :], part_of(gheads_ref, block, head)),
        )

    def soften(index):
        block, head, source = items[index]
        cols = slice(block * BLOCK, (block + 1) * BLOCK)
        part = slice(head * HEAD_DIM, (head + 1) * HEAD_DIM)
        delta = jnp.sum(prod_t[part, cols], axis=0, keepdims=True)
        scores, dsoft = raw.pop(index)
        soft = jnp.exp(scores - lse_pair[head : head + 1, cols])
        if source == block:
            soft = jnp.where(seen, soft, 0.0)
        soft_low[index] = (soft.astype(BF16), (soft * (dsoft - delta)).astype(BF16))

    def spread(index):
        block, head, source = items[index]
        rows = slice(source * BLOCK, (source + 1) * BLOCK)
        part = slice(head * HEAD_DIM, (head + 1) * HEAD_DIM)
        soft, dscore = soft_low.pop(index)
        dv = dot_nn(soft, part_of(gheads_ref, block, head))
        dk = dot_nn(dscore, part_of(q_ref, block, head))
        if head == 0 and source == block:
            dv_acc[rows, :] = dv
            dk_acc[rows, :] = dk
        else:
            dv_acc[rows, :] += dv
            dk_acc[rows, :] += dk
        dq = dot_nn(k_t[part, rows], dscore)
        dq_sums[block, head] = dq if source == 0 else dq_sums[block, head] + dq
        if source == block:
            dq_t[part, block * BLOCK : (block + 1) * BLOCK] = dq_sums.pop((block, head))

    for index in range(len(items) + 2):
        if index < len(items):
            score(index)
        if 0 <= index - 1 < len(items):
            soften(index - 1)
        if index >= 2:
            spread(index - 2)

    middle_events = {
        0: [(4, 1)],
        1: [(5, 3)],
        2: [(4, 2), (2, 3)],
        3: [("p0", 2)],
        4: [("p1", 1), ("p0", 3)],
        5: [("p1", 2)],
    }
    end_events = {
        0: [(2, 2), (3, 3)],
        1: [("p0", 1), (1, 2)],
        3: [("o", 1), (4, 3)],
        4: [("o", 2), (1, 3)],
        5: [("p2", 1), ("o", 3), ("p1", 3)],
    }
    if ring:
        for when, events in middle_events.items():

            @pl.when(step == when)
            def _():
                run(events)

        @pl.when(step == 0)
        def _():
            finish(ring_loads)

    for block in range(blocks):
        rows = slice(block * BLOCK, (block + 1) * BLOCK)
        stack_scr[rows, 0:PAIR] = (jnp.transpose(dq_t[:, rows]) * HEAD_DIM**-0.5).astype(BF16)
        stack_scr[rows, PAIR : 2 * PAIR] = dk_acc[rows, :].astype(BF16)
        dv = dv_acc[rows, :]
        stack_scr[rows, 2 * PAIR : 3 * PAIR] = dv.astype(BF16)
        one_acc[rows, :] += dot_nt(stack_scr[rows, :], w_ref[...])

    @pl.when(step >= 2 * (fresh_width // PAIR))
    def _():
        for block in range(blocks):
            rows = slice(block * BLOCK, (block + 1) * BLOCK)
            dv = dv_acc[rows, :]
            high = dv.astype(BF16)
            low = (dv - high.astype(F32)).astype(BF16)
            fv_t[:, rows] += dot_nt(sel_ref[...], high) + dot_nt(sel_ref[...], low)

    for chunk in range(1, chunks):

        @pl.when(step == 2 * chunk)
        def _():
            swaps[chunk - 1].wait_send()

    post_scr[lax.rem(step, 2)] = dot_nn(n1_t[...], stack_scr[...]).reshape(post_scr.shape[1:])
    for chunk in range(chunks):
        used = grads[chunk].shape[-1]

        @pl.when(step == 2 * chunk)
        def _():
            swaps[chunk].start()

        @pl.when(step == 2 * chunk + 1)
        def _():
            swaps[chunk].wait_recv()
            grads[chunk][...] += post_scr[1, ..., 0:used]
            if chunk == chunks - 1:
                swaps[chunk].wait_send()

    @pl.when(step == 0)
    def _():
        out_swap.wait()
        finish(loads)
        out_scr[0] += out_scr[1]

    if ring:
        for when, events in end_events.items():

            @pl.when(step == when)
            def _():
                run(events)

    @pl.when(step == steps - 1)
    def _():
        go(first_copies)
        sums_scr[...] = jnp.zeros_like(sums_scr)

        def leave(block):
            rows = row_block(block)
            normed, factor = norm_stats(x_scr[rows, :].astype(F32))
            grad_one = one_acc[rows, :]
            sums_scr[0:1, :] += jnp.sum(grad_one * normed, axis=0, keepdims=True)
            sums_scr[1:2, :] += jnp.sum(grad_one, axis=0, keepdims=True)
            one_acc[rows, :] = gmix_scr[rows, :] + norm_backward(
                grad_one, normed, factor, gain_ref[...][None, :]
            )

        each(blocks, leave)
        go(in_copies)
        vectors = jnp.concatenate(
            [sums_scr[0:2, :], vec2_ref[0:2, :], jnp.zeros((4, width), F32)], axis=0
        )
        if ring:
            up_out, down_out, q_out, k_out, v_out, o_out, vec_out = outs
            rows_dev = width // dp_size
            v_send[...] = jnp.zeros_like(v_send)
            for block in range(dp_size):
                v_send[block // 4, (block // 2) % 2, block % 2, :, 0:rows_dev] = vectors[
                    :, block * rows_dev : (block + 1) * rows_dev
                ]
            vec_swap.start()
            run([("p2", 2)])
            vec_swap.wait()
            v_recv[...] += v_send[...]
            run([("v", 1)])
            ff_block = up_out.shape[-1] // 6

            def put_ffn(index, total):
                cols = slice(index * ff_block, (index + 1) * ff_block)
                down_out[:, cols] = total[:, 0:ff_block]
                up_out[:, cols] = total[:, ff_block:]

            def put_proj(index, total):
                cols = slice(index * PAIR, (index + 1) * PAIR)
                q_out[:, cols] = total[:, 0:PAIR]
                k_out[:, cols] = total[:, PAIR : 2 * PAIR]
                if total.shape[1] > 2 * PAIR:
                    last = min((index + 1) * PAIR, fresh_width)
                    v_out[:, index * PAIR : last] = total[
                        :, 2 * PAIR : 2 * PAIR + last - index * PAIR
                    ]

            for chunk in range(6):
                put_ffn(chunk, flows[chunk].total())
            o_out[...] = flows["o"].total()
            run([("v", 2), ("p2", 3), ("v", 3)])
            put_proj(0, flows["p0"].total())
            put_proj(1, flows["p1"].total())
            put_proj(2, flows["p2"].total())
            vec_out[...] = flows["v"].total()
        else:
            vec_out = outs[-1]
            vec_out[...] = vectors
            stores = [
                pltpu.make_async_copy(grads[chunk], outs[chunk], local_sem.at[5 + chunk])
                for chunk in range(chunks)
            ]
            stores.append(pltpu.make_async_copy(out_scr.at[0], outs[chunks], local_sem.at[8]))
            go(stores)
            finish(stores)
        finish(in_copies)
        finish(first_copies)


def back(
    dp_size,
    ring,
    tokens,
    n1,
    q,
    k,
    v,
    attended,
    grad_heads,
    lse,
    grad_mixed,
    gain,
    weights,
    select,
    og_own,
    og_peer,
    vec2,
    exports,
    fresh_width,
    own_ff,
):
    width = tokens.shape[1]
    own_width = og_own.shape[-1]
    half = own_width // PAIR
    fv_width = select.shape[0]
    side = fv_width // 2
    pair_of = lambda i: lax.rem(i + 1, 2) * half + lax.div(i, 2)
    pair_block = pl.BlockSpec((SEQ_LEN, PAIR), lambda i: (0, pair_of(i)))
    used = [3 * PAIR if n * PAIR < fresh_width else 2 * PAIR for n in range(half)]
    grad_shapes = [place(ring, width, dp_size, columns) for columns in used]
    og_shape = place(ring, width, dp_size, own_width)
    scratch = [
        pltpu.VMEM((SEQ_LEN, width), BF16),
        pltpu.VMEM((SEQ_LEN, width), F32),
        pltpu.VMEM((width, SEQ_LEN), BF16),
        pltpu.VMEM((SEQ_LEN, PAIR), F32),
        pltpu.VMEM((SEQ_LEN, PAIR), F32),
        pltpu.VMEM((PAIR, SEQ_LEN), F32),
        pltpu.VMEM((SEQ_LEN, 3 * PAIR), BF16),
        pltpu.VMEM((SEQ_LEN, width), F32),
        pltpu.VMEM((fv_width, SEQ_LEN), F32),
        pltpu.VMEM((2,) + grad_shapes[0], F32),
        pltpu.VMEM((2,) + og_shape, F32),
        pltpu.VMEM((8, width), F32),
        pltpu.SemaphoreType.DMA((11,)),
    ]
    n_sems = 3 + half + (1 + (8 + half) * HOPS if ring else 0)
    scratch += [pltpu.SemaphoreType.DMA((n_sems,))] * 2
    scratch += [pltpu.VMEM(shape, F32) for shape in grad_shapes]
    if ring:
        depth, rows = dp_size // 4, width // dp_size

        def hops(columns, first, height=rows):
            shapes = [
                (2, depth // 2, 2, height, columns),
                (depth, height, columns),
                (depth - 1, height, columns),
            ]
            return [pltpu.VMEM(shape, F32) for shape in shapes[first:]]

        ff = exports[0].shape[-1]
        scratch += [
            pltpu.VMEM(place(ring, width, dp_size, ff), F32),
            pltpu.VMEM((4, 2, depth // 2, 2, rows, ff), F32),
            pltpu.VMEM((5, depth, rows, ff), F32),
            pltpu.VMEM((5, depth - 1, rows, ff), F32),
            pltpu.VMEM((2, 2, rows, ff), F32),
            pltpu.VMEM((2, 2, rows, ff // 2), F32),
            pltpu.VMEM((2, rows, ff // 2), F32),
        ]
        scratch += hops(own_width, 0)
        for columns in used:
            scratch += hops(columns, 0)
        vec_whole = pltpu.VMEM((depth, 2, 2, 8, PAIR), F32)
        scratch += [vec_whole, vec_whole] + hops(PAIR, 0, 8)
        totals = [
            (rows, own_ff),
            (rows, own_ff),
            (rows, own_width),
            (rows, own_width),
            (rows, fresh_width),
            (rows, own_width),
            (8, PAIR),
        ]
        total_specs = [fixed(shape) for shape in totals]
        export_args = list(exports)
        export_specs = [ANY] * len(export_args)
    else:
        totals = grad_shapes + [og_shape, (8, width)]
        total_specs = [ANY] * (half + 1) + [fixed((8, width))]
        export_args, export_specs = [], []
    in_specs = [
        ANY,
        fixed((SEQ_LEN, width)),
        pair_block,
        pair_block,
        pair_block,
        pair_block,
        pair_block,
        pl.BlockSpec((1, 8, SEQ_LEN), lambda i: (pair_of(i), 0, 0)),
        ANY,
        fixed((width,)),
        pl.BlockSpec((width, 3 * PAIR), lambda i: (0, pair_of(i))),
        pl.BlockSpec((fv_width, PAIR), lambda i: (0, pair_of(i))),
        ANY,
        ANY,
        fixed((8, width)),
    ] + export_specs
    return pl.pallas_call(
        functools.partial(
            back_kernel, dp_size, ring, (len(in_specs), 2 + len(totals), fresh_width)
        ),
        grid=(2 * half,),
        in_specs=in_specs,
        out_specs=[ANY, ANY] + total_specs,
        scratch_shapes=scratch,
        out_shape=[
            jax.ShapeDtypeStruct((2 * SEQ_LEN, width), F32),
            jax.ShapeDtypeStruct((side, 2 * SEQ_LEN), F32),
        ]
        + [jax.ShapeDtypeStruct(shape, F32) for shape in totals],
        compiler_params=params(2, 60),
        name="back",
    )(
        tokens,
        n1,
        q,
        k,
        v,
        attended,
        grad_heads,
        lse,
        grad_mixed,
        gain,
        weights,
        select,
        og_own,
        og_peer,
        vec2,
        *export_args,
    )


def collect_kernel(large, *refs):
    half = len(refs) // 2
    pairs = list(zip(refs[:half], refs[half:]))
    for source, target in pairs[:large]:
        target[...] = source[...]

    @pl.when(pl.program_id(0) == 0)
    def _():
        for source, target in pairs[large:]:
            target[...] = source[...]


def collect(tall, columns, small):
    blocks = 8
    rows = tall[0]
    specs = [pl.BlockSpec((rows.shape[0] // blocks, rows.shape[1]), lambda i: (i, 0))] * 2 + [
        pl.BlockSpec((columns.shape[0], columns.shape[1] // blocks), lambda i: (0, i)),
    ] + [fixed(array.shape) for array in small]
    arrays = tall + [columns] + small
    return pl.pallas_call(
        functools.partial(collect_kernel, 3),
        grid=(blocks,),
        in_specs=specs,
        out_specs=specs,
        out_shape=[jax.ShapeDtypeStruct(array.shape, array.dtype) for array in arrays],
        compiler_params=pltpu.CompilerParams(vmem_limit_bytes=60 * 1024 * 1024),
        name="collect",
    )(*arrays)


def on_device(
    dp_size,
    tokens,
    first_values,
    seq_count,
    skip_map,
    norm1_gain,
    norm1_shift,
    query_weight,
    key_weight,
    value_weight,
    out_weight,
    norm2_gain,
    norm2_shift,
    up_weight,
    down_weight,
    cotangent,
):
    width = tokens.shape[1]
    own_width = query_weight.shape[1]
    fresh_width = value_weight.shape[1]
    own_ff = up_weight.shape[1]
    ring = ring_of(dp_size, width)
    gain1, shift1, gain2, shift2 = norm1_gain, norm1_shift, norm2_gain, norm2_shift
    n1, q, k, v, attended, lse, weights, select, out_peer, up_peer, down_peer = front(
        dp_size,
        tokens,
        first_values,
        skip_map,
        gain1,
        shift1,
        query_weight,
        key_weight,
        value_weight.T,
        out_weight,
        up_weight,
        down_weight,
    )
    layer_out, grad_mixed, grad_heads, og_own, og_peer, vec2, *exports = middle(
        dp_size,
        ring,
        tokens,
        attended,
        cotangent,
        seq_count,
        gain2,
        shift2,
        out_weight,
        out_peer,
        (up_weight, down_weight),
        (up_peer, down_peer),
    )
    input_grad, first_grad, *totals = back(
        dp_size,
        ring,
        tokens,
        n1,
        q,
        k,
        v,
        attended,
        grad_heads,
        lse,
        grad_mixed,
        gain1,
        weights,
        select,
        og_own,
        og_peer,
        vec2,
        exports,
        fresh_width,
        own_ff,
    )
    if ring:
        *totals, vectors = totals
        layer_out, input_grad, first_grad, *totals = collect([layer_out, input_grad], first_grad, totals)
        up_total, down_t, query_total, key_total, value_total, out_t = totals
        rows = width // dp_size
        down_total, out_total = down_t.T, out_t.T
        gain1_total, shift1_total, gain2_total, shift2_total = (vectors[n, :rows] for n in range(4))
    else:
        *proj, out_grad, vectors = totals
        chunks = exports[0].shape[0]
        ff_block = own_ff // chunks
        vectors = vectors + lax.ppermute(vectors, "tensor", [(0, 1), (1, 0)])
        columns = list(proj) + [out_grad] + [exports[0][n] for n in range(chunks)]
        packed = jnp.concatenate(columns + [jnp.pad(vectors.T, ((0, 0), (0, 120)))], axis=1)
        summed = lax.psum_scatter(packed, "dp", scatter_dimension=0, tiled=True)
        heads, start = [[], [], []], 0
        for part in proj:
            for n in range(part.shape[1] // PAIR):
                heads[n].append(summed[:, start : start + PAIR])
                start += PAIR
        query_total, key_total, value_total = (jnp.concatenate(part, axis=1) for part in heads)
        value_total = value_total[:, :fresh_width]
        out_total = summed[:, start : start + own_width].T
        start += own_width
        pairs = summed[:, start : start + 2 * own_ff].reshape(-1, chunks, 2, ff_block)
        down_total = pairs[:, :, 0].reshape(-1, own_ff).T
        up_total = pairs[:, :, 1].reshape(-1, own_ff)
        start += 2 * own_ff
        gain1_total, shift1_total, gain2_total, shift2_total = (
            summed[:, start + n] for n in range(4)
        )
    return (
        layer_out,
        input_grad,
        first_grad.T,
        gain1_total,
        shift1_total,
        query_total,
        key_total,
        value_total,
        out_total,
        gain2_total,
        shift2_total,
        up_total,
        down_total,
    )


def solution(mesh):
    placed = (
        P("dp", None),
        P("dp", None),
        P("dp"),
        P("tensor"),
        P(),
        P(),
        P(None, "tensor"),
        P(None, "tensor"),
        P(None, "tensor"),
        P("tensor", None),
        P(),
        P(),
        P(None, "tensor"),
        P("tensor", None),
        P("dp", None),
    )
    return jax.shard_map(
        functools.partial(on_device, mesh.shape["dp"]),
        mesh=mesh,
        in_specs=placed,
        out_specs=(
            P("dp", None),
            P("dp", None),
            P("dp", "tensor"),
            P("dp"),
            P("dp"),
            P("dp", "tensor"),
            P("dp", "tensor"),
            P("dp", "tensor"),
            P("tensor", "dp"),
            P("dp"),
            P("dp"),
            P("dp", "tensor"),
            P("tensor", "dp"),
        ),
        check_vma=False,
    )
```

```python
import functools

import jax
import jax.numpy as jnp
from jax import lax
from jax.experimental import pallas as pl
from jax.experimental.pallas import tpu as pltpu
from jax.sharding import PartitionSpec as P

HEAD_DIM = 64
SEQ_LEN = 1024
BLOCK = 256
PAIR = 2 * HEAD_DIM
EPS = 1e-05
FILL = -1e30

F32 = jnp.float32
BF16 = jnp.bfloat16


def dot_nn(left, right):
    return lax.dot_general(left, right, (((1,), (0,)), ((), ())), preferred_element_type=F32)


def dot_nt(left, right):
    return lax.dot_general(left, right, (((1,), (1,)), ((), ())), preferred_element_type=F32)


def norm_stats(values_in):
    average = jnp.mean(values_in, axis=-1, keepdims=True)
    centered = values_in - average
    variance = jnp.mean(centered * centered, axis=-1, keepdims=True)
    factor = lax.rsqrt(variance + EPS)
    return centered * factor, factor


def norm_backward(grad, normed, factor, gain):
    scaled = grad * gain
    mean_plain = jnp.mean(scaled, axis=-1, keepdims=True)
    mean_cross = jnp.mean(scaled * normed, axis=-1, keepdims=True)
    return factor * (scaled - mean_plain - normed * mean_cross)


def each(count, body):
    lax.fori_loop(0, count, lambda index, carry: (body(index), carry)[1], 0)


def row_block(index):
    return pl.ds(pl.multiple_of(index * BLOCK, BLOCK), BLOCK)


def recast(source, target, rows=64):
    def one(index):
        part = pl.ds(pl.multiple_of(index * rows, rows), rows)
        target[part, :] = source[part, :].astype(target.dtype)

    each(source.shape[0] // rows, one)


def head_masks(rows):
    lanes = lax.broadcasted_iota(jnp.int32, (rows, PAIR), 1)
    return lanes < HEAD_DIM


def split_heads(pair_rows):
    first = head_masks(pair_rows.shape[0])
    zero = jnp.zeros_like(pair_rows)
    return jnp.where(first, pair_rows, zero), jnp.where(first, zero, pair_rows)


MESH = pl.DeviceIdType.MESH


def params(collective_id, vmem_mib):
    return pltpu.CompilerParams(
        vmem_limit_bytes=vmem_mib * 1024 * 1024,
        collective_id=collective_id,
        has_side_effects=True,
    )


def fixed(shape):
    zeros = (0,) * len(shape)
    return pl.BlockSpec(shape, lambda i: zeros, pipeline_mode=pl.Buffered(1))


ANY = pl.BlockSpec(memory_space=pl.ANY)
SMEM = pl.BlockSpec(memory_space=pltpu.SMEM)


def ring_of(dp_size, width):
    return dp_size == 4 * 4 and width % (8 * dp_size) == 0


def place(ring, width, dp_size, columns):
    if not ring:
        return (width, columns)
    return (2, 2, 2, 2, width // dp_size, columns)


class Link:
    def __init__(self, dp_size):
        self.dp = lax.axis_index("dp")
        self.core = lax.axis_index("tensor")
        self.x = lax.rem(self.dp, 2)
        self.y = lax.rem(lax.div(self.dp, 2), 2)
        self.z_low = lax.rem(lax.div(self.dp, 4), 2)
        self.z_high = lax.rem(lax.div(self.dp, 8), 2)
        self.peer = {"tensor": 1 - self.core}
        self.x_side = {"dp": self.dp + 1 - 2 * self.x}
        self.y_side = {"dp": self.dp + 2 - 4 * self.y}
        self.z_side = {"dp": self.dp + 4 - 8 * self.z_low}
        self.z_far = {"dp": self.dp + 8 - 16 * self.z_high}

    def greet(self, partners):
        barrier = pltpu.get_barrier_semaphore()
        for partner in partners:
            pl.semaphore_signal(barrier, inc=1, device_id=partner, device_id_type=MESH)

    def meet(self, partners):
        pl.semaphore_wait(pltpu.get_barrier_semaphore(), len(partners))


def remote(source, target, sems, index, device):
    send, recv = sems
    return pltpu.make_async_remote_copy(
        src_ref=source,
        dst_ref=target,
        send_sem=send.at[index],
        recv_sem=recv.at[index],
        device_id=device,
        device_id_type=MESH,
    )


def go(copies):
    for copy in copies:
        copy.start()


def finish(copies):
    for copy in copies:
        copy.wait()


HOPS = 6


class Chunk:
    def __init__(self, link, sems, base, whole, hop1, hop2=None, hop3=None, hop4=None):
        self.link, self.sems, self.base = link, sems, base
        self.held = [whole, hop1, hop2, hop3, hop4]
        self.sources = list(self.held)

    def hop(self, number):
        link, sems, base = self.link, self.sems, self.base
        source, landing = self.sources[number - 1], self.held[number]
        if number == 1:
            return [
                remote(source.at[0, :, :, 1 - link.x], landing.at[0], sems, base, link.x_side),
                remote(source.at[1, :, 1 - link.y], landing.at[1], sems, base + 1, link.y_side),
            ]
        if number == 2:
            return [
                remote(source.at[0, :, 1 - link.y], landing.at[0], sems, base + 2, link.y_side),
                remote(source.at[1, :, 1 - link.x], landing.at[1], sems, base + 3, link.x_side),
            ]
        if number == 3:
            return [
                remote(source.at[:, 1 - link.z_low], landing, sems, base + 4, link.z_side)
            ]
        return [remote(source.at[1 - link.z_high], landing, sems, base + 5, link.z_far)]

    def start(self, number):
        go(self.hop(number))

    def land(self, number):
        link = self.link
        finish(self.hop(number))
        own, landing = self.held[number - 1], self.held[number]

        def one(row):
            if number == 1:
                for other in range(2):
                    landing[0, row, other] += own[0, row, other, link.x]
                    landing[1, row, other] += own[1, row, link.y, other]
            elif number == 2:
                landing[0, row] += own[0, row, link.y]
                landing[1, row] += own[1, row, link.x]
            else:
                landing[row] += own[row, link.z_low]

        each(2, one)

    def total(self):
        finish(self.hop(4))
        return self.held[3][self.link.z_high] + self.held[4][...]


class DeepChunk:
    def __init__(self, link, sems, base, whole, hop1, hop2=None, hop3=None, hop4=None):
        self.link, self.sems, self.base = link, sems, base
        self.held = [whole, hop1, hop2, hop3, hop4]
        self.sources = list(self.held)

    def hop(self, number):
        link, sems, base = self.link, self.sems, self.base
        source, landing = self.sources[number - 1], self.held[number]
        if number == 1:
            return [remote(source.at[:, 1 - link.z_low], landing, sems, base, link.z_side)]
        if number == 2:
            return [remote(source.at[1 - link.z_high], landing, sems, base + 1, link.z_far)]
        if number == 3:
            side = landing.shape[-1]
            left, right = pl.ds(0, side), pl.ds(side, side)
            return [
                remote(
                    source.at[:, 1 - link.x, :, left], landing.at[0], sems, base + 2, link.x_side
                ),
                remote(
                    source.at[1 - link.y, :, :, right], landing.at[1], sems, base + 3, link.y_side
                ),
            ]
        return [
            remote(source.at[0, 1 - link.y], landing.at[0], sems, base + 4, link.y_side),
            remote(source.at[1, 1 - link.x], landing.at[1], sems, base + 5, link.x_side),
        ]

    def start(self, number):
        go(self.hop(number))

    def land(self, number):
        link = self.link
        finish(self.hop(number))
        own, landing = self.held[number - 1], self.held[number]

        def one(row):
            if number == 1:
                for other in range(4):
                    y, x = other // 2, other % 2
                    landing[row, y, x] += own[row, link.z_low, y, x]
            elif number == 2:
                for other in range(2):
                    landing[row, other] += own[row, other]
            else:
                side = landing.shape[-1]
                landing[0, row] += own[row, link.x, :, 0:side]
                landing[1, row] += own[link.y, row, :, side:]

        each(2, one)

    def total(self):
        finish(self.hop(4))
        own, landed = self.held[3], self.held[4]
        return jnp.concatenate(
            [own[0, self.link.y] + landed[0], own[1, self.link.x] + landed[1]], axis=-1
        )


def hop_shapes(rows, columns):
    return [
        (2, 2, 2, rows, columns),
        (2, 2, rows, columns),
        (2, rows, columns),
        (rows, columns),
    ]


def front_kernel(
    dp_size,
    tokens,
    first_values,
    skip_map,
    gain_ref,
    shift_ref,
    wq_ref,
    wk_ref,
    wv_ref,
    out_w,
    up_w,
    down_w,
    n1_ref,
    q_ref,
    k_ref,
    v_ref,
    att_ref,
    lse_ref,
    w_ref,
    sel_ref,
    out_peer,
    up_peer,
    down_peer,
    x_scr,
    fv_scr,
    proj_own,
    proj_send,
    proj_recv,
    sel_send,
    sel_recv,
    out_low,
    up_low,
    down_low,
    out_send,
    up_send,
    down_send,
    out_recv,
    up_recv,
    down_recv,
    lse_scr,
    local_sem,
    send_sem,
    recv_sem,
):
    step = pl.program_id(0)
    length, width = x_scr.shape
    blocks = length // BLOCK
    half = pl.num_programs(0) // 2
    own_width = wq_ref.shape[1]
    fresh_width = wv_ref.shape[0]
    fv_width = fv_scr.shape[1]
    link = Link(dp_size)
    sems = (send_sem, recv_sem)
    rows_here = pl.ds(link.core * length, length)
    local = [
        pltpu.make_async_copy(tokens.at[rows_here], x_scr, local_sem.at[0]),
        pltpu.make_async_copy(first_values.at[rows_here], fv_scr, local_sem.at[1]),
        pltpu.make_async_copy(up_w, up_low, local_sem.at[2]),
        pltpu.make_async_copy(down_w, down_low, local_sem.at[3]),
        pltpu.make_async_copy(out_w, out_low, local_sem.at[4]),
    ]
    early = [
        remote(proj_send, proj_recv, sems, 0, link.peer),
        remote(sel_send, sel_recv, sems, 1, link.peer),
    ]
    late = [
        remote(up_send, up_recv, sems, 2, link.peer),
        remote(down_send, down_recv, sems, 3, link.peer),
        remote(out_send, out_recv, sems, 4, link.peer),
    ]
    landed = [
        (late[0], up_recv, up_low, pltpu.make_async_copy(up_low, up_peer, local_sem.at[2])),
        (late[1], down_recv, down_low, pltpu.make_async_copy(down_low, down_peer, local_sem.at[3])),
        (late[2], out_recv, out_low, pltpu.make_async_copy(out_low, out_peer, local_sem.at[4])),
    ]

    @pl.when(step == 0)
    def _():
        link.greet([link.peer])
        go(local)
        proj_own[2, :, 0:fresh_width] = jnp.transpose(wv_ref[...])
        proj_own[2, :, fresh_width:] = jnp.zeros((width, own_width - fresh_width), BF16)
        for part, source in enumerate((wq_ref, wk_ref)):
            recast(source, proj_own.at[part])
        for part in range(3):
            recast(proj_own.at[part], proj_send.at[part])
        row = lax.broadcasted_iota(jnp.int32, (fv_width, own_width), 0)
        col = lax.broadcasted_iota(jnp.int32, (fv_width, own_width), 1)
        slots = (own_width - fresh_width) // HEAD_DIM
        target = jnp.full((fv_width, own_width), -1, jnp.int32)
        for slot in range(slots):
            start = fresh_width + slot * HEAD_DIM
            inside = jnp.logical_and(col >= start, col < start + HEAD_DIM)
            target = jnp.where(inside, skip_map[slot] * HEAD_DIM + col - start, target)
        chosen = jnp.where(row == target, 1.0, 0.0).astype(F32)
        sel_send[...] = chosen
        sel_ref[:, 0:own_width] = chosen.astype(BF16)
        link.meet([link.peer])
        go(early)
        lse_scr[...] = jnp.zeros_like(lse_scr)
        local[0].wait()
        local[1].wait()

        def one(block, carry):
            rows = pl.ds(block * BLOCK, BLOCK)
            normed, _ = norm_stats(x_scr[rows, :].astype(F32))
            n1_ref[rows, :] = (normed * gain_ref[...][None, :] + shift_ref[...][None, :]).astype(BF16)
            return carry

        lax.fori_loop(0, blocks, one, 0)

    @pl.when(step == half)
    def _():
        finish(early)
        sel_ref[:, own_width:] = sel_recv[...].astype(BF16)

    @pl.when(step < half)
    def _():
        cols = pl.ds(pl.multiple_of(step * PAIR, PAIR), PAIR)
        for part in range(3):
            w_ref[:, part * PAIR : (part + 1) * PAIR] = proj_own[part, :, cols]

    @pl.when(step >= half)
    def _():
        cols = pl.ds(pl.multiple_of((step - half) * PAIR, PAIR), PAIR)
        for part in range(3):
            w_ref[:, part * PAIR : (part + 1) * PAIR] = proj_recv[part, :, cols].astype(BF16)

    sel_cols = pl.ds(pl.multiple_of(step * PAIR, PAIR), PAIR)
    for block in range(blocks):
        rows = slice(block * BLOCK, (block + 1) * BLOCK)
        fused = dot_nn(n1_ref[rows, :], w_ref[...])
        picked = dot_nn(fv_scr[rows, :], sel_ref[:, sel_cols])
        q_ref[rows, :] = (fused[:, 0:PAIR].astype(BF16).astype(F32) * HEAD_DIM**-0.5).astype(BF16)
        k_ref[rows, :] = fused[:, PAIR : 2 * PAIR].astype(BF16)
        v_ref[rows, :] = (fused[:, 2 * PAIR :] + picked).astype(BF16)

    lane = lax.broadcasted_iota(jnp.int32, (BLOCK, PAIR), 1)
    row_pos = lax.broadcasted_iota(jnp.int32, (BLOCK, BLOCK), 0)
    col_pos = lax.broadcasted_iota(jnp.int32, (BLOCK, BLOCK), 1)
    seen = col_pos <= row_pos
    items = [(block, head) for block in range(blocks) for head in range(2)]
    scores, weights, partial = {}, {}, {}

    def score(index):
        block, head = items[index]
        lo, hi = block * BLOCK, (block + 1) * BLOCK
        query = split_heads(q_ref[lo:hi, :])[head]
        diag = dot_nt(query, k_ref[lo:hi, :])
        scores[index] = (diag, dot_nt(query, k_ref[0:lo, :]) if block else None)

    def soften(index):
        block, head = items[index]
        lo, hi = block * BLOCK, (block + 1) * BLOCK
        diag, past = scores.pop(index)
        diag = jnp.where(seen, diag, FILL)
        peak = jnp.max(diag, axis=-1, keepdims=True)
        if block:
            peak = jnp.maximum(peak, jnp.max(past, axis=-1, keepdims=True))
        diag = jnp.exp(diag - peak)
        mass = jnp.sum(diag, axis=-1, keepdims=True)
        if block:
            past = jnp.exp(past - peak)
            mass = mass + jnp.sum(past, axis=-1, keepdims=True)
        inverse = 1.0 / mass
        weights[index] = (
            (diag * inverse).astype(BF16),
            (past * inverse).astype(BF16) if block else None,
        )
        lse_scr[lo:hi, :] = jnp.where(
            lane == 2 * step + head, peak + jnp.log(mass), lse_scr[lo:hi, :]
        )

    def attend(index):
        block, head = items[index]
        lo, hi = block * BLOCK, (block + 1) * BLOCK
        diag, past = weights.pop(index)
        total = dot_nn(diag, split_heads(v_ref[lo:hi, :])[head])
        if block:
            total = total + dot_nn(past, split_heads(v_ref[0:lo, :])[head])
        if head == 0:
            partial[block] = total
        else:
            att_ref[lo:hi, :] = (partial.pop(block) + total).astype(BF16)

    for index in range(len(items) + 2):
        if index < len(items):
            score(index)
        if 0 <= index - 1 < len(items):
            soften(index - 1)
        if index >= 2:
            attend(index - 2)

    @pl.when(step == 0)
    def _():
        for copy in local[2:]:
            copy.wait()
        recast(up_low, up_send)
        recast(down_low, down_send)
        recast(out_low, out_send)
        go(late)

    @pl.when(step == pl.num_programs(0) - 2)
    def _():
        for copy, recv, low, store in landed:
            copy.wait()
            recast(recv, low)
            store.start()

    @pl.when(step == pl.num_programs(0) - 1)
    def _():
        for block in range(blocks):
            lo, hi = block * BLOCK, (block + 1) * BLOCK
            turned = jnp.transpose(lse_scr[lo:hi, :])
            for pair in range(lse_ref.shape[0]):
                lse_ref[pair, 0:2, lo:hi] = turned[2 * pair : 2 * pair + 2, :]
        for _, _, _, store in landed:
            store.wait()


def front(dp_size, tokens, first_values, skip_map, gain, shift, wq, wk, wv, out_w, up_w, down_w):
    width = tokens.shape[1]
    own_width = wq.shape[1]
    half = own_width // PAIR
    fv_width = first_values.shape[1]
    pair_block = pl.BlockSpec((SEQ_LEN, PAIR), lambda i: (0, i))
    pair_out = jax.ShapeDtypeStruct((SEQ_LEN, 2 * own_width), BF16)
    return pl.pallas_call(
        functools.partial(front_kernel, dp_size),
        grid=(2 * half,),
        in_specs=[
            ANY,
            ANY,
            SMEM,
            fixed((width,)),
            fixed((width,)),
            fixed(wq.shape),
            fixed(wk.shape),
            fixed(wv.shape),
            ANY,
            ANY,
            ANY,
        ],
        out_specs=[
            fixed((SEQ_LEN, width)),
            pair_block,
            pair_block,
            pair_block,
            pair_block,
            fixed((2 * half, 8, SEQ_LEN)),
            pl.BlockSpec((width, 3 * PAIR), lambda i: (0, i)),
            fixed((fv_width, 2 * own_width)),
            ANY,
            ANY,
            ANY,
        ],
        scratch_shapes=[
            pltpu.VMEM((SEQ_LEN, width), BF16),
            pltpu.VMEM((SEQ_LEN, fv_width), BF16),
            pltpu.VMEM((3, width, own_width), BF16),
            pltpu.VMEM((3, width, own_width), F32),
            pltpu.VMEM((3, width, own_width), F32),
            pltpu.VMEM((fv_width, own_width), F32),
            pltpu.VMEM((fv_width, own_width), F32),
            pltpu.VMEM(out_w.shape, BF16),
            pltpu.VMEM(up_w.shape, BF16),
            pltpu.VMEM(down_w.shape, BF16),
            pltpu.VMEM(out_w.shape, F32),
            pltpu.VMEM(up_w.shape, F32),
            pltpu.VMEM(down_w.shape, F32),
            pltpu.VMEM(out_w.shape, F32),
            pltpu.VMEM(up_w.shape, F32),
            pltpu.VMEM(down_w.shape, F32),
            pltpu.VMEM((SEQ_LEN, PAIR), F32),
            pltpu.SemaphoreType.DMA((5,)),
            pltpu.SemaphoreType.DMA((5,)),
            pltpu.SemaphoreType.DMA((5,)),
        ],
        out_shape=[
            jax.ShapeDtypeStruct((SEQ_LEN, width), BF16),
            pair_out,
            pair_out,
            pair_out,
            pair_out,
            jax.ShapeDtypeStruct((2 * half, 8, SEQ_LEN), F32),
            jax.ShapeDtypeStruct((width, 6 * own_width), BF16),
            jax.ShapeDtypeStruct((fv_width, 2 * own_width), BF16),
            jax.ShapeDtypeStruct(out_w.shape, BF16),
            jax.ShapeDtypeStruct(up_w.shape, BF16),
            jax.ShapeDtypeStruct(down_w.shape, BF16),
        ],
        compiler_params=params(0, 60),
        name="front",
    )(tokens, first_values, skip_map, gain, shift, wq, wk, wv, out_w, up_w, down_w)


def gelu_pair(upper):
    scale = (2.0 / jnp.pi) ** 0.5
    square = upper * upper
    inner = upper * (scale + (scale * 0.044715) * square)
    tanh = jnp.tanh(inner)
    cdf = 0.5 + 0.5 * tanh
    slope = cdf + 0.5 * upper * (1.0 - tanh * tanh) * (scale + (3.0 * scale * 0.044715) * square)
    return upper * cdf, slope


def middle_kernel(dp_size, ring, n_exports, *refs):
    (
        tokens,
        attended,
        cotangent,
        seq_count,
        gain_ref,
        shift_ref,
        wo_own,
        wo_peer,
        up_own,
        down_own,
        up_peer,
        down_peer,
        layer_out,
        gmix_out,
        gheads_ref,
        og_own,
        og_peer,
        vec_ref,
    ) = refs[:18]
    exports = refs[18 : 18 + n_exports]
    (
        att_ref,
        mixed_scr,
        stage_scr,
        two_scr,
        low_scr,
        two_t,
        low_t,
        act_scr,
        gup_scr,
        up_scr,
        down_scr,
        wo_scr,
        post_scr,
        grad_scr,
        local_sem,
        send_sem,
        recv_sem,
    ) = refs[18 + n_exports : 35 + n_exports]
    ring_scr = refs[35 + n_exports :]
    step = pl.program_id(0)
    steps = pl.num_programs(0)
    length, width = mixed_scr.shape
    blocks = length // BLOCK
    own_width = wo_own.shape[0]
    own_ff = up_own.shape[1]
    chunks = grad_scr.shape[0]
    ff_block = own_ff // chunks
    link = Link(dp_size)
    sems = (send_sem, recv_sem)
    rows_here = pl.ds(link.core * length, length)
    x_ref = gheads_ref
    loads = [
        pltpu.make_async_copy(tokens.at[rows_here], x_ref, local_sem.at[0]),
        pltpu.make_async_copy(wo_own, wo_scr.at[pl.ds(0, own_width)], local_sem.at[1]),
        pltpu.make_async_copy(wo_peer, wo_scr.at[pl.ds(own_width, own_width)], local_sem.at[2]),
        pltpu.make_async_copy(cotangent.at[rows_here], low_scr, local_sem.at[3]),
        pltpu.make_async_copy(attended, att_ref, local_sem.at[16]),
    ]
    weight_loads = [
        pltpu.make_async_copy(up_own, up_scr.at[:, pl.ds(0, own_ff)], local_sem.at[4]),
        pltpu.make_async_copy(up_peer, up_scr.at[:, pl.ds(own_ff, own_ff)], local_sem.at[5]),
        pltpu.make_async_copy(down_own, down_scr.at[pl.ds(0, own_ff)], local_sem.at[6]),
        pltpu.make_async_copy(down_peer, down_scr.at[pl.ds(own_ff, own_ff)], local_sem.at[7]),
    ]
    gmix_copy = pltpu.make_async_copy(mixed_scr, gmix_out, local_sem.at[8])

    def layer_copies(block):
        rows = pl.ds(link.core * length + block * BLOCK, BLOCK)
        return [
            pltpu.make_async_copy(
                stage_scr.at[lax.rem(block, 2)], layer_out.at[rows], local_sem.at[9 + block]
            ),
            remote(stage_scr.at[lax.rem(block, 2)], layer_out.at[rows], sems, block, link.peer),
        ]


    def swap(chunk):
        return remote(
            post_scr.at[lax.rem(chunk, 2)], grad_scr.at[chunk], sems, blocks + chunk, link.peer
        )

    flows = {}
    if ring:
        base = blocks + chunks
        hop1, hop2, deep1 = ring_scr
        for slot, chunk in enumerate((0, 2, 4, 5)):
            flows[chunk] = Chunk(
                link,
                sems,
                base + HOPS * chunk,
                grad_scr.at[chunk],
                hop1.at[slot],
                None if chunk else hop2,
            )
        for slot, chunk in enumerate((1, 3)):
            flows[chunk] = DeepChunk(
                link, sems, base + HOPS * chunk, grad_scr.at[chunk], deep1.at[slot]
            )

    partners = [link.peer]
    if ring:
        partners += [link.x_side, link.y_side, link.z_side]

    def run(events):
        for chunk, number in events:
            if ring:
                if number > 1:
                    flows[chunk].land(number - 1)
                flows[chunk].start(number)

    @pl.when(step == 0)
    def _():
        link.greet(partners)
        go(loads)
        go(weight_loads)
        finish(loads)
        live = jnp.where(link.core < seq_count[0], 1.0, 0.0).astype(F32)

        def enter(block):
            rows = row_block(block)
            mixed = x_ref[rows, :].astype(F32) + dot_nn(att_ref[rows, :], wo_scr[...])
            mixed_scr[rows, :] = mixed
            normed, _ = norm_stats(mixed)
            two_low = (normed * gain_ref[...][None, :] + shift_ref[...][None, :]).astype(BF16)
            two_scr[rows, :] = two_low
            two_t[:, rows] = jnp.transpose(two_low)
            low = (low_scr[rows, :].astype(F32) * live).astype(BF16)
            low_scr[rows, :] = low
            low_t[:, rows] = jnp.transpose(low)

        each(blocks, enter)
        finish(weight_loads)
        link.meet(partners)

    last = lax.div(step, steps - 1)
    mine = (1 - lax.rem(step, 2)) * lax.div(step + steps - 1, steps) + last
    mine_index = lax.div(step - 1 + lax.div(steps - step, steps), 2)
    post_index = lax.div(step + 1, 2)
    turn = mine * mine_index + (1 - mine) * (chunks + post_index)
    slot = 2 * mine + (1 - mine) * lax.rem(post_index, 2)
    cols = pl.ds(pl.multiple_of(turn * ff_block, ff_block), ff_block)
    for block in range(blocks):
        rows = slice(block * BLOCK, (block + 1) * BLOCK)
        upper = dot_nn(two_scr[rows, :], up_scr[:, cols])
        active, slope = gelu_pair(upper)
        act_scr[rows, cols] = active.astype(BF16)
        grad_active = dot_nt(low_scr[rows, :], down_scr[cols, :])
        gup_scr[rows, cols] = (grad_active * slope).astype(BF16)

    block_shape = grad_scr.shape[1:-1] + (ff_block,)
    @pl.when(jnp.logical_and(mine == 0, post_index > 1))
    def _():
        swap(post_index - 2).wait_send()

    post_scr[slot, ..., 0:ff_block] = dot_nn(low_t[...], act_scr[:, cols]).reshape(block_shape)
    post_scr[slot, ..., ff_block:] = dot_nn(two_t[...], gup_scr[:, cols]).reshape(block_shape)

    @pl.when(mine == 0)
    def _():
        swap(post_index).start()

    @pl.when(mine == 1)
    def _():
        swap(mine_index).wait_recv()
        grad_scr[mine_index] += post_scr[2]

    if ring:
        for when, events in {
            2: [(0, 1)],
            4: [(1, 1)],
            6: [(2, 1)],
            8: [(3, 1), (0, 2)],
            10: [(4, 1)],
            11: [(5, 1)],
        }.items():

            @pl.when(step == when)
            def _():
                run(events)

    @pl.when(step == steps - 1)
    def _():
        swap(chunks - 2).wait_send()
        swap(chunks - 1).wait_send()
        if not ring:
            whole_copy = pltpu.make_async_copy(grad_scr, exports[0], local_sem.at[13])
            whole_copy.start()

        def leave(block):
            rows = row_block(block)

            @pl.when(block > 1)
            def _():
                finish(layer_copies(block - 2))

            stage_scr[lax.rem(block, 2)] = mixed_scr[rows, :] + dot_nn(
                act_scr[rows, :], down_scr[...]
            )
            go(layer_copies(block))

        each(blocks, leave)
        vec_ref[...] = jnp.zeros_like(vec_ref)

        def turn_back(block):
            rows = row_block(block)
            grad_two = dot_nt(gup_scr[rows, :], up_scr[...])
            normed, factor = norm_stats(mixed_scr[rows, :])
            vec_ref[0:1, :] += jnp.sum(grad_two * normed, axis=0, keepdims=True)
            vec_ref[1:2, :] += jnp.sum(grad_two, axis=0, keepdims=True)
            grad_mixed = low_scr[rows, :].astype(F32) + norm_backward(
                grad_two, normed, factor, gain_ref[...][None, :]
            )
            mixed_scr[rows, :] = grad_mixed
            grad_attn = grad_mixed.astype(BF16)
            low_t[:, rows] = jnp.transpose(grad_attn)
            gheads_ref[rows, :] = dot_nt(grad_attn, wo_scr[...]).astype(BF16)

        each(blocks, turn_back)
        gmix_copy.start()
        og_peer[...] = dot_nn(low_t[...], att_ref[:, own_width:]).reshape(og_peer.shape)
        og_own[...] = dot_nn(low_t[...], att_ref[:, 0:own_width]).reshape(og_own.shape)
        if ring:
            at_one, at_two, at_deep = exports
            outs = [
                pltpu.make_async_copy(hop1.at[pl.ds(1, 3)], at_one, local_sem.at[13]),
                pltpu.make_async_copy(hop2, at_two, local_sem.at[14]),
                pltpu.make_async_copy(deep1, at_deep, local_sem.at[15]),
            ]
            flows[0].land(2)
            outs[1].start()
            flows[1].land(1)
            flows[3].land(1)
            outs[2].start()
            flows[2].land(1)
            flows[5].land(1)
            flows[4].land(1)
            outs[0].start()
            finish(outs)
        else:
            whole_copy.wait()
        gmix_copy.wait()
        finish(layer_copies(blocks - 2))
        finish(layer_copies(blocks - 1))


def middle(
    dp_size, ring, tokens, attended, cotangent, seq_count, gain, shift, wo_own, wo_peer, own, peer
):
    width = tokens.shape[1]
    own_ff = own[0].shape[1]
    own_width = wo_own.shape[0]
    chunks = 6
    ff_block = own_ff // chunks
    grad_shape = place(ring, width, dp_size, 2 * ff_block)
    og_shape = place(ring, width, dp_size, own_width)
    scratch = []
    if ring:
        hop1, hop2, _, _ = hop_shapes(width // dp_size, 2 * ff_block)
        export_shapes = [(3,) + hop1, hop2, (2,) + hop1]
        scratch = [
            pltpu.VMEM((4,) + hop1, F32),
            pltpu.VMEM(hop2, F32),
            pltpu.VMEM((2,) + hop1, F32),
        ]
    else:
        export_shapes = [(chunks,) + grad_shape]
    blocks = SEQ_LEN // BLOCK
    n_sems = blocks + chunks + HOPS * chunks
    return pl.pallas_call(
        functools.partial(middle_kernel, dp_size, ring, len(export_shapes)),
        grid=(2 * chunks,),
        in_specs=[
            ANY,
            ANY,
            ANY,
            SMEM,
            fixed((width,)),
            fixed((width,)),
            ANY,
            ANY,
            ANY,
            ANY,
            ANY,
            ANY,
        ],
        out_specs=[
            ANY,
            ANY,
            fixed((SEQ_LEN, 2 * own_width)),
            fixed(og_shape),
            fixed(og_shape),
            fixed((8, width)),
        ]
        + [ANY] * len(export_shapes),
        scratch_shapes=[
            pltpu.VMEM((SEQ_LEN, 2 * own_width), BF16),
            pltpu.VMEM((SEQ_LEN, width), F32),
            pltpu.VMEM((2, BLOCK, width), F32),
            pltpu.VMEM((SEQ_LEN, width), BF16),
            pltpu.VMEM((SEQ_LEN, width), BF16),
            pltpu.VMEM((width, SEQ_LEN), BF16),
            pltpu.VMEM((width, SEQ_LEN), BF16),
            pltpu.VMEM((SEQ_LEN, 2 * own_ff), BF16),
            pltpu.VMEM((SEQ_LEN, 2 * own_ff), BF16),
            pltpu.VMEM((width, 2 * own_ff), BF16),
            pltpu.VMEM((2 * own_ff, width), BF16),
            pltpu.VMEM((2 * own_width, width), BF16),
            pltpu.VMEM((3,) + grad_shape, F32),
            pltpu.VMEM((chunks,) + grad_shape, F32),
            pltpu.SemaphoreType.DMA((17,)),
            pltpu.SemaphoreType.DMA((n_sems,)),
            pltpu.SemaphoreType.DMA((n_sems,)),
        ]
        + scratch,
        out_shape=[
            jax.ShapeDtypeStruct((2 * SEQ_LEN, width), F32),
            jax.ShapeDtypeStruct((SEQ_LEN, width), F32),
            jax.ShapeDtypeStruct((SEQ_LEN, 2 * own_width), BF16),
            jax.ShapeDtypeStruct(og_shape, F32),
            jax.ShapeDtypeStruct(og_shape, F32),
            jax.ShapeDtypeStruct((8, width), F32),
        ]
        + [jax.ShapeDtypeStruct(shape, F32) for shape in export_shapes],
        compiler_params=params(1, 60),
        name="middle",
    )(tokens, attended, cotangent, seq_count, gain, shift, wo_own, wo_peer, *own, *peer)


def back_kernel(dp_size, ring, counts, *refs):
    n_in, n_out, fresh_width = counts
    (
        tokens,
        n1_ref,
        q_ref,
        k_ref,
        v_ref,
        att_ref,
        gheads_ref,
        lse_ref,
        gmix,
        gain_ref,
        w_ref,
        sel_ref,
        og_own,
        og_peer,
        vec2_ref,
    ) = refs[:15]
    exports = refs[15:n_in]
    in_grad, first_grad = refs[n_in : n_in + 2]
    outs = refs[n_in + 2 : n_in + n_out]
    scratch = refs[n_in + n_out :]
    (
        x_scr,
        gmix_scr,
        n1_t,
        dk_acc,
        dv_acc,
        dq_t,
        stack_scr,
        one_acc,
        fv_t,
        post_scr,
        out_scr,
        sums_scr,
        local_sem,
        send_sem,
        recv_sem,
    ) = scratch[:15]
    step = pl.program_id(0)
    steps = pl.num_programs(0)
    length, width = x_scr.shape
    blocks = length // BLOCK
    link = Link(dp_size)
    sems = (send_sem, recv_sem)
    rows_here = pl.ds(link.core * length, length)
    chunks = lse_ref.shape[0] * steps // 2
    grads = scratch[15 : 15 + chunks]
    ring_scr = list(scratch[15 + chunks :])
    side = fv_t.shape[0] // 2
    loads = [
        pltpu.make_async_copy(tokens.at[rows_here], x_scr, local_sem.at[0]),
        pltpu.make_async_copy(gmix, gmix_scr, local_sem.at[1]),
        pltpu.make_async_copy(og_own, out_scr.at[0], local_sem.at[2]),
    ]
    out_swap = remote(og_peer, out_scr.at[1], sems, 0, link.peer)
    swaps = [
        remote(
            post_scr.at[0, ..., pl.ds(0, grads[chunk].shape[-1])],
            grads[chunk],
            sems,
            1 + chunk,
            link.peer,
        )
        for chunk in range(chunks)
    ]
    base = 1 + chunks
    in_copies = [
        remote(one_acc, in_grad.at[rows_here], sems, base, link.peer),
        pltpu.make_async_copy(one_acc, in_grad.at[rows_here], local_sem.at[3]),
    ]
    seq_cols = pl.ds(pl.multiple_of(link.core * length, length), length)
    first_copies = [
        remote(
            fv_t.at[pl.ds((1 - link.core) * side, side)],
            first_grad.at[:, seq_cols],
            sems,
            base + 1,
            link.peer,
        ),
        pltpu.make_async_copy(
            fv_t.at[pl.ds(link.core * side, side)], first_grad.at[:, seq_cols], local_sem.at[4]
        ),
    ]
    base += 2
    flows = {}
    if ring:
        at_one, at_two, at_deep = exports
        hop1, hop2, hop3, hop4, deep1, deep2, deep3, deep4 = ring_scr[:8]
        del ring_scr[:8]
        for slot, chunk in enumerate((0, 2, 4, 5)):
            flows[chunk] = Chunk(
                link,
                sems,
                base + slot * HOPS,
                None,
                None if chunk == 0 else hop1.at[slot - 1],
                hop2.at[slot],
                hop3.at[slot],
                hop4.at[slot],
            )
            if chunk:
                flows[chunk].sources[1] = at_one.at[slot - 1]
        flows[0].sources[2] = at_two
        for slot, chunk in enumerate((1, 3)):
            flows[chunk] = DeepChunk(
                link,
                sems,
                base + (4 + slot) * HOPS,
                None,
                deep1.at[slot],
                deep2.at[slot],
                deep3.at[slot],
                deep4.at[slot],
            )
            flows[chunk].sources[1] = at_deep.at[slot]
        ring_loads = [
            pltpu.make_async_copy(at_one, hop1, local_sem.at[5]),
            pltpu.make_async_copy(at_two, hop2.at[0], local_sem.at[6]),
            pltpu.make_async_copy(at_deep.at[0, link.z_high], deep1.at[0], local_sem.at[7]),
            pltpu.make_async_copy(at_deep.at[1, link.z_high], deep1.at[1], local_sem.at[8]),
        ]
        wholes = {"o": out_scr.at[0]}
        wholes.update({"p%d" % n: grads[n] for n in range(chunks)})
        place_in = base + 6 * HOPS
        for name, whole in wholes.items():
            flows[name] = Chunk(link, sems, place_in, whole, *ring_scr[:4])
            del ring_scr[:4]
            place_in += HOPS
        v_send, v_recv = ring_scr[:2]
        flows["v"] = Chunk(link, sems, place_in, v_recv, *ring_scr[2:6])
        vec_swap = remote(v_send, v_recv, sems, place_in + HOPS, link.peer)

    ready = [(1, 2), (2, 2), (3, 2), (4, 2), (5, 2), (0, 3)]

    def run(events):
        for name, number in events:
            if ring:
                if number > 1 and (name, number) not in ready:
                    flows[name].land(number - 1)
                flows[name].start(number)

    @pl.when(step == 0)
    def _():
        partners = [link.peer]
        if ring:
            partners += [link.x_side, link.y_side, link.z_side, link.z_far]
        link.greet(partners)
        link.meet(partners)
        if ring:
            flows[2].start(2)
            flows[3].start(2)
            flows[5].start(2)
            flows[0].start(3)
        out_swap.start()
        go(loads)
        if ring:
            go(ring_loads)
        for block in range(blocks):
            rows = slice(block * BLOCK, (block + 1) * BLOCK)
            n1_t[:, rows] = jnp.transpose(n1_ref[rows, :])
        one_acc[...] = jnp.zeros_like(one_acc)
        fv_t[...] = jnp.zeros_like(fv_t)

    k_t = jnp.transpose(k_ref[...])
    prod_t = jnp.transpose(gheads_ref[...].astype(F32) * att_ref[...].astype(F32))
    lse_pair = lse_ref[0]
    row_pos = lax.broadcasted_iota(jnp.int32, (BLOCK, BLOCK), 0)
    col_pos = lax.broadcasted_iota(jnp.int32, (BLOCK, BLOCK), 1)
    seen = row_pos <= col_pos
    items = [
        (block, head, source)
        for block in range(blocks)
        for head in range(2)
        for source in range(block + 1)
    ]
    raw, soft_low, dq_sums = {}, {}, {}

    def part_of(ref, block, head):
        return split_heads(ref[block * BLOCK : (block + 1) * BLOCK, :])[head]

    def score(index):
        block, head, source = items[index]
        rows = slice(source * BLOCK, (source + 1) * BLOCK)
        raw[index] = (
            dot_nt(k_ref[rows, :], part_of(q_ref, block, head)),
            dot_nt(v_ref[rows, :], part_of(gheads_ref, block, head)),
        )

    def soften(index):
        block, head, source = items[index]
        cols = slice(block * BLOCK, (block + 1) * BLOCK)
        part = slice(head * HEAD_DIM, (head + 1) * HEAD_DIM)
        delta = jnp.sum(prod_t[part, cols], axis=0, keepdims=True)
        scores, dsoft = raw.pop(index)
        soft = jnp.exp(scores - lse_pair[head : head + 1, cols])
        if source == block:
            soft = jnp.where(seen, soft, 0.0)
        soft_low[index] = (soft.astype(BF16), (soft * (dsoft - delta)).astype(BF16))

    def spread(index):
        block, head, source = items[index]
        rows = slice(source * BLOCK, (source + 1) * BLOCK)
        part = slice(head * HEAD_DIM, (head + 1) * HEAD_DIM)
        soft, dscore = soft_low.pop(index)
        dv = dot_nn(soft, part_of(gheads_ref, block, head))
        dk = dot_nn(dscore, part_of(q_ref, block, head))
        if head == 0 and source == block:
            dv_acc[rows, :] = dv
            dk_acc[rows, :] = dk
        else:
            dv_acc[rows, :] += dv
            dk_acc[rows, :] += dk
        dq = dot_nn(k_t[part, rows], dscore)
        dq_sums[block, head] = dq if source == 0 else dq_sums[block, head] + dq
        if source == block:
            dq_t[part, block * BLOCK : (block + 1) * BLOCK] = dq_sums.pop((block, head))

    for index in range(len(items) + 2):
        if index < len(items):
            score(index)
        if 0 <= index - 1 < len(items):
            soften(index - 1)
        if index >= 2:
            spread(index - 2)

    middle_events = {
        2: [(5, 3)],
        3: [(3, 3), (4, 3)],
        4: [("o", 3), (5, 4)],
        5: [("p1", 2), (4, 4)],
    }
    end_events = {
        0: [("o", 1)],
        1: [("p0", 1), (1, 2), (4, 2), (2, 3)],
        2: [("o", 2)],
        3: [("p1", 1)],
        4: [("p0", 2)],
        5: [("p2", 1), ("p0", 3), (0, 4), (2, 4), ("o", 4)],
    }
    if ring:
        for when, events in middle_events.items():

            @pl.when(step == when)
            def _():
                run(events)

        @pl.when(step == 0)
        def _():
            finish(ring_loads)

    for block in range(blocks):
        rows = slice(block * BLOCK, (block + 1) * BLOCK)
        stack_scr[rows, 0:PAIR] = (jnp.transpose(dq_t[:, rows]) * HEAD_DIM**-0.5).astype(BF16)
        stack_scr[rows, PAIR : 2 * PAIR] = dk_acc[rows, :].astype(BF16)
        dv = dv_acc[rows, :]
        stack_scr[rows, 2 * PAIR : 3 * PAIR] = dv.astype(BF16)
        one_acc[rows, :] += dot_nt(stack_scr[rows, :], w_ref[...])

    @pl.when(step >= 2 * (fresh_width // PAIR))
    def _():
        for block in range(blocks):
            rows = slice(block * BLOCK, (block + 1) * BLOCK)
            dv = dv_acc[rows, :]
            high = dv.astype(BF16)
            low = (dv - high.astype(F32)).astype(BF16)
            fv_t[:, rows] += dot_nt(sel_ref[...], high) + dot_nt(sel_ref[...], low)

    for chunk in range(1, chunks):

        @pl.when(step == 2 * chunk)
        def _():
            swaps[chunk - 1].wait_send()

    post_scr[lax.rem(step, 2)] = dot_nn(n1_t[...], stack_scr[...]).reshape(post_scr.shape[1:])
    for chunk in range(chunks):
        used = grads[chunk].shape[-1]

        @pl.when(step == 2 * chunk)
        def _():
            swaps[chunk].start()

        @pl.when(step == 2 * chunk + 1)
        def _():
            swaps[chunk].wait_recv()
            grads[chunk][...] += post_scr[1, ..., 0:used]
            if chunk == chunks - 1:
                swaps[chunk].wait_send()

    @pl.when(step == 0)
    def _():
        out_swap.wait()
        finish(loads)
        out_scr[0] += out_scr[1]

    if ring:
        for when, events in end_events.items():

            @pl.when(step == when)
            def _():
                run(events)

    @pl.when(step == steps - 1)
    def _():
        go(first_copies)
        sums_scr[...] = jnp.zeros_like(sums_scr)

        def leave(block):
            rows = row_block(block)
            normed, factor = norm_stats(x_scr[rows, :].astype(F32))
            grad_one = one_acc[rows, :]
            sums_scr[0:1, :] += jnp.sum(grad_one * normed, axis=0, keepdims=True)
            sums_scr[1:2, :] += jnp.sum(grad_one, axis=0, keepdims=True)
            one_acc[rows, :] = gmix_scr[rows, :] + norm_backward(
                grad_one, normed, factor, gain_ref[...][None, :]
            )

        each(blocks, leave)
        go(in_copies)
        vectors = jnp.concatenate(
            [sums_scr[0:2, :], vec2_ref[0:2, :], jnp.zeros((4, width), F32)], axis=0
        )
        if ring:
            up_out, down_out, q_out, k_out, v_out, o_out, vec_out = outs
            rows_dev = width // dp_size
            v_send[...] = jnp.zeros_like(v_send)
            for block in range(dp_size):
                v_send[block // 8, block // 4 % 2, block // 2 % 2, block % 2, :, 0:rows_dev] = vectors[
                    :, block * rows_dev : (block + 1) * rows_dev
                ]
            vec_swap.start()
            run([("p2", 2)])
            vec_swap.wait()
            v_recv[...] += v_send[...]
            run(
                [("v", 1), (1, 3), ("p1", 3), ("p2", 3), ("v", 2), (1, 4), (3, 4), ("p0", 4), ("p1", 4), ("v", 3), ("p2", 4), ("v", 4)]
            )
            ff_block = up_out.shape[-1] // 6

            def put_ffn(index, total):
                cols = slice(index * ff_block, (index + 1) * ff_block)
                down_out[:, cols] = total[:, 0:ff_block]
                up_out[:, cols] = total[:, ff_block:]

            def put_proj(index, total):
                cols = slice(index * PAIR, (index + 1) * PAIR)
                q_out[:, cols] = total[:, 0:PAIR]
                k_out[:, cols] = total[:, PAIR : 2 * PAIR]
                if total.shape[1] > 2 * PAIR:
                    last = min((index + 1) * PAIR, fresh_width)
                    v_out[:, index * PAIR : last] = total[
                        :, 2 * PAIR : 2 * PAIR + last - index * PAIR
                    ]

            for chunk in range(6):
                put_ffn(chunk, flows[chunk].total())
            o_out[...] = flows["o"].total()
            put_proj(0, flows["p0"].total())
            put_proj(1, flows["p1"].total())
            put_proj(2, flows["p2"].total())
            vec_out[...] = flows["v"].total()
        else:
            vec_out = outs[-1]
            vec_out[...] = vectors
            stores = [
                pltpu.make_async_copy(grads[chunk], outs[chunk], local_sem.at[5 + chunk])
                for chunk in range(chunks)
            ]
            stores.append(pltpu.make_async_copy(out_scr.at[0], outs[chunks], local_sem.at[8]))
            go(stores)
            finish(stores)
        finish(in_copies)
        finish(first_copies)


def back(
    dp_size,
    ring,
    tokens,
    n1,
    q,
    k,
    v,
    attended,
    grad_heads,
    lse,
    grad_mixed,
    gain,
    weights,
    select,
    og_own,
    og_peer,
    vec2,
    exports,
    fresh_width,
    own_ff,
):
    width = tokens.shape[1]
    own_width = og_own.shape[-1]
    half = own_width // PAIR
    fv_width = select.shape[0]
    side = fv_width // 2
    pair_of = lambda i: lax.rem(i + 1, 2) * half + lax.div(i, 2)
    pair_block = pl.BlockSpec((SEQ_LEN, PAIR), lambda i: (0, pair_of(i)))
    used = [3 * PAIR if n * PAIR < fresh_width else 2 * PAIR for n in range(half)]
    grad_shapes = [place(ring, width, dp_size, columns) for columns in used]
    og_shape = place(ring, width, dp_size, own_width)
    scratch = [
        pltpu.VMEM((SEQ_LEN, width), BF16),
        pltpu.VMEM((SEQ_LEN, width), F32),
        pltpu.VMEM((width, SEQ_LEN), BF16),
        pltpu.VMEM((SEQ_LEN, PAIR), F32),
        pltpu.VMEM((SEQ_LEN, PAIR), F32),
        pltpu.VMEM((PAIR, SEQ_LEN), F32),
        pltpu.VMEM((SEQ_LEN, 3 * PAIR), BF16),
        pltpu.VMEM((SEQ_LEN, width), F32),
        pltpu.VMEM((fv_width, SEQ_LEN), F32),
        pltpu.VMEM((2,) + grad_shapes[0], F32),
        pltpu.VMEM((2,) + og_shape, F32),
        pltpu.VMEM((8, width), F32),
        pltpu.SemaphoreType.DMA((11,)),
    ]
    n_sems = 3 + half + (1 + (8 + half) * HOPS if ring else 0)
    scratch += [pltpu.SemaphoreType.DMA((n_sems,))] * 2
    scratch += [pltpu.VMEM(shape, F32) for shape in grad_shapes]
    if ring:
        rows = width // dp_size

        def hops(columns, height=rows, count=None):
            lead = () if count is None else (count,)
            return [lead + shape for shape in hop_shapes(height, columns)]

        ff = exports[0].shape[-1]
        shapes = [(3,) + hops(ff)[0]] + hops(ff, count=4)[1:]
        shapes += [(2, 2, 2, rows, ff)] * 2
        shapes += [(2, 2, 2, rows, ff // 2), (2, 2, rows, ff // 2)]
        shapes += hops(own_width)
        for columns in used:
            shapes += hops(columns)
        vec_whole = place(ring, width, dp_size, PAIR)[:4] + (8, PAIR)
        shapes += [vec_whole, vec_whole] + hops(PAIR, 8)
        scratch += [pltpu.VMEM(shape, F32) for shape in shapes]
        totals = [
            (rows, own_ff),
            (rows, own_ff),
            (rows, own_width),
            (rows, own_width),
            (rows, fresh_width),
            (rows, own_width),
            (8, PAIR),
        ]
        total_specs = [fixed(shape) for shape in totals]
        export_args = list(exports)
        export_specs = [ANY] * len(export_args)
    else:
        totals = grad_shapes + [og_shape, (8, width)]
        total_specs = [ANY] * (half + 1) + [fixed((8, width))]
        export_args, export_specs = [], []
    in_specs = [
        ANY,
        fixed((SEQ_LEN, width)),
        pair_block,
        pair_block,
        pair_block,
        pair_block,
        pair_block,
        pl.BlockSpec((1, 8, SEQ_LEN), lambda i: (pair_of(i), 0, 0)),
        ANY,
        fixed((width,)),
        pl.BlockSpec((width, 3 * PAIR), lambda i: (0, pair_of(i))),
        pl.BlockSpec((fv_width, PAIR), lambda i: (0, pair_of(i))),
        ANY,
        ANY,
        fixed((8, width)),
    ] + export_specs
    return pl.pallas_call(
        functools.partial(
            back_kernel, dp_size, ring, (len(in_specs), 2 + len(totals), fresh_width)
        ),
        grid=(2 * half,),
        in_specs=in_specs,
        out_specs=[ANY, ANY] + total_specs,
        scratch_shapes=scratch,
        out_shape=[
            jax.ShapeDtypeStruct((2 * SEQ_LEN, width), F32),
            jax.ShapeDtypeStruct((side, 2 * SEQ_LEN), F32),
        ]
        + [jax.ShapeDtypeStruct(shape, F32) for shape in totals],
        compiler_params=params(2, 60),
        name="back",
    )(
        tokens,
        n1,
        q,
        k,
        v,
        attended,
        grad_heads,
        lse,
        grad_mixed,
        gain,
        weights,
        select,
        og_own,
        og_peer,
        vec2,
        *export_args,
    )


def collect_kernel(large, *refs):
    half = len(refs) // 2
    pairs = list(zip(refs[:half], refs[half:]))
    for source, target in pairs[:large]:
        target[...] = source[...]

    @pl.when(pl.program_id(0) == 0)
    def _():
        for source, target in pairs[large:]:
            target[...] = source[...]


def collect(tall, columns, small):
    blocks = 8
    rows = tall[0]
    specs = [pl.BlockSpec((rows.shape[0] // blocks, rows.shape[1]), lambda i: (i, 0))] * 2 + [
        pl.BlockSpec((columns.shape[0], columns.shape[1] // blocks), lambda i: (0, i)),
    ] + [fixed(array.shape) for array in small]
    arrays = tall + [columns] + small
    return pl.pallas_call(
        functools.partial(collect_kernel, 3),
        grid=(blocks,),
        in_specs=specs,
        out_specs=specs,
        out_shape=[jax.ShapeDtypeStruct(array.shape, array.dtype) for array in arrays],
        compiler_params=pltpu.CompilerParams(vmem_limit_bytes=60 * 1024 * 1024),
        name="collect",
    )(*arrays)


def on_device(
    dp_size,
    tokens,
    first_values,
    seq_count,
    skip_map,
    norm1_gain,
    norm1_shift,
    query_weight,
    key_weight,
    value_weight,
    out_weight,
    norm2_gain,
    norm2_shift,
    up_weight,
    down_weight,
    cotangent,
):
    width = tokens.shape[1]
    own_width = query_weight.shape[1]
    fresh_width = value_weight.shape[1]
    own_ff = up_weight.shape[1]
    ring = ring_of(dp_size, width)
    gain1, shift1, gain2, shift2 = norm1_gain, norm1_shift, norm2_gain, norm2_shift
    n1, q, k, v, attended, lse, weights, select, out_peer, up_peer, down_peer = front(
        dp_size,
        tokens,
        first_values,
        skip_map,
        gain1,
        shift1,
        query_weight,
        key_weight,
        value_weight.T,
        out_weight,
        up_weight,
        down_weight,
    )
    layer_out, grad_mixed, grad_heads, og_own, og_peer, vec2, *exports = middle(
        dp_size,
        ring,
        tokens,
        attended,
        cotangent,
        seq_count,
        gain2,
        shift2,
        out_weight,
        out_peer,
        (up_weight, down_weight),
        (up_peer, down_peer),
    )
    input_grad, first_grad, *totals = back(
        dp_size,
        ring,
        tokens,
        n1,
        q,
        k,
        v,
        attended,
        grad_heads,
        lse,
        grad_mixed,
        gain1,
        weights,
        select,
        og_own,
        og_peer,
        vec2,
        exports,
        fresh_width,
        own_ff,
    )
    if ring:
        *totals, vectors = totals
        layer_out, input_grad, first_grad, *totals = collect([layer_out, input_grad], first_grad, totals)
        up_total, down_t, query_total, key_total, value_total, out_t = totals
        rows = width // dp_size
        down_total, out_total = down_t.T, out_t.T
        gain1_total, shift1_total, gain2_total, shift2_total = (vectors[n, :rows] for n in range(4))
    else:
        *proj, out_grad, vectors = totals
        chunks = exports[0].shape[0]
        ff_block = own_ff // chunks
        vectors = vectors + lax.ppermute(vectors, "tensor", [(0, 1), (1, 0)])
        columns = list(proj) + [out_grad] + [exports[0][n] for n in range(chunks)]
        packed = jnp.concatenate(columns + [jnp.pad(vectors.T, ((0, 0), (0, 120)))], axis=1)
        summed = lax.psum_scatter(packed, "dp", scatter_dimension=0, tiled=True)
        heads, start = [[], [], []], 0
        for part in proj:
            for n in range(part.shape[1] // PAIR):
                heads[n].append(summed[:, start : start + PAIR])
                start += PAIR
        query_total, key_total, value_total = (jnp.concatenate(part, axis=1) for part in heads)
        value_total = value_total[:, :fresh_width]
        out_total = summed[:, start : start + own_width].T
        start += own_width
        pairs = summed[:, start : start + 2 * own_ff].reshape(-1, chunks, 2, ff_block)
        down_total = pairs[:, :, 0].reshape(-1, own_ff).T
        up_total = pairs[:, :, 1].reshape(-1, own_ff)
        start += 2 * own_ff
        gain1_total, shift1_total, gain2_total, shift2_total = (
            summed[:, start + n] for n in range(4)
        )
    return (
        layer_out,
        input_grad,
        first_grad.T,
        gain1_total,
        shift1_total,
        query_total,
        key_total,
        value_total,
        out_total,
        gain2_total,
        shift2_total,
        up_total,
        down_total,
    )


def solution(mesh):
    placed = (
        P("dp", None),
        P("dp", None),
        P("dp"),
        P("tensor"),
        P(),
        P(),
        P(None, "tensor"),
        P(None, "tensor"),
        P(None, "tensor"),
        P("tensor", None),
        P(),
        P(),
        P(None, "tensor"),
        P("tensor", None),
        P("dp", None),
    )
    return jax.shard_map(
        functools.partial(on_device, mesh.shape["dp"]),
        mesh=mesh,
        in_specs=placed,
        out_specs=(
            P("dp", None),
            P("dp", None),
            P("dp", "tensor"),
            P("dp"),
            P("dp"),
            P("dp", "tensor"),
            P("dp", "tensor"),
            P("dp", "tensor"),
            P("tensor", "dp"),
            P("dp"),
            P("dp"),
            P("dp", "tensor"),
            P("tensor", "dp"),
        ),
        check_vma=False,
    )
```

```python
import functools

import jax
import jax.numpy as jnp
from jax import lax
from jax.experimental import pallas as pl
from jax.experimental.pallas import tpu as pltpu
from jax.sharding import PartitionSpec as P

HEAD_DIM = 64
SEQ_LEN = 1024
BLOCK = 256
PAIR = 2 * HEAD_DIM
EPS = 1e-05
FILL = -1e30

F32 = jnp.float32
BF16 = jnp.bfloat16


def dot_nn(left, right):
    return lax.dot_general(left, right, (((1,), (0,)), ((), ())), preferred_element_type=F32)


def dot_nt(left, right):
    return lax.dot_general(left, right, (((1,), (1,)), ((), ())), preferred_element_type=F32)


def norm_stats(values_in):
    average = jnp.mean(values_in, axis=-1, keepdims=True)
    centered = values_in - average
    variance = jnp.mean(centered * centered, axis=-1, keepdims=True)
    factor = lax.rsqrt(variance + EPS)
    return centered * factor, factor


def norm_backward(grad, normed, factor, gain):
    scaled = grad * gain
    mean_plain = jnp.mean(scaled, axis=-1, keepdims=True)
    mean_cross = jnp.mean(scaled * normed, axis=-1, keepdims=True)
    return factor * (scaled - mean_plain - normed * mean_cross)


def each(count, body):
    lax.fori_loop(0, count, lambda index, carry: (body(index), carry)[1], 0)


def row_block(index):
    return pl.ds(pl.multiple_of(index * BLOCK, BLOCK), BLOCK)


def recast(source, target, rows=64):
    def one(index):
        part = pl.ds(pl.multiple_of(index * rows, rows), rows)
        target[part, :] = source[part, :].astype(target.dtype)

    each(source.shape[0] // rows, one)


def head_masks(rows):
    lanes = lax.broadcasted_iota(jnp.int32, (rows, PAIR), 1)
    return lanes < HEAD_DIM


def split_heads(pair_rows):
    first = head_masks(pair_rows.shape[0])
    zero = jnp.zeros_like(pair_rows)
    return jnp.where(first, pair_rows, zero), jnp.where(first, zero, pair_rows)


MESH = pl.DeviceIdType.MESH


def params(collective_id, vmem_mib):
    return pltpu.CompilerParams(
        vmem_limit_bytes=vmem_mib * 1024 * 1024,
        collective_id=collective_id,
        has_side_effects=True,
    )


def fixed(shape):
    zeros = (0,) * len(shape)
    return pl.BlockSpec(shape, lambda i: zeros, pipeline_mode=pl.Buffered(1))


ANY = pl.BlockSpec(memory_space=pl.ANY)
SMEM = pl.BlockSpec(memory_space=pltpu.SMEM)


def ring_of(dp_size, width):
    return dp_size == 4 * 4 and width % (8 * dp_size) == 0


def place(ring, width, dp_size, columns):
    if not ring:
        return (width, columns)
    return (2, 2, 2, 2, width // dp_size, columns)


class Link:
    def __init__(self, dp_size):
        self.dp = lax.axis_index("dp")
        self.core = lax.axis_index("tensor")
        self.x = lax.rem(self.dp, 2)
        self.y = lax.rem(lax.div(self.dp, 2), 2)
        self.z_low = lax.rem(lax.div(self.dp, 4), 2)
        self.z_high = lax.rem(lax.div(self.dp, 8), 2)
        self.peer = {"tensor": 1 - self.core}
        self.x_side = {"dp": self.dp + 1 - 2 * self.x}
        self.y_side = {"dp": self.dp + 2 - 4 * self.y}
        self.z_side = {"dp": self.dp + 4 - 8 * self.z_low}
        self.z_far = {"dp": self.dp + 8 - 16 * self.z_high}

    def greet(self, partners):
        barrier = pltpu.get_barrier_semaphore()
        for partner in partners:
            pl.semaphore_signal(barrier, inc=1, device_id=partner, device_id_type=MESH)

    def meet(self, partners):
        pl.semaphore_wait(pltpu.get_barrier_semaphore(), len(partners))


def remote(source, target, sems, index, device):
    send, recv = sems
    return pltpu.make_async_remote_copy(
        src_ref=source,
        dst_ref=target,
        send_sem=send.at[index],
        recv_sem=recv.at[index],
        device_id=device,
        device_id_type=MESH,
    )


def go(copies):
    for copy in copies:
        copy.start()


def finish(copies):
    for copy in copies:
        copy.wait()


HOPS = 6


class Chunk:
    def __init__(self, link, sems, base, whole, hop1, hop2=None, hop3=None, hop4=None):
        self.link, self.sems, self.base = link, sems, base
        self.held = [whole, hop1, hop2, hop3, hop4]
        self.sources = list(self.held)

    def hop(self, number):
        link, sems, base = self.link, self.sems, self.base
        source, landing = self.sources[number - 1], self.held[number]
        if number == 1:
            return [
                remote(source.at[0, :, :, 1 - link.x], landing.at[0], sems, base, link.x_side),
                remote(source.at[1, :, 1 - link.y], landing.at[1], sems, base + 1, link.y_side),
            ]
        if number == 2:
            return [
                remote(source.at[0, :, 1 - link.y], landing.at[0], sems, base + 2, link.y_side),
                remote(source.at[1, :, 1 - link.x], landing.at[1], sems, base + 3, link.x_side),
            ]
        if number == 3:
            return [
                remote(source.at[:, 1 - link.z_low], landing, sems, base + 4, link.z_side)
            ]
        return [remote(source.at[1 - link.z_high], landing, sems, base + 5, link.z_far)]

    def start(self, number):
        go(self.hop(number))

    def land(self, number):
        link = self.link
        finish(self.hop(number))
        own, landing = self.held[number - 1], self.held[number]

        def one(row):
            if number == 1:
                for other in range(2):
                    landing[0, row, other] += own[0, row, other, link.x]
                    landing[1, row, other] += own[1, row, link.y, other]
            elif number == 2:
                landing[0, row] += own[0, row, link.y]
                landing[1, row] += own[1, row, link.x]
            else:
                landing[row] += own[row, link.z_low]

        each(2, one)

    def total(self):
        finish(self.hop(4))
        return self.held[3][self.link.z_high] + self.held[4][...]


class DeepChunk:
    def __init__(self, link, sems, base, whole, hop1, hop2=None, hop3=None, hop4=None):
        self.link, self.sems, self.base = link, sems, base
        self.held = [whole, hop1, hop2, hop3, hop4]
        self.sources = list(self.held)

    def hop(self, number):
        link, sems, base = self.link, self.sems, self.base
        source, landing = self.sources[number - 1], self.held[number]
        if number == 1:
            return [remote(source.at[:, 1 - link.z_low], landing, sems, base, link.z_side)]
        if number == 2:
            return [remote(source.at[1 - link.z_high], landing, sems, base + 1, link.z_far)]
        if number == 3:
            side = landing.shape[-1]
            left, right = pl.ds(0, side), pl.ds(side, side)
            return [
                remote(
                    source.at[:, 1 - link.x, :, left], landing.at[0], sems, base + 2, link.x_side
                ),
                remote(
                    source.at[1 - link.y, :, :, right], landing.at[1], sems, base + 3, link.y_side
                ),
            ]
        return [
            remote(source.at[0, 1 - link.y], landing.at[0], sems, base + 4, link.y_side),
            remote(source.at[1, 1 - link.x], landing.at[1], sems, base + 5, link.x_side),
        ]

    def start(self, number):
        go(self.hop(number))

    def land(self, number):
        link = self.link
        finish(self.hop(number))
        own, landing = self.held[number - 1], self.held[number]

        def one(row):
            if number == 1:
                for other in range(4):
                    y, x = other // 2, other % 2
                    landing[row, y, x] += own[row, link.z_low, y, x]
            elif number == 2:
                for other in range(2):
                    landing[row, other] += own[row, other]
            else:
                side = landing.shape[-1]
                landing[0, row] += own[row, link.x, :, 0:side]
                landing[1, row] += own[link.y, row, :, side:]

        each(2, one)

    def total(self):
        finish(self.hop(4))
        own, landed = self.held[3], self.held[4]
        return jnp.concatenate(
            [own[0, self.link.y] + landed[0], own[1, self.link.x] + landed[1]], axis=-1
        )


def hop_shapes(rows, columns):
    return [
        (2, 2, 2, rows, columns),
        (2, 2, rows, columns),
        (2, rows, columns),
        (rows, columns),
    ]


def front_kernel(
    dp_size,
    tokens,
    first_values,
    skip_map,
    gain_ref,
    shift_ref,
    wq_ref,
    wk_ref,
    wv_ref,
    out_w,
    up_w,
    down_w,
    n1_ref,
    q_ref,
    k_ref,
    v_ref,
    att_ref,
    lse_ref,
    w_ref,
    sel_ref,
    out_peer,
    up_peer,
    down_peer,
    x_scr,
    fv_scr,
    proj_own,
    proj_send,
    proj_recv,
    sel_send,
    sel_recv,
    out_low,
    up_low,
    down_low,
    out_send,
    up_send,
    down_send,
    out_recv,
    up_recv,
    down_recv,
    lse_scr,
    local_sem,
    send_sem,
    recv_sem,
):
    step = pl.program_id(0)
    length, width = x_scr.shape
    blocks = length // BLOCK
    half = pl.num_programs(0) // 2
    own_width = wq_ref.shape[1]
    fresh_width = wv_ref.shape[0]
    fv_width = fv_scr.shape[1]
    link = Link(dp_size)
    sems = (send_sem, recv_sem)
    rows_here = pl.ds(link.core * length, length)
    local = [
        pltpu.make_async_copy(tokens.at[rows_here], x_scr, local_sem.at[0]),
        pltpu.make_async_copy(first_values.at[rows_here], fv_scr, local_sem.at[1]),
        pltpu.make_async_copy(up_w, up_low, local_sem.at[2]),
        pltpu.make_async_copy(down_w, down_low, local_sem.at[3]),
        pltpu.make_async_copy(out_w, out_low, local_sem.at[4]),
    ]
    early = [
        remote(proj_send, proj_recv, sems, 0, link.peer),
        remote(sel_send, sel_recv, sems, 1, link.peer),
    ]
    late = [
        remote(up_send, up_recv, sems, 2, link.peer),
        remote(down_send, down_recv, sems, 3, link.peer),
        remote(out_send, out_recv, sems, 4, link.peer),
    ]
    landed = [
        (late[0], up_recv, up_low, pltpu.make_async_copy(up_low, up_peer, local_sem.at[2])),
        (late[1], down_recv, down_low, pltpu.make_async_copy(down_low, down_peer, local_sem.at[3])),
        (late[2], out_recv, out_low, pltpu.make_async_copy(out_low, out_peer, local_sem.at[4])),
    ]

    @pl.when(step == 0)
    def _():
        link.greet([link.peer])
        go(local)
        proj_own[2, :, 0:fresh_width] = jnp.transpose(wv_ref[...])
        proj_own[2, :, fresh_width:] = jnp.zeros((width, own_width - fresh_width), BF16)
        for part, source in enumerate((wq_ref, wk_ref)):
            recast(source, proj_own.at[part])
        for part in range(3):
            recast(proj_own.at[part], proj_send.at[part])
        row = lax.broadcasted_iota(jnp.int32, (fv_width, own_width), 0)
        col = lax.broadcasted_iota(jnp.int32, (fv_width, own_width), 1)
        slots = (own_width - fresh_width) // HEAD_DIM
        target = jnp.full((fv_width, own_width), -1, jnp.int32)
        for slot in range(slots):
            start = fresh_width + slot * HEAD_DIM
            inside = jnp.logical_and(col >= start, col < start + HEAD_DIM)
            target = jnp.where(inside, skip_map[slot] * HEAD_DIM + col - start, target)
        chosen = jnp.where(row == target, 1.0, 0.0).astype(F32)
        sel_send[...] = chosen
        sel_ref[:, 0:own_width] = chosen.astype(BF16)
        link.meet([link.peer])
        go(early)
        lse_scr[...] = jnp.zeros_like(lse_scr)
        local[0].wait()
        local[1].wait()

        def one(block, carry):
            rows = pl.ds(block * BLOCK, BLOCK)
            normed, _ = norm_stats(x_scr[rows, :].astype(F32))
            n1_ref[rows, :] = (normed * gain_ref[...][None, :] + shift_ref[...][None, :]).astype(BF16)
            return carry

        lax.fori_loop(0, blocks, one, 0)

    @pl.when(step == half)
    def _():
        finish(early)
        sel_ref[:, own_width:] = sel_recv[...].astype(BF16)

    @pl.when(step < half)
    def _():
        cols = pl.ds(pl.multiple_of(step * PAIR, PAIR), PAIR)
        for part in range(3):
            w_ref[:, part * PAIR : (part + 1) * PAIR] = proj_own[part, :, cols]

    @pl.when(step >= half)
    def _():
        cols = pl.ds(pl.multiple_of((step - half) * PAIR, PAIR), PAIR)
        for part in range(3):
            w_ref[:, part * PAIR : (part + 1) * PAIR] = proj_recv[part, :, cols].astype(BF16)

    sel_cols = pl.ds(pl.multiple_of(step * PAIR, PAIR), PAIR)
    for block in range(blocks):
        rows = slice(block * BLOCK, (block + 1) * BLOCK)
        fused = dot_nn(n1_ref[rows, :], w_ref[...])
        picked = dot_nn(fv_scr[rows, :], sel_ref[:, sel_cols])
        q_ref[rows, :] = (fused[:, 0:PAIR].astype(BF16).astype(F32) * HEAD_DIM**-0.5).astype(BF16)
        k_ref[rows, :] = fused[:, PAIR : 2 * PAIR].astype(BF16)
        v_ref[rows, :] = (fused[:, 2 * PAIR :] + picked).astype(BF16)

    lane = lax.broadcasted_iota(jnp.int32, (BLOCK, PAIR), 1)
    row_pos = lax.broadcasted_iota(jnp.int32, (BLOCK, BLOCK), 0)
    col_pos = lax.broadcasted_iota(jnp.int32, (BLOCK, BLOCK), 1)
    seen = col_pos <= row_pos
    items = [(block, head) for block in range(blocks) for head in range(2)]
    scores, weights, partial = {}, {}, {}

    def score(index):
        block, head = items[index]
        lo, hi = block * BLOCK, (block + 1) * BLOCK
        query = split_heads(q_ref[lo:hi, :])[head]
        diag = dot_nt(query, k_ref[lo:hi, :])
        scores[index] = (diag, dot_nt(query, k_ref[0:lo, :]) if block else None)

    def soften(index):
        block, head = items[index]
        lo, hi = block * BLOCK, (block + 1) * BLOCK
        diag, past = scores.pop(index)
        diag = jnp.where(seen, diag, FILL)
        peak = jnp.max(diag, axis=-1, keepdims=True)
        if block:
            peak = jnp.maximum(peak, jnp.max(past, axis=-1, keepdims=True))
        diag = jnp.exp(diag - peak)
        mass = jnp.sum(diag, axis=-1, keepdims=True)
        if block:
            past = jnp.exp(past - peak)
            mass = mass + jnp.sum(past, axis=-1, keepdims=True)
        inverse = 1.0 / mass
        weights[index] = (
            (diag * inverse).astype(BF16),
            (past * inverse).astype(BF16) if block else None,
        )
        lse_scr[lo:hi, :] = jnp.where(
            lane == 2 * step + head, peak + jnp.log(mass), lse_scr[lo:hi, :]
        )

    def attend(index):
        block, head = items[index]
        lo, hi = block * BLOCK, (block + 1) * BLOCK
        diag, past = weights.pop(index)
        total = dot_nn(diag, split_heads(v_ref[lo:hi, :])[head])
        if block:
            total = total + dot_nn(past, split_heads(v_ref[0:lo, :])[head])
        if head == 0:
            partial[block] = total
        else:
            att_ref[lo:hi, :] = (partial.pop(block) + total).astype(BF16)

    for index in range(len(items) + 2):
        if index < len(items):
            score(index)
        if 0 <= index - 1 < len(items):
            soften(index - 1)
        if index >= 2:
            attend(index - 2)

    @pl.when(step == 0)
    def _():
        for copy in local[2:]:
            copy.wait()
        recast(up_low, up_send)
        recast(down_low, down_send)
        recast(out_low, out_send)
        go(late)

    @pl.when(step == pl.num_programs(0) - 2)
    def _():
        for copy, recv, low, store in landed:
            copy.wait()
            recast(recv, low)
            store.start()

    @pl.when(step == pl.num_programs(0) - 1)
    def _():
        for block in range(blocks):
            lo, hi = block * BLOCK, (block + 1) * BLOCK
            turned = jnp.transpose(lse_scr[lo:hi, :])
            for pair in range(lse_ref.shape[0]):
                lse_ref[pair, 0:2, lo:hi] = turned[2 * pair : 2 * pair + 2, :]
        for _, _, _, store in landed:
            store.wait()


def front(dp_size, tokens, first_values, skip_map, gain, shift, wq, wk, wv, out_w, up_w, down_w):
    width = tokens.shape[1]
    own_width = wq.shape[1]
    half = own_width // PAIR
    fv_width = first_values.shape[1]
    pair_block = pl.BlockSpec((SEQ_LEN, PAIR), lambda i: (0, i))
    pair_out = jax.ShapeDtypeStruct((SEQ_LEN, 2 * own_width), BF16)
    return pl.pallas_call(
        functools.partial(front_kernel, dp_size),
        grid=(2 * half,),
        in_specs=[
            ANY,
            ANY,
            SMEM,
            fixed((width,)),
            fixed((width,)),
            fixed(wq.shape),
            fixed(wk.shape),
            fixed(wv.shape),
            ANY,
            ANY,
            ANY,
        ],
        out_specs=[
            fixed((SEQ_LEN, width)),
            pair_block,
            pair_block,
            pair_block,
            pair_block,
            fixed((2 * half, 8, SEQ_LEN)),
            pl.BlockSpec((width, 3 * PAIR), lambda i: (0, i)),
            fixed((fv_width, 2 * own_width)),
            ANY,
            ANY,
            ANY,
        ],
        scratch_shapes=[
            pltpu.VMEM((SEQ_LEN, width), BF16),
            pltpu.VMEM((SEQ_LEN, fv_width), BF16),
            pltpu.VMEM((3, width, own_width), BF16),
            pltpu.VMEM((3, width, own_width), F32),
            pltpu.VMEM((3, width, own_width), F32),
            pltpu.VMEM((fv_width, own_width), F32),
            pltpu.VMEM((fv_width, own_width), F32),
            pltpu.VMEM(out_w.shape, BF16),
            pltpu.VMEM(up_w.shape, BF16),
            pltpu.VMEM(down_w.shape, BF16),
            pltpu.VMEM(out_w.shape, F32),
            pltpu.VMEM(up_w.shape, F32),
            pltpu.VMEM(down_w.shape, F32),
            pltpu.VMEM(out_w.shape, F32),
            pltpu.VMEM(up_w.shape, F32),
            pltpu.VMEM(down_w.shape, F32),
            pltpu.VMEM((SEQ_LEN, PAIR), F32),
            pltpu.SemaphoreType.DMA((5,)),
            pltpu.SemaphoreType.DMA((5,)),
            pltpu.SemaphoreType.DMA((5,)),
        ],
        out_shape=[
            jax.ShapeDtypeStruct((SEQ_LEN, width), BF16),
            pair_out,
            pair_out,
            pair_out,
            pair_out,
            jax.ShapeDtypeStruct((2 * half, 8, SEQ_LEN), F32),
            jax.ShapeDtypeStruct((width, 6 * own_width), BF16),
            jax.ShapeDtypeStruct((fv_width, 2 * own_width), BF16),
            jax.ShapeDtypeStruct(out_w.shape, BF16),
            jax.ShapeDtypeStruct(up_w.shape, BF16),
            jax.ShapeDtypeStruct(down_w.shape, BF16),
        ],
        compiler_params=params(0, 60),
        name="front",
    )(tokens, first_values, skip_map, gain, shift, wq, wk, wv, out_w, up_w, down_w)


def gelu_pair(upper):
    scale = (2.0 / jnp.pi) ** 0.5
    square = upper * upper
    inner = upper * (scale + (scale * 0.044715) * square)
    tanh = jnp.tanh(inner)
    cdf = 0.5 + 0.5 * tanh
    slope = cdf + 0.5 * upper * (1.0 - tanh * tanh) * (scale + (3.0 * scale * 0.044715) * square)
    return upper * cdf, slope


def middle_kernel(dp_size, ring, n_exports, *refs):
    (
        tokens,
        attended,
        cotangent,
        seq_count,
        gain_ref,
        shift_ref,
        wo_own,
        wo_peer,
        up_own,
        down_own,
        up_peer,
        down_peer,
        layer_out,
        gmix_out,
        gheads_ref,
        og_own,
        og_peer,
        vec_ref,
    ) = refs[:18]
    exports = refs[18 : 18 + n_exports]
    (
        att_ref,
        mixed_scr,
        stage_scr,
        two_scr,
        low_scr,
        two_t,
        low_t,
        act_scr,
        gup_scr,
        up_scr,
        down_scr,
        wo_scr,
        post_scr,
        grad_scr,
        local_sem,
        send_sem,
        recv_sem,
    ) = refs[18 + n_exports : 35 + n_exports]
    ring_scr = refs[35 + n_exports :]
    step = pl.program_id(0)
    steps = pl.num_programs(0)
    length, width = mixed_scr.shape
    blocks = length // BLOCK
    own_width = wo_own.shape[0]
    own_ff = up_own.shape[1]
    chunks = grad_scr.shape[0]
    ff_block = own_ff // chunks
    link = Link(dp_size)
    sems = (send_sem, recv_sem)
    rows_here = pl.ds(link.core * length, length)
    x_ref = gheads_ref
    loads = [
        pltpu.make_async_copy(tokens.at[rows_here], x_ref, local_sem.at[0]),
        pltpu.make_async_copy(wo_own, wo_scr.at[pl.ds(0, own_width)], local_sem.at[1]),
        pltpu.make_async_copy(wo_peer, wo_scr.at[pl.ds(own_width, own_width)], local_sem.at[2]),
        pltpu.make_async_copy(cotangent.at[rows_here], low_scr, local_sem.at[3]),
        pltpu.make_async_copy(attended, att_ref, local_sem.at[16]),
    ]
    weight_loads = [
        pltpu.make_async_copy(up_own, up_scr.at[:, pl.ds(0, own_ff)], local_sem.at[4]),
        pltpu.make_async_copy(up_peer, up_scr.at[:, pl.ds(own_ff, own_ff)], local_sem.at[5]),
        pltpu.make_async_copy(down_own, down_scr.at[pl.ds(0, own_ff)], local_sem.at[6]),
        pltpu.make_async_copy(down_peer, down_scr.at[pl.ds(own_ff, own_ff)], local_sem.at[7]),
    ]
    gmix_copy = pltpu.make_async_copy(mixed_scr, gmix_out, local_sem.at[8])

    def layer_copies(block):
        rows = pl.ds(link.core * length + block * BLOCK, BLOCK)
        return [
            pltpu.make_async_copy(
                stage_scr.at[lax.rem(block, 2)], layer_out.at[rows], local_sem.at[9 + block]
            ),
            remote(stage_scr.at[lax.rem(block, 2)], layer_out.at[rows], sems, block, link.peer),
        ]


    def swap(chunk):
        return remote(
            post_scr.at[lax.rem(chunk, 2)], grad_scr.at[chunk], sems, blocks + chunk, link.peer
        )

    flows = {}
    if ring:
        base = blocks + chunks
        hop1, hop2, deep1 = ring_scr
        for slot, chunk in enumerate((0, 2, 4, 5)):
            flows[chunk] = Chunk(
                link,
                sems,
                base + HOPS * chunk,
                grad_scr.at[chunk],
                hop1.at[slot],
                None if chunk else hop2,
            )
        for slot, chunk in enumerate((1, 3)):
            flows[chunk] = DeepChunk(
                link, sems, base + HOPS * chunk, grad_scr.at[chunk], deep1.at[slot]
            )

    partners = [link.peer]
    if ring:
        partners += [link.x_side, link.y_side, link.z_side]

    def run(events):
        for chunk, number in events:
            if ring:
                if number > 1:
                    flows[chunk].land(number - 1)
                flows[chunk].start(number)

    @pl.when(step == 0)
    def _():
        link.greet(partners)
        go(loads)
        go(weight_loads)
        finish(loads)
        live = jnp.where(link.core < seq_count[0], 1.0, 0.0).astype(F32)

        def enter(block):
            rows = row_block(block)
            mixed = x_ref[rows, :].astype(F32) + dot_nn(att_ref[rows, :], wo_scr[...])
            mixed_scr[rows, :] = mixed
            normed, _ = norm_stats(mixed)
            two_low = (normed * gain_ref[...][None, :] + shift_ref[...][None, :]).astype(BF16)
            two_scr[rows, :] = two_low
            two_t[:, rows] = jnp.transpose(two_low)
            low = (low_scr[rows, :].astype(F32) * live).astype(BF16)
            low_scr[rows, :] = low
            low_t[:, rows] = jnp.transpose(low)

        each(blocks, enter)
        finish(weight_loads)
        link.meet(partners)

    last = lax.div(step, steps - 1)
    mine = (1 - lax.rem(step, 2)) * lax.div(step + steps - 1, steps) + last
    mine_index = lax.div(step - 1 + lax.div(steps - step, steps), 2)
    post_index = lax.div(step + 1, 2)
    turn = mine * mine_index + (1 - mine) * (chunks + post_index)
    slot = 2 * mine + (1 - mine) * lax.rem(post_index, 2)
    cols = pl.ds(pl.multiple_of(turn * ff_block, ff_block), ff_block)
    for block in range(blocks):
        rows = slice(block * BLOCK, (block + 1) * BLOCK)
        upper = dot_nn(two_scr[rows, :], up_scr[:, cols])
        active, slope = gelu_pair(upper)
        act_scr[rows, cols] = active.astype(BF16)
        grad_active = dot_nt(low_scr[rows, :], down_scr[cols, :])
        gup_scr[rows, cols] = (grad_active * slope).astype(BF16)

    block_shape = grad_scr.shape[1:-1] + (ff_block,)
    @pl.when(jnp.logical_and(mine == 0, post_index > 1))
    def _():
        swap(post_index - 2).wait_send()

    post_scr[slot, ..., 0:ff_block] = dot_nn(low_t[...], act_scr[:, cols]).reshape(block_shape)
    post_scr[slot, ..., ff_block:] = dot_nn(two_t[...], gup_scr[:, cols]).reshape(block_shape)

    @pl.when(mine == 0)
    def _():
        swap(post_index).start()

    @pl.when(mine == 1)
    def _():
        swap(mine_index).wait_recv()
        grad_scr[mine_index] += post_scr[2]

    if ring:
        for when, events in {
            2: [(0, 1)],
            4: [(1, 1)],
            6: [(2, 1)],
            8: [(3, 1), (0, 2)],
            10: [(4, 1)],
            11: [(5, 1)],
        }.items():

            @pl.when(step == when)
            def _():
                run(events)

    @pl.when(step == steps - 1)
    def _():
        swap(chunks - 2).wait_send()
        swap(chunks - 1).wait_send()
        if not ring:
            whole_copy = pltpu.make_async_copy(grad_scr, exports[0], local_sem.at[13])
            whole_copy.start()

        def leave(block):
            rows = row_block(block)

            @pl.when(block > 1)
            def _():
                finish(layer_copies(block - 2))

            stage_scr[lax.rem(block, 2)] = mixed_scr[rows, :] + dot_nn(
                act_scr[rows, :], down_scr[...]
            )
            go(layer_copies(block))

        each(blocks, leave)
        vec_ref[...] = jnp.zeros_like(vec_ref)

        def turn_back(block):
            rows = row_block(block)
            grad_two = dot_nt(gup_scr[rows, :], up_scr[...])
            normed, factor = norm_stats(mixed_scr[rows, :])
            vec_ref[0:1, :] += jnp.sum(grad_two * normed, axis=0, keepdims=True)
            vec_ref[1:2, :] += jnp.sum(grad_two, axis=0, keepdims=True)
            grad_mixed = low_scr[rows, :].astype(F32) + norm_backward(
                grad_two, normed, factor, gain_ref[...][None, :]
            )
            mixed_scr[rows, :] = grad_mixed
            grad_attn = grad_mixed.astype(BF16)
            low_t[:, rows] = jnp.transpose(grad_attn)
            gheads_ref[rows, :] = dot_nt(grad_attn, wo_scr[...]).astype(BF16)

        each(blocks, turn_back)
        gmix_copy.start()
        og_peer[...] = dot_nn(low_t[...], att_ref[:, own_width:]).reshape(og_peer.shape)
        og_own[...] = dot_nn(low_t[...], att_ref[:, 0:own_width]).reshape(og_own.shape)
        if ring:
            at_one, at_two, at_deep = exports
            outs = [
                pltpu.make_async_copy(hop1.at[pl.ds(1, 3)], at_one, local_sem.at[13]),
                pltpu.make_async_copy(hop2, at_two, local_sem.at[14]),
                pltpu.make_async_copy(deep1, at_deep, local_sem.at[15]),
            ]
            flows[0].land(2)
            outs[1].start()
            flows[1].land(1)
            flows[3].land(1)
            outs[2].start()
            flows[2].land(1)
            flows[5].land(1)
            flows[4].land(1)
            outs[0].start()
            finish(outs)
        else:
            whole_copy.wait()
        gmix_copy.wait()
        finish(layer_copies(blocks - 2))
        finish(layer_copies(blocks - 1))


def middle(
    dp_size, ring, tokens, attended, cotangent, seq_count, gain, shift, wo_own, wo_peer, own, peer
):
    width = tokens.shape[1]
    own_ff = own[0].shape[1]
    own_width = wo_own.shape[0]
    chunks = 6
    ff_block = own_ff // chunks
    grad_shape = place(ring, width, dp_size, 2 * ff_block)
    og_shape = place(ring, width, dp_size, own_width)
    scratch = []
    if ring:
        hop1, hop2, _, _ = hop_shapes(width // dp_size, 2 * ff_block)
        export_shapes = [(3,) + hop1, hop2, (2,) + hop1]
        scratch = [
            pltpu.VMEM((4,) + hop1, F32),
            pltpu.VMEM(hop2, F32),
            pltpu.VMEM((2,) + hop1, F32),
        ]
    else:
        export_shapes = [(chunks,) + grad_shape]
    blocks = SEQ_LEN // BLOCK
    n_sems = blocks + chunks + HOPS * chunks
    return pl.pallas_call(
        functools.partial(middle_kernel, dp_size, ring, len(export_shapes)),
        grid=(2 * chunks,),
        in_specs=[
            ANY,
            ANY,
            ANY,
            SMEM,
            fixed((width,)),
            fixed((width,)),
            ANY,
            ANY,
            ANY,
            ANY,
            ANY,
            ANY,
        ],
        out_specs=[
            ANY,
            ANY,
            fixed((SEQ_LEN, 2 * own_width)),
            fixed(og_shape),
            fixed(og_shape),
            fixed((8, width)),
        ]
        + [ANY] * len(export_shapes),
        scratch_shapes=[
            pltpu.VMEM((SEQ_LEN, 2 * own_width), BF16),
            pltpu.VMEM((SEQ_LEN, width), F32),
            pltpu.VMEM((2, BLOCK, width), F32),
            pltpu.VMEM((SEQ_LEN, width), BF16),
            pltpu.VMEM((SEQ_LEN, width), BF16),
            pltpu.VMEM((width, SEQ_LEN), BF16),
            pltpu.VMEM((width, SEQ_LEN), BF16),
            pltpu.VMEM((SEQ_LEN, 2 * own_ff), BF16),
            pltpu.VMEM((SEQ_LEN, 2 * own_ff), BF16),
            pltpu.VMEM((width, 2 * own_ff), BF16),
            pltpu.VMEM((2 * own_ff, width), BF16),
            pltpu.VMEM((2 * own_width, width), BF16),
            pltpu.VMEM((3,) + grad_shape, F32),
            pltpu.VMEM((chunks,) + grad_shape, F32),
            pltpu.SemaphoreType.DMA((17,)),
            pltpu.SemaphoreType.DMA((n_sems,)),
            pltpu.SemaphoreType.DMA((n_sems,)),
        ]
        + scratch,
        out_shape=[
            jax.ShapeDtypeStruct((2 * SEQ_LEN, width), F32),
            jax.ShapeDtypeStruct((SEQ_LEN, width), F32),
            jax.ShapeDtypeStruct((SEQ_LEN, 2 * own_width), BF16),
            jax.ShapeDtypeStruct(og_shape, F32),
            jax.ShapeDtypeStruct(og_shape, F32),
            jax.ShapeDtypeStruct((8, width), F32),
        ]
        + [jax.ShapeDtypeStruct(shape, F32) for shape in export_shapes],
        compiler_params=params(1, 60),
        name="middle",
    )(tokens, attended, cotangent, seq_count, gain, shift, wo_own, wo_peer, *own, *peer)


def back_kernel(dp_size, ring, counts, *refs):
    n_in, n_out, fresh_width = counts
    (
        tokens,
        n1_ref,
        q_ref,
        k_ref,
        v_ref,
        att_ref,
        gheads_ref,
        lse_ref,
        gmix,
        gain_ref,
        w_ref,
        sel_ref,
        og_own,
        og_peer,
        vec2_ref,
    ) = refs[:15]
    exports = refs[15:n_in]
    in_grad, first_grad = refs[n_in : n_in + 2]
    outs = refs[n_in + 2 : n_in + n_out]
    scratch = refs[n_in + n_out :]
    (
        x_scr,
        gmix_scr,
        n1_t,
        dk_acc,
        dv_acc,
        dq_t,
        stack_scr,
        one_acc,
        fv_t,
        post_scr,
        out_scr,
        sums_scr,
        local_sem,
        send_sem,
        recv_sem,
    ) = scratch[:15]
    step = pl.program_id(0)
    steps = pl.num_programs(0)
    length, width = x_scr.shape
    blocks = length // BLOCK
    link = Link(dp_size)
    sems = (send_sem, recv_sem)
    rows_here = pl.ds(link.core * length, length)
    chunks = lse_ref.shape[0] * steps // 2
    grads = scratch[15 : 15 + chunks]
    ring_scr = list(scratch[15 + chunks :])
    side = fv_t.shape[0] // 2
    loads = [
        pltpu.make_async_copy(tokens.at[rows_here], x_scr, local_sem.at[0]),
        pltpu.make_async_copy(gmix, gmix_scr, local_sem.at[1]),
        pltpu.make_async_copy(og_own, out_scr.at[0], local_sem.at[2]),
    ]
    out_swap = remote(og_peer, out_scr.at[1], sems, 0, link.peer)
    swaps = [
        remote(
            post_scr.at[0, ..., pl.ds(0, grads[chunk].shape[-1])],
            grads[chunk],
            sems,
            1 + chunk,
            link.peer,
        )
        for chunk in range(chunks)
    ]
    base = 1 + chunks
    in_copies = [
        remote(one_acc, in_grad.at[rows_here], sems, base, link.peer),
        pltpu.make_async_copy(one_acc, in_grad.at[rows_here], local_sem.at[3]),
    ]
    seq_cols = pl.ds(pl.multiple_of(link.core * length, length), length)
    first_copies = [
        remote(
            fv_t.at[pl.ds((1 - link.core) * side, side)],
            first_grad.at[:, seq_cols],
            sems,
            base + 1,
            link.peer,
        ),
        pltpu.make_async_copy(
            fv_t.at[pl.ds(link.core * side, side)], first_grad.at[:, seq_cols], local_sem.at[4]
        ),
    ]
    base += 2
    flows = {}
    if ring:
        at_one, at_two, at_deep = exports
        hop1, hop2, hop3, hop4, deep1, deep2, deep3, deep4 = ring_scr[:8]
        del ring_scr[:8]
        for slot, chunk in enumerate((0, 2, 4, 5)):
            flows[chunk] = Chunk(
                link,
                sems,
                base + slot * HOPS,
                None,
                None if chunk == 0 else hop1.at[slot - 1],
                hop2.at[slot],
                hop3.at[slot],
                hop4.at[slot],
            )
            if chunk:
                flows[chunk].sources[1] = at_one.at[slot - 1]
        flows[0].sources[2] = at_two
        for slot, chunk in enumerate((1, 3)):
            flows[chunk] = DeepChunk(
                link,
                sems,
                base + (4 + slot) * HOPS,
                None,
                deep1.at[slot],
                deep2.at[slot],
                deep3.at[slot],
                deep4.at[slot],
            )
            flows[chunk].sources[1] = at_deep.at[slot]
        ring_loads = [
            pltpu.make_async_copy(at_one, hop1, local_sem.at[5]),
            pltpu.make_async_copy(at_two, hop2.at[0], local_sem.at[6]),
            pltpu.make_async_copy(at_deep.at[0, link.z_high], deep1.at[0], local_sem.at[7]),
            pltpu.make_async_copy(at_deep.at[1, link.z_high], deep1.at[1], local_sem.at[8]),
        ]
        wholes = {"o": out_scr.at[0]}
        wholes.update({"p%d" % n: grads[n] for n in range(chunks)})
        place_in = base + 6 * HOPS
        for name, whole in wholes.items():
            flows[name] = Chunk(link, sems, place_in, whole, *ring_scr[:4])
            del ring_scr[:4]
            place_in += HOPS
        v_send, v_recv = ring_scr[:2]
        flows["v"] = Chunk(link, sems, place_in, v_recv, *ring_scr[2:6])
        vec_swap = remote(v_send, v_recv, sems, place_in + HOPS, link.peer)

    ready = [(1, 2), (2, 2), (3, 2), (4, 2), (5, 2), (0, 3)]

    def run(events):
        for name, number in events:
            if ring:
                if number > 1 and (name, number) not in ready:
                    flows[name].land(number - 1)
                flows[name].start(number)

    @pl.when(step == 0)
    def _():
        partners = [link.peer]
        if ring:
            partners += [link.x_side, link.y_side, link.z_side, link.z_far]
        link.greet(partners)
        link.meet(partners)
        if ring:
            flows[2].start(2)
            flows[3].start(2)
            flows[5].start(2)
            flows[0].start(3)
        out_swap.start()
        go(loads)
        if ring:
            go(ring_loads)
        for block in range(blocks):
            rows = slice(block * BLOCK, (block + 1) * BLOCK)
            n1_t[:, rows] = jnp.transpose(n1_ref[rows, :])
        one_acc[...] = jnp.zeros_like(one_acc)
        fv_t[...] = jnp.zeros_like(fv_t)

    k_t = jnp.transpose(k_ref[...])
    prod_t = jnp.transpose(gheads_ref[...].astype(F32) * att_ref[...].astype(F32))
    lse_pair = lse_ref[0]
    row_pos = lax.broadcasted_iota(jnp.int32, (BLOCK, BLOCK), 0)
    col_pos = lax.broadcasted_iota(jnp.int32, (BLOCK, BLOCK), 1)
    seen = row_pos <= col_pos
    items = [
        (block, head, source)
        for block in range(blocks)
        for head in range(2)
        for source in range(block + 1)
    ]
    raw, soft_low, dq_sums = {}, {}, {}

    def part_of(ref, block, head):
        return split_heads(ref[block * BLOCK : (block + 1) * BLOCK, :])[head]

    def score(index):
        block, head, source = items[index]
        rows = slice(source * BLOCK, (source + 1) * BLOCK)
        raw[index] = (
            dot_nt(k_ref[rows, :], part_of(q_ref, block, head)),
            dot_nt(v_ref[rows, :], part_of(gheads_ref, block, head)),
        )

    def soften(index):
        block, head, source = items[index]
        cols = slice(block * BLOCK, (block + 1) * BLOCK)
        part = slice(head * HEAD_DIM, (head + 1) * HEAD_DIM)
        delta = jnp.sum(prod_t[part, cols], axis=0, keepdims=True)
        scores, dsoft = raw.pop(index)
        soft = jnp.exp(scores - lse_pair[head : head + 1, cols])
        if source == block:
            soft = jnp.where(seen, soft, 0.0)
        soft_low[index] = (soft.astype(BF16), (soft * (dsoft - delta)).astype(BF16))

    def spread(index):
        block, head, source = items[index]
        rows = slice(source * BLOCK, (source + 1) * BLOCK)
        part = slice(head * HEAD_DIM, (head + 1) * HEAD_DIM)
        soft, dscore = soft_low.pop(index)
        dv = dot_nn(soft, part_of(gheads_ref, block, head))
        dk = dot_nn(dscore, part_of(q_ref, block, head))
        if head == 0 and source == block:
            dv_acc[rows, :] = dv
            dk_acc[rows, :] = dk
        else:
            dv_acc[rows, :] += dv
            dk_acc[rows, :] += dk
        dq = dot_nn(k_t[part, rows], dscore)
        dq_sums[block, head] = dq if source == 0 else dq_sums[block, head] + dq
        if source == block:
            dq_t[part, block * BLOCK : (block + 1) * BLOCK] = dq_sums.pop((block, head))

    for index in range(len(items) + 2):
        if index < len(items):
            score(index)
        if 0 <= index - 1 < len(items):
            soften(index - 1)
        if index >= 2:
            spread(index - 2)

    middle_events = {
        2: [(5, 3)],
        3: [(3, 3), (4, 3)],
        4: [("o", 3), (5, 4)],
        5: [("p1", 2), (4, 4)],
    }
    end_events = {
        0: [("o", 1)],
        1: [("p0", 1), (1, 2), (4, 2), (2, 3)],
        2: [("o", 2)],
        3: [("p1", 1)],
        4: [("p0", 2)],
        5: [("p2", 1), ("p0", 3), (0, 4), (2, 4), ("o", 4)],
    }
    if ring:
        for when, events in middle_events.items():

            @pl.when(step == when)
            def _():
                run(events)

        @pl.when(step == 0)
        def _():
            finish(ring_loads)

    for block in range(blocks):
        rows = slice(block * BLOCK, (block + 1) * BLOCK)
        stack_scr[rows, 0:PAIR] = (jnp.transpose(dq_t[:, rows]) * HEAD_DIM**-0.5).astype(BF16)
        stack_scr[rows, PAIR : 2 * PAIR] = dk_acc[rows, :].astype(BF16)
        dv = dv_acc[rows, :]
        stack_scr[rows, 2 * PAIR : 3 * PAIR] = dv.astype(BF16)
        one_acc[rows, :] += dot_nt(stack_scr[rows, :], w_ref[...])

    @pl.when(step >= 2 * (fresh_width // PAIR))
    def _():
        for block in range(blocks):
            rows = slice(block * BLOCK, (block + 1) * BLOCK)
            dv = dv_acc[rows, :]
            high = dv.astype(BF16)
            low = (dv - high.astype(F32)).astype(BF16)
            fv_t[:, rows] += dot_nt(sel_ref[...], high) + dot_nt(sel_ref[...], low)

    for chunk in range(1, chunks):

        @pl.when(step == 2 * chunk)
        def _():
            swaps[chunk - 1].wait_send()

    post_scr[lax.rem(step, 2)] = dot_nn(n1_t[...], stack_scr[...]).reshape(post_scr.shape[1:])
    for chunk in range(chunks):
        used = grads[chunk].shape[-1]

        @pl.when(step == 2 * chunk)
        def _():
            swaps[chunk].start()

        @pl.when(step == 2 * chunk + 1)
        def _():
            swaps[chunk].wait_recv()
            grads[chunk][...] += post_scr[1, ..., 0:used]
            if chunk == chunks - 1:
                swaps[chunk].wait_send()

    @pl.when(step == 0)
    def _():
        out_swap.wait()
        finish(loads)
        out_scr[0] += out_scr[1]

    if ring:
        for when, events in end_events.items():

            @pl.when(step == when)
            def _():
                run(events)

    @pl.when(step == steps - 1)
    def _():
        go(first_copies)
        sums_scr[...] = jnp.zeros_like(sums_scr)

        def leave(block):
            rows = row_block(block)
            normed, factor = norm_stats(x_scr[rows, :].astype(F32))
            grad_one = one_acc[rows, :]
            sums_scr[0:1, :] += jnp.sum(grad_one * normed, axis=0, keepdims=True)
            sums_scr[1:2, :] += jnp.sum(grad_one, axis=0, keepdims=True)
            one_acc[rows, :] = gmix_scr[rows, :] + norm_backward(
                grad_one, normed, factor, gain_ref[...][None, :]
            )

        each(blocks, leave)
        go(in_copies)
        vectors = jnp.concatenate(
            [sums_scr[0:2, :], vec2_ref[0:2, :], jnp.zeros((4, width), F32)], axis=0
        )
        if ring:
            up_out, down_out, q_out, k_out, v_out, o_out, vec_out = outs
            rows_dev = width // dp_size
            v_send[...] = jnp.zeros_like(v_send)
            for block in range(dp_size):
                v_send[block // 8, block // 4 % 2, block // 2 % 2, block % 2, :, 0:rows_dev] = vectors[
                    :, block * rows_dev : (block + 1) * rows_dev
                ]
            vec_swap.start()
            run([("p2", 2)])
            vec_swap.wait()
            v_recv[...] += v_send[...]
            run(
                [("v", 1), (1, 3), ("p1", 3), ("p2", 3), ("v", 2), (1, 4), (3, 4), ("p0", 4), ("p1", 4), ("v", 3), ("p2", 4), ("v", 4)]
            )
            ff_block = up_out.shape[-1] // 6

            def put_ffn(index, total):
                cols = slice(index * ff_block, (index + 1) * ff_block)
                down_out[:, cols] = total[:, 0:ff_block]
                up_out[:, cols] = total[:, ff_block:]

            def put_proj(index, total):
                cols = slice(index * PAIR, (index + 1) * PAIR)
                q_out[:, cols] = total[:, 0:PAIR]
                k_out[:, cols] = total[:, PAIR : 2 * PAIR]
                if total.shape[1] > 2 * PAIR:
                    last = min((index + 1) * PAIR, fresh_width)
                    v_out[:, index * PAIR : last] = total[
                        :, 2 * PAIR : 2 * PAIR + last - index * PAIR
                    ]

            for chunk in range(6):
                put_ffn(chunk, flows[chunk].total())
            o_out[...] = flows["o"].total()
            put_proj(0, flows["p0"].total())
            put_proj(1, flows["p1"].total())
            put_proj(2, flows["p2"].total())
            vec_out[...] = flows["v"].total()
        else:
            vec_out = outs[-1]
            vec_out[...] = vectors
            stores = [
                pltpu.make_async_copy(grads[chunk], outs[chunk], local_sem.at[5 + chunk])
                for chunk in range(chunks)
            ]
            stores.append(pltpu.make_async_copy(out_scr.at[0], outs[chunks], local_sem.at[8]))
            go(stores)
            finish(stores)
        finish(in_copies)
        finish(first_copies)


def back(
    dp_size,
    ring,
    tokens,
    n1,
    q,
    k,
    v,
    attended,
    grad_heads,
    lse,
    grad_mixed,
    gain,
    weights,
    select,
    og_own,
    og_peer,
    vec2,
    exports,
    fresh_width,
    own_ff,
):
    width = tokens.shape[1]
    own_width = og_own.shape[-1]
    half = own_width // PAIR
    fv_width = select.shape[0]
    side = fv_width // 2
    pair_of = lambda i: lax.rem(i + 1, 2) * half + lax.div(i, 2)
    pair_block = pl.BlockSpec((SEQ_LEN, PAIR), lambda i: (0, pair_of(i)))
    used = [3 * PAIR if n * PAIR < fresh_width else 2 * PAIR for n in range(half)]
    grad_shapes = [place(ring, width, dp_size, columns) for columns in used]
    og_shape = place(ring, width, dp_size, own_width)
    scratch = [
        pltpu.VMEM((SEQ_LEN, width), BF16),
        pltpu.VMEM((SEQ_LEN, width), F32),
        pltpu.VMEM((width, SEQ_LEN), BF16),
        pltpu.VMEM((SEQ_LEN, PAIR), F32),
        pltpu.VMEM((SEQ_LEN, PAIR), F32),
        pltpu.VMEM((PAIR, SEQ_LEN), F32),
        pltpu.VMEM((SEQ_LEN, 3 * PAIR), BF16),
        pltpu.VMEM((SEQ_LEN, width), F32),
        pltpu.VMEM((fv_width, SEQ_LEN), F32),
        pltpu.VMEM((2,) + grad_shapes[0], F32),
        pltpu.VMEM((2,) + og_shape, F32),
        pltpu.VMEM((8, width), F32),
        pltpu.SemaphoreType.DMA((11,)),
    ]
    n_sems = 3 + half + (1 + (8 + half) * HOPS if ring else 0)
    scratch += [pltpu.SemaphoreType.DMA((n_sems,))] * 2
    scratch += [pltpu.VMEM(shape, F32) for shape in grad_shapes]
    if ring:
        rows = width // dp_size

        def hops(columns, height=rows, count=None):
            lead = () if count is None else (count,)
            return [lead + shape for shape in hop_shapes(height, columns)]

        ff = exports[0].shape[-1]
        shapes = [(3,) + hops(ff)[0]] + hops(ff, count=4)[1:]
        shapes += [(2, 2, 2, rows, ff)] * 2
        shapes += [(2, 2, 2, rows, ff // 2), (2, 2, rows, ff // 2)]
        shapes += hops(own_width)
        for columns in used:
            shapes += hops(columns)
        vec_whole = place(ring, width, dp_size, PAIR)[:4] + (8, PAIR)
        shapes += [vec_whole, vec_whole] + hops(PAIR, 8)
        scratch += [pltpu.VMEM(shape, F32) for shape in shapes]
        totals = [
            (rows, own_ff),
            (rows, own_ff),
            (rows, own_width),
            (rows, own_width),
            (rows, fresh_width),
            (rows, own_width),
            (8, PAIR),
        ]
        total_specs = [fixed(shape) for shape in totals]
        export_args = list(exports)
        export_specs = [ANY] * len(export_args)
    else:
        totals = grad_shapes + [og_shape, (8, width)]
        total_specs = [ANY] * (half + 1) + [fixed((8, width))]
        export_args, export_specs = [], []
    in_specs = [
        ANY,
        fixed((SEQ_LEN, width)),
        pair_block,
        pair_block,
        pair_block,
        pair_block,
        pair_block,
        pl.BlockSpec((1, 8, SEQ_LEN), lambda i: (pair_of(i), 0, 0)),
        ANY,
        fixed((width,)),
        pl.BlockSpec((width, 3 * PAIR), lambda i: (0, pair_of(i))),
        pl.BlockSpec((fv_width, PAIR), lambda i: (0, pair_of(i))),
        ANY,
        ANY,
        fixed((8, width)),
    ] + export_specs
    return pl.pallas_call(
        functools.partial(
            back_kernel, dp_size, ring, (len(in_specs), 2 + len(totals), fresh_width)
        ),
        grid=(2 * half,),
        in_specs=in_specs,
        out_specs=[ANY, ANY] + total_specs,
        scratch_shapes=scratch,
        out_shape=[
            jax.ShapeDtypeStruct((2 * SEQ_LEN, width), F32),
            jax.ShapeDtypeStruct((side, 2 * SEQ_LEN), F32),
        ]
        + [jax.ShapeDtypeStruct(shape, F32) for shape in totals],
        compiler_params=params(2, 60),
        name="back",
    )(
        tokens,
        n1,
        q,
        k,
        v,
        attended,
        grad_heads,
        lse,
        grad_mixed,
        gain,
        weights,
        select,
        og_own,
        og_peer,
        vec2,
        *export_args,
    )


def collect_kernel(large, *refs):
    half = len(refs) // 2
    pairs = list(zip(refs[:half], refs[half:]))
    for source, target in pairs[:large]:
        target[...] = source[...]

    @pl.when(pl.program_id(0) == 0)
    def _():
        for source, target in pairs[large:]:
            target[...] = source[...]


def collect(tall, columns, small):
    blocks = 2
    rows = tall[0]
    specs = [pl.BlockSpec((rows.shape[0] // blocks, rows.shape[1]), lambda i: (i, 0))] * 2 + [
        pl.BlockSpec((columns.shape[0], columns.shape[1] // blocks), lambda i: (0, i)),
    ] + [fixed(array.shape) for array in small]
    arrays = tall + [columns] + small
    return pl.pallas_call(
        functools.partial(collect_kernel, 3),
        grid=(blocks,),
        in_specs=specs,
        out_specs=specs,
        out_shape=[jax.ShapeDtypeStruct(array.shape, array.dtype) for array in arrays],
        compiler_params=pltpu.CompilerParams(vmem_limit_bytes=60 * 1024 * 1024),
        name="collect",
    )(*arrays)


def on_device(
    dp_size,
    tokens,
    first_values,
    seq_count,
    skip_map,
    norm1_gain,
    norm1_shift,
    query_weight,
    key_weight,
    value_weight,
    out_weight,
    norm2_gain,
    norm2_shift,
    up_weight,
    down_weight,
    cotangent,
):
    width = tokens.shape[1]
    own_width = query_weight.shape[1]
    fresh_width = value_weight.shape[1]
    own_ff = up_weight.shape[1]
    ring = ring_of(dp_size, width)
    gain1, shift1, gain2, shift2 = norm1_gain, norm1_shift, norm2_gain, norm2_shift
    n1, q, k, v, attended, lse, weights, select, out_peer, up_peer, down_peer = front(
        dp_size,
        tokens,
        first_values,
        skip_map,
        gain1,
        shift1,
        query_weight,
        key_weight,
        value_weight.T,
        out_weight,
        up_weight,
        down_weight,
    )
    layer_out, grad_mixed, grad_heads, og_own, og_peer, vec2, *exports = middle(
        dp_size,
        ring,
        tokens,
        attended,
        cotangent,
        seq_count,
        gain2,
        shift2,
        out_weight,
        out_peer,
        (up_weight, down_weight),
        (up_peer, down_peer),
    )
    input_grad, first_grad, *totals = back(
        dp_size,
        ring,
        tokens,
        n1,
        q,
        k,
        v,
        attended,
        grad_heads,
        lse,
        grad_mixed,
        gain1,
        weights,
        select,
        og_own,
        og_peer,
        vec2,
        exports,
        fresh_width,
        own_ff,
    )
    if ring:
        *totals, vectors = totals
        layer_out, input_grad, first_grad, *totals = collect([layer_out, input_grad], first_grad, totals)
        up_total, down_t, query_total, key_total, value_total, out_t = totals
        rows = width // dp_size
        down_total, out_total = down_t.T, out_t.T
        gain1_total, shift1_total, gain2_total, shift2_total = (vectors[n, :rows] for n in range(4))
    else:
        *proj, out_grad, vectors = totals
        chunks = exports[0].shape[0]
        ff_block = own_ff // chunks
        vectors = vectors + lax.ppermute(vectors, "tensor", [(0, 1), (1, 0)])
        columns = list(proj) + [out_grad] + [exports[0][n] for n in range(chunks)]
        packed = jnp.concatenate(columns + [jnp.pad(vectors.T, ((0, 0), (0, 120)))], axis=1)
        summed = lax.psum_scatter(packed, "dp", scatter_dimension=0, tiled=True)
        heads, start = [[], [], []], 0
        for part in proj:
            for n in range(part.shape[1] // PAIR):
                heads[n].append(summed[:, start : start + PAIR])
                start += PAIR
        query_total, key_total, value_total = (jnp.concatenate(part, axis=1) for part in heads)
        value_total = value_total[:, :fresh_width]
        out_total = summed[:, start : start + own_width].T
        start += own_width
        pairs = summed[:, start : start + 2 * own_ff].reshape(-1, chunks, 2, ff_block)
        down_total = pairs[:, :, 0].reshape(-1, own_ff).T
        up_total = pairs[:, :, 1].reshape(-1, own_ff)
        start += 2 * own_ff
        gain1_total, shift1_total, gain2_total, shift2_total = (
            summed[:, start + n] for n in range(4)
        )
    return (
        layer_out,
        input_grad,
        first_grad.T,
        gain1_total,
        shift1_total,
        query_total,
        key_total,
        value_total,
        out_total,
        gain2_total,
        shift2_total,
        up_total,
        down_total,
    )


def solution(mesh):
    placed = (
        P("dp", None),
        P("dp", None),
        P("dp"),
        P("tensor"),
        P(),
        P(),
        P(None, "tensor"),
        P(None, "tensor"),
        P(None, "tensor"),
        P("tensor", None),
        P(),
        P(),
        P(None, "tensor"),
        P("tensor", None),
        P("dp", None),
    )
    return jax.shard_map(
        functools.partial(on_device, mesh.shape["dp"]),
        mesh=mesh,
        in_specs=placed,
        out_specs=(
            P("dp", None),
            P("dp", None),
            P("dp", "tensor"),
            P("dp"),
            P("dp"),
            P("dp", "tensor"),
            P("dp", "tensor"),
            P("dp", "tensor"),
            P("tensor", "dp"),
            P("dp"),
            P("dp"),
            P("dp", "tensor"),
            P("tensor", "dp"),
        ),
        check_vma=False,
    )
```

```python
import functools

import jax
import jax.numpy as jnp
from jax import lax
from jax.experimental import pallas as pl
from jax.experimental.pallas import tpu as pltpu
from jax.sharding import PartitionSpec as P

HEAD_DIM = 64
SEQ_LEN = 1024
BLOCK = 256
PAIR = 2 * HEAD_DIM
EPS = 1e-05
FILL = -1e30

F32 = jnp.float32
BF16 = jnp.bfloat16


def dot_nn(left, right):
    return lax.dot_general(left, right, (((1,), (0,)), ((), ())), preferred_element_type=F32)


def dot_nt(left, right):
    return lax.dot_general(left, right, (((1,), (1,)), ((), ())), preferred_element_type=F32)


def norm_stats(values_in):
    average = jnp.mean(values_in, axis=-1, keepdims=True)
    centered = values_in - average
    variance = jnp.mean(centered * centered, axis=-1, keepdims=True)
    factor = lax.rsqrt(variance + EPS)
    return centered * factor, factor


def norm_backward(grad, normed, factor, gain):
    scaled = grad * gain
    mean_plain = jnp.mean(scaled, axis=-1, keepdims=True)
    mean_cross = jnp.mean(scaled * normed, axis=-1, keepdims=True)
    return factor * (scaled - mean_plain - normed * mean_cross)


def each(count, body):
    lax.fori_loop(0, count, lambda index, carry: (body(index), carry)[1], 0)


def row_block(index):
    return pl.ds(pl.multiple_of(index * BLOCK, BLOCK), BLOCK)


def recast(source, target, rows=128):
    def one(index):
        part = pl.ds(pl.multiple_of(index * rows, rows), rows)
        target[part, :] = source[part, :].astype(target.dtype)

    each(source.shape[0] // rows, one)


def head_masks(rows):
    lanes = lax.broadcasted_iota(jnp.int32, (rows, PAIR), 1)
    return lanes < HEAD_DIM


def split_heads(pair_rows):
    first = head_masks(pair_rows.shape[0])
    zero = jnp.zeros_like(pair_rows)
    return jnp.where(first, pair_rows, zero), jnp.where(first, zero, pair_rows)


MESH = pl.DeviceIdType.MESH


def params(collective_id, vmem_mib):
    return pltpu.CompilerParams(
        vmem_limit_bytes=vmem_mib * 1024 * 1024,
        collective_id=collective_id,
        has_side_effects=True,
    )


def fixed(shape):
    zeros = (0,) * len(shape)
    return pl.BlockSpec(shape, lambda i: zeros, pipeline_mode=pl.Buffered(1))


ANY = pl.BlockSpec(memory_space=pl.ANY)
SMEM = pl.BlockSpec(memory_space=pltpu.SMEM)


def ring_of(dp_size, width):
    return dp_size == 4 * 4 and width % (8 * dp_size) == 0


def place(ring, width, dp_size, columns):
    if not ring:
        return (width, columns)
    return (2, 2, 2, 2, width // dp_size, columns)


class Link:
    def __init__(self, dp_size):
        self.dp = lax.axis_index("dp")
        self.core = lax.axis_index("tensor")
        self.x = lax.rem(self.dp, 2)
        self.y = lax.rem(lax.div(self.dp, 2), 2)
        self.z_low = lax.rem(lax.div(self.dp, 4), 2)
        self.z_high = lax.rem(lax.div(self.dp, 8), 2)
        self.peer = {"tensor": 1 - self.core}
        self.x_side = {"dp": self.dp + 1 - 2 * self.x}
        self.y_side = {"dp": self.dp + 2 - 4 * self.y}
        self.z_side = {"dp": self.dp + 4 - 8 * self.z_low}
        self.z_far = {"dp": self.dp + 8 - 16 * self.z_high}

    def greet(self, partners):
        barrier = pltpu.get_barrier_semaphore()
        for partner in partners:
            pl.semaphore_signal(barrier, inc=1, device_id=partner, device_id_type=MESH)

    def meet(self, partners):
        pl.semaphore_wait(pltpu.get_barrier_semaphore(), len(partners))


def remote(source, target, sems, index, device):
    send, recv = sems
    return pltpu.make_async_remote_copy(
        src_ref=source,
        dst_ref=target,
        send_sem=send.at[index],
        recv_sem=recv.at[index],
        device_id=device,
        device_id_type=MESH,
    )


def go(copies):
    for copy in copies:
        copy.start()


def finish(copies):
    for copy in copies:
        copy.wait()


HOPS = 6


class Chunk:
    def __init__(self, link, sems, base, whole, hop1, hop2=None, hop3=None, hop4=None):
        self.link, self.sems, self.base = link, sems, base
        self.held = [whole, hop1, hop2, hop3, hop4]
        self.sources = list(self.held)

    def hop(self, number):
        link, sems, base = self.link, self.sems, self.base
        source, landing = self.sources[number - 1], self.held[number]
        if number == 1:
            return [
                remote(source.at[0, :, :, 1 - link.x], landing.at[0], sems, base, link.x_side),
                remote(source.at[1, :, 1 - link.y], landing.at[1], sems, base + 1, link.y_side),
            ]
        if number == 2:
            return [
                remote(source.at[0, :, 1 - link.y], landing.at[0], sems, base + 2, link.y_side),
                remote(source.at[1, :, 1 - link.x], landing.at[1], sems, base + 3, link.x_side),
            ]
        if number == 3:
            return [
                remote(source.at[:, 1 - link.z_low], landing, sems, base + 4, link.z_side)
            ]
        return [remote(source.at[1 - link.z_high], landing, sems, base + 5, link.z_far)]

    def start(self, number):
        go(self.hop(number))

    def land(self, number):
        link = self.link
        finish(self.hop(number))
        own, landing = self.held[number - 1], self.held[number]

        def one(row):
            if number == 1:
                for other in range(2):
                    landing[0, row, other] += own[0, row, other, link.x]
                    landing[1, row, other] += own[1, row, link.y, other]
            elif number == 2:
                landing[0, row] += own[0, row, link.y]
                landing[1, row] += own[1, row, link.x]
            else:
                landing[row] += own[row, link.z_low]

        each(2, one)

    def total(self):
        finish(self.hop(4))
        return self.held[3][self.link.z_high] + self.held[4][...]


class DeepChunk:
    def __init__(self, link, sems, base, whole, hop1, hop2=None, hop3=None, hop4=None):
        self.link, self.sems, self.base = link, sems, base
        self.held = [whole, hop1, hop2, hop3, hop4]
        self.sources = list(self.held)

    def hop(self, number):
        link, sems, base = self.link, self.sems, self.base
        source, landing = self.sources[number - 1], self.held[number]
        if number == 1:
            return [remote(source.at[:, 1 - link.z_low], landing, sems, base, link.z_side)]
        if number == 2:
            return [remote(source.at[1 - link.z_high], landing, sems, base + 1, link.z_far)]
        if number == 3:
            side = landing.shape[-1]
            left, right = pl.ds(0, side), pl.ds(side, side)
            return [
                remote(
                    source.at[:, 1 - link.x, :, left], landing.at[0], sems, base + 2, link.x_side
                ),
                remote(
                    source.at[1 - link.y, :, :, right], landing.at[1], sems, base + 3, link.y_side
                ),
            ]
        return [
            remote(source.at[0, 1 - link.y], landing.at[0], sems, base + 4, link.y_side),
            remote(source.at[1, 1 - link.x], landing.at[1], sems, base + 5, link.x_side),
        ]

    def start(self, number):
        go(self.hop(number))

    def land(self, number):
        link = self.link
        finish(self.hop(number))
        own, landing = self.held[number - 1], self.held[number]

        def one(row):
            if number == 1:
                for other in range(4):
                    y, x = other // 2, other % 2
                    landing[row, y, x] += own[row, link.z_low, y, x]
            elif number == 2:
                for other in range(2):
                    landing[row, other] += own[row, other]
            else:
                side = landing.shape[-1]
                landing[0, row] += own[row, link.x, :, 0:side]
                landing[1, row] += own[link.y, row, :, side:]

        each(2, one)

    def total(self):
        finish(self.hop(4))
        own, landed = self.held[3], self.held[4]
        return jnp.concatenate(
            [own[0, self.link.y] + landed[0], own[1, self.link.x] + landed[1]], axis=-1
        )


def hop_shapes(rows, columns):
    return [
        (2, 2, 2, rows, columns),
        (2, 2, rows, columns),
        (2, rows, columns),
        (rows, columns),
    ]


def front_kernel(
    dp_size,
    tokens,
    first_values,
    skip_map,
    gain_ref,
    shift_ref,
    wq_ref,
    wk_ref,
    wv_ref,
    out_w,
    up_w,
    down_w,
    n1_ref,
    q_ref,
    k_ref,
    v_ref,
    att_ref,
    lse_ref,
    w_ref,
    sel_ref,
    out_peer,
    up_peer,
    down_peer,
    x_scr,
    fv_scr,
    proj_own,
    proj_send,
    proj_recv,
    sel_send,
    sel_recv,
    out_low,
    up_low,
    down_low,
    out_send,
    up_send,
    down_send,
    out_recv,
    up_recv,
    down_recv,
    lse_scr,
    local_sem,
    send_sem,
    recv_sem,
):
    step = pl.program_id(0)
    length, width = x_scr.shape
    blocks = length // BLOCK
    half = pl.num_programs(0) // 2
    own_width = wq_ref.shape[1]
    fresh_width = wv_ref.shape[0]
    fv_width = fv_scr.shape[1]
    link = Link(dp_size)
    sems = (send_sem, recv_sem)
    rows_here = pl.ds(link.core * length, length)
    local = [
        pltpu.make_async_copy(tokens.at[rows_here], x_scr, local_sem.at[0]),
        pltpu.make_async_copy(first_values.at[rows_here], fv_scr, local_sem.at[1]),
        pltpu.make_async_copy(up_w, up_low, local_sem.at[2]),
        pltpu.make_async_copy(down_w, down_low, local_sem.at[3]),
        pltpu.make_async_copy(out_w, out_low, local_sem.at[4]),
    ]
    early = [
        remote(proj_send, proj_recv, sems, 0, link.peer),
        remote(sel_send, sel_recv, sems, 1, link.peer),
    ]
    late = [
        remote(up_send, up_recv, sems, 2, link.peer),
        remote(down_send, down_recv, sems, 3, link.peer),
        remote(out_send, out_recv, sems, 4, link.peer),
    ]
    landed = [
        (late[0], up_recv, up_low, pltpu.make_async_copy(up_low, up_peer, local_sem.at[2])),
        (late[1], down_recv, down_low, pltpu.make_async_copy(down_low, down_peer, local_sem.at[3])),
        (late[2], out_recv, out_low, pltpu.make_async_copy(out_low, out_peer, local_sem.at[4])),
    ]

    @pl.when(step == 0)
    def _():
        link.greet([link.peer])
        go(local)
        proj_own[2, :, 0:fresh_width] = jnp.transpose(wv_ref[...])
        proj_own[2, :, fresh_width:] = jnp.zeros((width, own_width - fresh_width), BF16)
        for part, source in enumerate((wq_ref, wk_ref)):
            recast(source, proj_own.at[part])
        for part in range(3):
            recast(proj_own.at[part], proj_send.at[part])
        row = lax.broadcasted_iota(jnp.int32, (fv_width, own_width), 0)
        col = lax.broadcasted_iota(jnp.int32, (fv_width, own_width), 1)
        slots = (own_width - fresh_width) // HEAD_DIM
        target = jnp.full((fv_width, own_width), -1, jnp.int32)
        for slot in range(slots):
            start = fresh_width + slot * HEAD_DIM
            inside = jnp.logical_and(col >= start, col < start + HEAD_DIM)
            target = jnp.where(inside, skip_map[slot] * HEAD_DIM + col - start, target)
        chosen = jnp.where(row == target, 1.0, 0.0).astype(F32)
        sel_send[...] = chosen
        sel_ref[:, 0:own_width] = chosen.astype(BF16)
        link.meet([link.peer])
        go(early)
        lse_scr[...] = jnp.zeros_like(lse_scr)
        local[0].wait()
        local[1].wait()

        def one(block, carry):
            rows = pl.ds(block * BLOCK, BLOCK)
            normed, _ = norm_stats(x_scr[rows, :].astype(F32))
            n1_ref[rows, :] = (normed * gain_ref[...][None, :] + shift_ref[...][None, :]).astype(BF16)
            return carry

        lax.fori_loop(0, blocks, one, 0)

    @pl.when(step == half)
    def _():
        finish(early)
        sel_ref[:, own_width:] = sel_recv[...].astype(BF16)

    @pl.when(step < half)
    def _():
        cols = pl.ds(pl.multiple_of(step * PAIR, PAIR), PAIR)
        for part in range(3):
            w_ref[:, part * PAIR : (part + 1) * PAIR] = proj_own[part, :, cols]

    @pl.when(step >= half)
    def _():
        cols = pl.ds(pl.multiple_of((step - half) * PAIR, PAIR), PAIR)
        for part in range(3):
            w_ref[:, part * PAIR : (part + 1) * PAIR] = proj_recv[part, :, cols].astype(BF16)

    sel_cols = pl.ds(pl.multiple_of(step * PAIR, PAIR), PAIR)
    for block in range(blocks):
        rows = slice(block * BLOCK, (block + 1) * BLOCK)
        fused = dot_nn(n1_ref[rows, :], w_ref[...])
        picked = dot_nn(fv_scr[rows, :], sel_ref[:, sel_cols])
        q_ref[rows, :] = (fused[:, 0:PAIR].astype(BF16).astype(F32) * HEAD_DIM**-0.5).astype(BF16)
        k_ref[rows, :] = fused[:, PAIR : 2 * PAIR].astype(BF16)
        v_ref[rows, :] = (fused[:, 2 * PAIR :] + picked).astype(BF16)

    lane = lax.broadcasted_iota(jnp.int32, (BLOCK, PAIR), 1)
    row_pos = lax.broadcasted_iota(jnp.int32, (BLOCK, BLOCK), 0)
    col_pos = lax.broadcasted_iota(jnp.int32, (BLOCK, BLOCK), 1)
    seen = col_pos <= row_pos
    items = [(block, head) for block in range(blocks) for head in range(2)]
    scores, weights, partial = {}, {}, {}

    def score(index):
        block, head = items[index]
        lo, hi = block * BLOCK, (block + 1) * BLOCK
        query = split_heads(q_ref[lo:hi, :])[head]
        diag = dot_nt(query, k_ref[lo:hi, :])
        scores[index] = (diag, dot_nt(query, k_ref[0:lo, :]) if block else None)

    def soften(index):
        block, head = items[index]
        lo, hi = block * BLOCK, (block + 1) * BLOCK
        diag, past = scores.pop(index)
        diag = jnp.where(seen, diag, FILL)
        peak = jnp.max(diag, axis=-1, keepdims=True)
        if block:
            peak = jnp.maximum(peak, jnp.max(past, axis=-1, keepdims=True))
        diag = jnp.exp(diag - peak)
        mass = jnp.sum(diag, axis=-1, keepdims=True)
        if block:
            past = jnp.exp(past - peak)
            mass = mass + jnp.sum(past, axis=-1, keepdims=True)
        inverse = 1.0 / mass
        weights[index] = (
            (diag * inverse).astype(BF16),
            (past * inverse).astype(BF16) if block else None,
        )
        lse_scr[lo:hi, :] = jnp.where(
            lane == 2 * step + head, peak + jnp.log(mass), lse_scr[lo:hi, :]
        )

    def attend(index):
        block, head = items[index]
        lo, hi = block * BLOCK, (block + 1) * BLOCK
        diag, past = weights.pop(index)
        total = dot_nn(diag, split_heads(v_ref[lo:hi, :])[head])
        if block:
            total = total + dot_nn(past, split_heads(v_ref[0:lo, :])[head])
        if head == 0:
            partial[block] = total
        else:
            att_ref[lo:hi, :] = (partial.pop(block) + total).astype(BF16)

    for index in range(len(items) + 2):
        if index < len(items):
            score(index)
        if 0 <= index - 1 < len(items):
            soften(index - 1)
        if index >= 2:
            attend(index - 2)

    @pl.when(step == 0)
    def _():
        for copy in local[2:]:
            copy.wait()
        recast(up_low, up_send)
        recast(down_low, down_send)
        recast(out_low, out_send)
        go(late)

    @pl.when(step == pl.num_programs(0) - 2)
    def _():
        for copy, recv, low, store in landed:
            copy.wait()
            recast(recv, low)
            store.start()

    @pl.when(step == pl.num_programs(0) - 1)
    def _():
        for block in range(blocks):
            lo, hi = block * BLOCK, (block + 1) * BLOCK
            turned = jnp.transpose(lse_scr[lo:hi, :])
            for pair in range(lse_ref.shape[0]):
                lse_ref[pair, 0:2, lo:hi] = turned[2 * pair : 2 * pair + 2, :]
        for _, _, _, store in landed:
            store.wait()


def front(dp_size, tokens, first_values, skip_map, gain, shift, wq, wk, wv, out_w, up_w, down_w):
    width = tokens.shape[1]
    own_width = wq.shape[1]
    half = own_width // PAIR
    fv_width = first_values.shape[1]
    pair_block = pl.BlockSpec((SEQ_LEN, PAIR), lambda i: (0, i))
    pair_out = jax.ShapeDtypeStruct((SEQ_LEN, 2 * own_width), BF16)
    return pl.pallas_call(
        functools.partial(front_kernel, dp_size),
        grid=(2 * half,),
        in_specs=[
            ANY,
            ANY,
            SMEM,
            fixed((width,)),
            fixed((width,)),
            fixed(wq.shape),
            fixed(wk.shape),
            fixed(wv.shape),
            ANY,
            ANY,
            ANY,
        ],
        out_specs=[
            fixed((SEQ_LEN, width)),
            pair_block,
            pair_block,
            pair_block,
            pair_block,
            fixed((2 * half, 8, SEQ_LEN)),
            pl.BlockSpec((width, 3 * PAIR), lambda i: (0, i)),
            fixed((fv_width, 2 * own_width)),
            ANY,
            ANY,
            ANY,
        ],
        scratch_shapes=[
            pltpu.VMEM((SEQ_LEN, width), BF16),
            pltpu.VMEM((SEQ_LEN, fv_width), BF16),
            pltpu.VMEM((3, width, own_width), BF16),
            pltpu.VMEM((3, width, own_width), F32),
            pltpu.VMEM((3, width, own_width), F32),
            pltpu.VMEM((fv_width, own_width), F32),
            pltpu.VMEM((fv_width, own_width), F32),
            pltpu.VMEM(out_w.shape, BF16),
            pltpu.VMEM(up_w.shape, BF16),
            pltpu.VMEM(down_w.shape, BF16),
            pltpu.VMEM(out_w.shape, F32),
            pltpu.VMEM(up_w.shape, F32),
            pltpu.VMEM(down_w.shape, F32),
            pltpu.VMEM(out_w.shape, F32),
            pltpu.VMEM(up_w.shape, F32),
            pltpu.VMEM(down_w.shape, F32),
            pltpu.VMEM((SEQ_LEN, PAIR), F32),
            pltpu.SemaphoreType.DMA((5,)),
            pltpu.SemaphoreType.DMA((5,)),
            pltpu.SemaphoreType.DMA((5,)),
        ],
        out_shape=[
            jax.ShapeDtypeStruct((SEQ_LEN, width), BF16),
            pair_out,
            pair_out,
            pair_out,
            pair_out,
            jax.ShapeDtypeStruct((2 * half, 8, SEQ_LEN), F32),
            jax.ShapeDtypeStruct((width, 6 * own_width), BF16),
            jax.ShapeDtypeStruct((fv_width, 2 * own_width), BF16),
            jax.ShapeDtypeStruct(out_w.shape, BF16),
            jax.ShapeDtypeStruct(up_w.shape, BF16),
            jax.ShapeDtypeStruct(down_w.shape, BF16),
        ],
        compiler_params=params(0, 60),
        name="front",
    )(tokens, first_values, skip_map, gain, shift, wq, wk, wv, out_w, up_w, down_w)


def gelu_pair(upper):
    scale = (2.0 / jnp.pi) ** 0.5
    square = upper * upper
    inner = upper * (scale + (scale * 0.044715) * square)
    tanh = jnp.tanh(inner)
    cdf = 0.5 + 0.5 * tanh
    slope = cdf + 0.5 * upper * (1.0 - tanh * tanh) * (scale + (3.0 * scale * 0.044715) * square)
    return upper * cdf, slope


def middle_kernel(dp_size, ring, n_exports, *refs):
    (
        tokens,
        attended,
        cotangent,
        seq_count,
        gain_ref,
        shift_ref,
        wo_own,
        wo_peer,
        up_own,
        down_own,
        up_peer,
        down_peer,
        layer_out,
        gmix_out,
        gheads_ref,
        og_own,
        og_peer,
        vec_ref,
    ) = refs[:18]
    exports = refs[18 : 18 + n_exports]
    (
        att_ref,
        mixed_scr,
        stage_scr,
        two_scr,
        low_scr,
        two_t,
        low_t,
        act_scr,
        gup_scr,
        up_scr,
        down_scr,
        wo_scr,
        post_scr,
        grad_scr,
        local_sem,
        send_sem,
        recv_sem,
    ) = refs[18 + n_exports : 35 + n_exports]
    ring_scr = refs[35 + n_exports :]
    step = pl.program_id(0)
    steps = pl.num_programs(0)
    length, width = mixed_scr.shape
    blocks = length // BLOCK
    own_width = wo_own.shape[0]
    own_ff = up_own.shape[1]
    chunks = grad_scr.shape[0]
    ff_block = own_ff // chunks
    link = Link(dp_size)
    sems = (send_sem, recv_sem)
    rows_here = pl.ds(link.core * length, length)
    x_ref = gheads_ref
    loads = [
        pltpu.make_async_copy(tokens.at[rows_here], x_ref, local_sem.at[0]),
        pltpu.make_async_copy(wo_own, wo_scr.at[pl.ds(0, own_width)], local_sem.at[1]),
        pltpu.make_async_copy(wo_peer, wo_scr.at[pl.ds(own_width, own_width)], local_sem.at[2]),
        pltpu.make_async_copy(cotangent.at[rows_here], low_scr, local_sem.at[3]),
        pltpu.make_async_copy(attended, att_ref, local_sem.at[16]),
    ]
    weight_loads = [
        pltpu.make_async_copy(up_own, up_scr.at[:, pl.ds(0, own_ff)], local_sem.at[4]),
        pltpu.make_async_copy(up_peer, up_scr.at[:, pl.ds(own_ff, own_ff)], local_sem.at[5]),
        pltpu.make_async_copy(down_own, down_scr.at[pl.ds(0, own_ff)], local_sem.at[6]),
        pltpu.make_async_copy(down_peer, down_scr.at[pl.ds(own_ff, own_ff)], local_sem.at[7]),
    ]
    gmix_copy = pltpu.make_async_copy(mixed_scr, gmix_out, local_sem.at[8])

    def layer_copies(block):
        rows = pl.ds(link.core * length + block * BLOCK, BLOCK)
        return [
            pltpu.make_async_copy(
                stage_scr.at[lax.rem(block, 2)], layer_out.at[rows], local_sem.at[9 + block]
            ),
            remote(stage_scr.at[lax.rem(block, 2)], layer_out.at[rows], sems, block, link.peer),
        ]


    def swap(chunk):
        return remote(
            post_scr.at[lax.rem(chunk, 2)], grad_scr.at[chunk], sems, blocks + chunk, link.peer
        )

    flows = {}
    if ring:
        base = blocks + chunks
        hop1, hop2, deep1 = ring_scr
        for slot, chunk in enumerate((0, 2, 4, 5)):
            flows[chunk] = Chunk(
                link,
                sems,
                base + HOPS * chunk,
                grad_scr.at[chunk],
                hop1.at[slot],
                None if chunk else hop2,
            )
        for slot, chunk in enumerate((1, 3)):
            flows[chunk] = DeepChunk(
                link, sems, base + HOPS * chunk, grad_scr.at[chunk], deep1.at[slot]
            )

    partners = [link.peer]
    if ring:
        partners += [link.x_side, link.y_side, link.z_side]

    def run(events):
        for chunk, number in events:
            if ring:
                if number > 1:
                    flows[chunk].land(number - 1)
                flows[chunk].start(number)

    @pl.when(step == 0)
    def _():
        link.greet(partners)
        go(loads)
        go(weight_loads)
        finish(loads)
        live = jnp.where(link.core < seq_count[0], 1.0, 0.0).astype(F32)

        def enter(block):
            rows = row_block(block)
            mixed = x_ref[rows, :].astype(F32) + dot_nn(att_ref[rows, :], wo_scr[...])
            mixed_scr[rows, :] = mixed
            normed, _ = norm_stats(mixed)
            two_low = (normed * gain_ref[...][None, :] + shift_ref[...][None, :]).astype(BF16)
            two_scr[rows, :] = two_low
            two_t[:, rows] = jnp.transpose(two_low)
            low = (low_scr[rows, :].astype(F32) * live).astype(BF16)
            low_scr[rows, :] = low
            low_t[:, rows] = jnp.transpose(low)

        each(blocks, enter)
        finish(weight_loads)
        link.meet(partners)

    last = lax.div(step, steps - 1)
    mine = (1 - lax.rem(step, 2)) * lax.div(step + steps - 1, steps) + last
    mine_index = lax.div(step - 1 + lax.div(steps - step, steps), 2)
    post_index = lax.div(step + 1, 2)
    turn = mine * mine_index + (1 - mine) * (chunks + post_index)
    slot = 2 * mine + (1 - mine) * lax.rem(post_index, 2)
    cols = pl.ds(pl.multiple_of(turn * ff_block, ff_block), ff_block)
    for block in range(blocks):
        rows = slice(block * BLOCK, (block + 1) * BLOCK)
        upper = dot_nn(two_scr[rows, :], up_scr[:, cols])
        active, slope = gelu_pair(upper)
        act_scr[rows, cols] = active.astype(BF16)
        grad_active = dot_nt(low_scr[rows, :], down_scr[cols, :])
        gup_scr[rows, cols] = (grad_active * slope).astype(BF16)

    block_shape = grad_scr.shape[1:-1] + (ff_block,)
    @pl.when(jnp.logical_and(mine == 0, post_index > 1))
    def _():
        swap(post_index - 2).wait_send()

    post_scr[slot, ..., 0:ff_block] = dot_nn(low_t[...], act_scr[:, cols]).reshape(block_shape)
    post_scr[slot, ..., ff_block:] = dot_nn(two_t[...], gup_scr[:, cols]).reshape(block_shape)

    @pl.when(mine == 0)
    def _():
        swap(post_index).start()

    @pl.when(mine == 1)
    def _():
        swap(mine_index).wait_recv()
        grad_scr[mine_index] += post_scr[2]

    if ring:
        for when, events in {
            2: [(0, 1)],
            4: [(1, 1)],
            6: [(2, 1)],
            8: [(3, 1), (0, 2)],
            10: [(4, 1)],
            11: [(5, 1)],
        }.items():

            @pl.when(step == when)
            def _():
                run(events)

    @pl.when(step == steps - 1)
    def _():
        swap(chunks - 2).wait_send()
        swap(chunks - 1).wait_send()
        if not ring:
            whole_copy = pltpu.make_async_copy(grad_scr, exports[0], local_sem.at[13])
            whole_copy.start()

        def leave(block):
            rows = row_block(block)

            @pl.when(block > 1)
            def _():
                finish(layer_copies(block - 2))

            stage_scr[lax.rem(block, 2)] = mixed_scr[rows, :] + dot_nn(
                act_scr[rows, :], down_scr[...]
            )
            go(layer_copies(block))

        each(blocks, leave)
        vec_ref[...] = jnp.zeros_like(vec_ref)

        def turn_back(block):
            rows = row_block(block)
            grad_two = dot_nt(gup_scr[rows, :], up_scr[...])
            normed, factor = norm_stats(mixed_scr[rows, :])
            vec_ref[0:1, :] += jnp.sum(grad_two * normed, axis=0, keepdims=True)
            vec_ref[1:2, :] += jnp.sum(grad_two, axis=0, keepdims=True)
            grad_mixed = low_scr[rows, :].astype(F32) + norm_backward(
                grad_two, normed, factor, gain_ref[...][None, :]
            )
            mixed_scr[rows, :] = grad_mixed
            grad_attn = grad_mixed.astype(BF16)
            low_t[:, rows] = jnp.transpose(grad_attn)
            gheads_ref[rows, :] = dot_nt(grad_attn, wo_scr[...]).astype(BF16)

        each(blocks, turn_back)
        gmix_copy.start()
        og_peer[...] = dot_nn(low_t[...], att_ref[:, own_width:]).reshape(og_peer.shape)
        og_own[...] = dot_nn(low_t[...], att_ref[:, 0:own_width]).reshape(og_own.shape)
        if ring:
            at_one, at_two, at_deep = exports
            outs = [
                pltpu.make_async_copy(hop1.at[pl.ds(1, 3)], at_one, local_sem.at[13]),
                pltpu.make_async_copy(hop2, at_two, local_sem.at[14]),
                pltpu.make_async_copy(deep1, at_deep, local_sem.at[15]),
            ]
            flows[0].land(2)
            outs[1].start()
            flows[1].land(1)
            flows[3].land(1)
            outs[2].start()
            flows[2].land(1)
            flows[5].land(1)
            flows[4].land(1)
            outs[0].start()
            finish(outs)
        else:
            whole_copy.wait()
        gmix_copy.wait()
        finish(layer_copies(blocks - 2))
        finish(layer_copies(blocks - 1))


def middle(
    dp_size, ring, tokens, attended, cotangent, seq_count, gain, shift, wo_own, wo_peer, own, peer
):
    width = tokens.shape[1]
    own_ff = own[0].shape[1]
    own_width = wo_own.shape[0]
    chunks = 6
    ff_block = own_ff // chunks
    grad_shape = place(ring, width, dp_size, 2 * ff_block)
    og_shape = place(ring, width, dp_size, own_width)
    scratch = []
    if ring:
        hop1, hop2, _, _ = hop_shapes(width // dp_size, 2 * ff_block)
        export_shapes = [(3,) + hop1, hop2, (2,) + hop1]
        scratch = [
            pltpu.VMEM((4,) + hop1, F32),
            pltpu.VMEM(hop2, F32),
            pltpu.VMEM((2,) + hop1, F32),
        ]
    else:
        export_shapes = [(chunks,) + grad_shape]
    blocks = SEQ_LEN // BLOCK
    n_sems = blocks + chunks + HOPS * chunks
    return pl.pallas_call(
        functools.partial(middle_kernel, dp_size, ring, len(export_shapes)),
        grid=(2 * chunks,),
        in_specs=[
            ANY,
            ANY,
            ANY,
            SMEM,
            fixed((width,)),
            fixed((width,)),
            ANY,
            ANY,
            ANY,
            ANY,
            ANY,
            ANY,
        ],
        out_specs=[
            ANY,
            ANY,
            fixed((SEQ_LEN, 2 * own_width)),
            fixed(og_shape),
            fixed(og_shape),
            fixed((8, width)),
        ]
        + [ANY] * len(export_shapes),
        scratch_shapes=[
            pltpu.VMEM((SEQ_LEN, 2 * own_width), BF16),
            pltpu.VMEM((SEQ_LEN, width), F32),
            pltpu.VMEM((2, BLOCK, width), F32),
            pltpu.VMEM((SEQ_LEN, width), BF16),
            pltpu.VMEM((SEQ_LEN, width), BF16),
            pltpu.VMEM((width, SEQ_LEN), BF16),
            pltpu.VMEM((width, SEQ_LEN), BF16),
            pltpu.VMEM((SEQ_LEN, 2 * own_ff), BF16),
            pltpu.VMEM((SEQ_LEN, 2 * own_ff), BF16),
            pltpu.VMEM((width, 2 * own_ff), BF16),
            pltpu.VMEM((2 * own_ff, width), BF16),
            pltpu.VMEM((2 * own_width, width), BF16),
            pltpu.VMEM((3,) + grad_shape, F32),
            pltpu.VMEM((chunks,) + grad_shape, F32),
            pltpu.SemaphoreType.DMA((17,)),
            pltpu.SemaphoreType.DMA((n_sems,)),
            pltpu.SemaphoreType.DMA((n_sems,)),
        ]
        + scratch,
        out_shape=[
            jax.ShapeDtypeStruct((2 * SEQ_LEN, width), F32),
            jax.ShapeDtypeStruct((SEQ_LEN, width), F32),
            jax.ShapeDtypeStruct((SEQ_LEN, 2 * own_width), BF16),
            jax.ShapeDtypeStruct(og_shape, F32),
            jax.ShapeDtypeStruct(og_shape, F32),
            jax.ShapeDtypeStruct((8, width), F32),
        ]
        + [jax.ShapeDtypeStruct(shape, F32) for shape in export_shapes],
        compiler_params=params(1, 60),
        name="middle",
    )(tokens, attended, cotangent, seq_count, gain, shift, wo_own, wo_peer, *own, *peer)


def back_kernel(dp_size, ring, counts, *refs):
    n_in, n_out, fresh_width = counts
    (
        tokens,
        n1_ref,
        q_ref,
        k_ref,
        v_ref,
        att_ref,
        gheads_ref,
        lse_ref,
        gmix,
        gain_ref,
        w_ref,
        sel_ref,
        og_own,
        og_peer,
        vec2_ref,
    ) = refs[:15]
    exports = refs[15:n_in]
    in_grad, first_grad = refs[n_in : n_in + 2]
    outs = refs[n_in + 2 : n_in + n_out]
    scratch = refs[n_in + n_out :]
    (
        x_scr,
        gmix_scr,
        n1_t,
        dk_acc,
        dv_acc,
        dq_t,
        stack_scr,
        one_acc,
        fv_t,
        post_scr,
        out_scr,
        sums_scr,
        local_sem,
        send_sem,
        recv_sem,
    ) = scratch[:15]
    step = pl.program_id(0)
    steps = pl.num_programs(0)
    length, width = x_scr.shape
    blocks = length // BLOCK
    link = Link(dp_size)
    sems = (send_sem, recv_sem)
    rows_here = pl.ds(link.core * length, length)
    chunks = lse_ref.shape[0] * steps // 2
    grads = scratch[15 : 15 + chunks]
    ring_scr = list(scratch[15 + chunks :])
    side = fv_t.shape[0] // 2
    loads = [
        pltpu.make_async_copy(tokens.at[rows_here], x_scr, local_sem.at[0]),
        pltpu.make_async_copy(gmix, gmix_scr, local_sem.at[1]),
        pltpu.make_async_copy(og_own, out_scr.at[0], local_sem.at[2]),
    ]
    out_swap = remote(og_peer, out_scr.at[1], sems, 0, link.peer)
    swaps = [
        remote(
            post_scr.at[0, ..., pl.ds(0, grads[chunk].shape[-1])],
            grads[chunk],
            sems,
            1 + chunk,
            link.peer,
        )
        for chunk in range(chunks)
    ]
    base = 1 + chunks
    in_copies = [
        remote(one_acc, in_grad.at[rows_here], sems, base, link.peer),
        pltpu.make_async_copy(one_acc, in_grad.at[rows_here], local_sem.at[3]),
    ]
    seq_cols = pl.ds(pl.multiple_of(link.core * length, length), length)
    first_copies = [
        remote(
            fv_t.at[pl.ds((1 - link.core) * side, side)],
            first_grad.at[:, seq_cols],
            sems,
            base + 1,
            link.peer,
        ),
        pltpu.make_async_copy(
            fv_t.at[pl.ds(link.core * side, side)], first_grad.at[:, seq_cols], local_sem.at[4]
        ),
    ]
    base += 2
    flows = {}
    if ring:
        at_one, at_two, at_deep = exports
        hop1, hop2, hop3, hop4, deep1, deep2, deep3, deep4 = ring_scr[:8]
        del ring_scr[:8]
        for slot, chunk in enumerate((0, 2, 4, 5)):
            flows[chunk] = Chunk(
                link,
                sems,
                base + slot * HOPS,
                None,
                None if chunk == 0 else hop1.at[slot - 1],
                hop2.at[slot],
                hop3.at[slot],
                hop4.at[slot],
            )
            if chunk:
                flows[chunk].sources[1] = at_one.at[slot - 1]
        flows[0].sources[2] = at_two
        for slot, chunk in enumerate((1, 3)):
            flows[chunk] = DeepChunk(
                link,
                sems,
                base + (4 + slot) * HOPS,
                None,
                deep1.at[slot],
                deep2.at[slot],
                deep3.at[slot],
                deep4.at[slot],
            )
            flows[chunk].sources[1] = at_deep.at[slot]
        ring_loads = [
            pltpu.make_async_copy(at_one, hop1, local_sem.at[5]),
            pltpu.make_async_copy(at_two, hop2.at[0], local_sem.at[6]),
            pltpu.make_async_copy(at_deep.at[0, link.z_high], deep1.at[0], local_sem.at[7]),
            pltpu.make_async_copy(at_deep.at[1, link.z_high], deep1.at[1], local_sem.at[8]),
        ]
        wholes = {"o": out_scr.at[0]}
        wholes.update({"p%d" % n: grads[n] for n in range(chunks)})
        place_in = base + 6 * HOPS
        for name, whole in wholes.items():
            flows[name] = Chunk(link, sems, place_in, whole, *ring_scr[:4])
            del ring_scr[:4]
            place_in += HOPS
        v_send, v_recv = ring_scr[:2]
        flows["v"] = Chunk(link, sems, place_in, v_recv, *ring_scr[2:6])
        vec_swap = remote(v_send, v_recv, sems, place_in + HOPS, link.peer)

    ready = [(1, 2), (2, 2), (3, 2), (4, 2), (5, 2), (0, 3)]

    def run(events):
        for name, number in events:
            if ring:
                if number > 1 and (name, number) not in ready:
                    flows[name].land(number - 1)
                flows[name].start(number)

    @pl.when(step == 0)
    def _():
        partners = [link.peer]
        if ring:
            partners += [link.x_side, link.y_side, link.z_side, link.z_far]
        link.greet(partners)
        link.meet(partners)
        if ring:
            flows[2].start(2)
            flows[3].start(2)
            flows[5].start(2)
            flows[0].start(3)
        out_swap.start()
        go(loads)
        if ring:
            go(ring_loads)
        for block in range(blocks):
            rows = slice(block * BLOCK, (block + 1) * BLOCK)
            n1_t[:, rows] = jnp.transpose(n1_ref[rows, :])
        one_acc[...] = jnp.zeros_like(one_acc)
        fv_t[...] = jnp.zeros_like(fv_t)

    k_t = jnp.transpose(k_ref[...])
    prod_t = jnp.transpose(gheads_ref[...].astype(F32) * att_ref[...].astype(F32))
    lse_pair = lse_ref[0]
    row_pos = lax.broadcasted_iota(jnp.int32, (BLOCK, BLOCK), 0)
    col_pos = lax.broadcasted_iota(jnp.int32, (BLOCK, BLOCK), 1)
    seen = row_pos <= col_pos
    items = [
        (block, head, source)
        for block in range(blocks)
        for head in range(2)
        for source in range(block + 1)
    ]
    raw, soft_low, dq_sums = {}, {}, {}

    def part_of(ref, block, head):
        return split_heads(ref[block * BLOCK : (block + 1) * BLOCK, :])[head]

    def score(index):
        block, head, source = items[index]
        rows = slice(source * BLOCK, (source + 1) * BLOCK)
        raw[index] = (
            dot_nt(k_ref[rows, :], part_of(q_ref, block, head)),
            dot_nt(v_ref[rows, :], part_of(gheads_ref, block, head)),
        )

    def soften(index):
        block, head, source = items[index]
        cols = slice(block * BLOCK, (block + 1) * BLOCK)
        part = slice(head * HEAD_DIM, (head + 1) * HEAD_DIM)
        delta = jnp.sum(prod_t[part, cols], axis=0, keepdims=True)
        scores, dsoft = raw.pop(index)
        soft = jnp.exp(scores - lse_pair[head : head + 1, cols])
        if source == block:
            soft = jnp.where(seen, soft, 0.0)
        soft_low[index] = (soft.astype(BF16), (soft * (dsoft - delta)).astype(BF16))

    def spread(index):
        block, head, source = items[index]
        rows = slice(source * BLOCK, (source + 1) * BLOCK)
        part = slice(head * HEAD_DIM, (head + 1) * HEAD_DIM)
        soft, dscore = soft_low.pop(index)
        dv = dot_nn(soft, part_of(gheads_ref, block, head))
        dk = dot_nn(dscore, part_of(q_ref, block, head))
        if head == 0 and source == block:
            dv_acc[rows, :] = dv
            dk_acc[rows, :] = dk
        else:
            dv_acc[rows, :] += dv
            dk_acc[rows, :] += dk
        dq = dot_nn(k_t[part, rows], dscore)
        dq_sums[block, head] = dq if source == 0 else dq_sums[block, head] + dq
        if source == block:
            dq_t[part, block * BLOCK : (block + 1) * BLOCK] = dq_sums.pop((block, head))

    for index in range(len(items) + 2):
        if index < len(items):
            score(index)
        if 0 <= index - 1 < len(items):
            soften(index - 1)
        if index >= 2:
            spread(index - 2)

    middle_events = {
        2: [(5, 3)],
        3: [(3, 3), (4, 3)],
        4: [("o", 3), (5, 4)],
        5: [("p1", 2), (4, 4)],
    }
    end_events = {
        0: [("o", 1)],
        1: [("p0", 1), (1, 2), (4, 2), (2, 3)],
        2: [("o", 2)],
        3: [("p1", 1)],
        4: [("p0", 2)],
        5: [("p2", 1), ("p0", 3), (0, 4), (2, 4), ("o", 4)],
    }
    if ring:
        for when, events in middle_events.items():

            @pl.when(step == when)
            def _():
                run(events)

        @pl.when(step == 0)
        def _():
            finish(ring_loads)

    for block in range(blocks):
        rows = slice(block * BLOCK, (block + 1) * BLOCK)
        stack_scr[rows, 0:PAIR] = (jnp.transpose(dq_t[:, rows]) * HEAD_DIM**-0.5).astype(BF16)
        stack_scr[rows, PAIR : 2 * PAIR] = dk_acc[rows, :].astype(BF16)
        dv = dv_acc[rows, :]
        stack_scr[rows, 2 * PAIR : 3 * PAIR] = dv.astype(BF16)
        one_acc[rows, :] += dot_nt(stack_scr[rows, :], w_ref[...])

    @pl.when(step >= 2 * (fresh_width // PAIR))
    def _():
        for block in range(blocks):
            rows = slice(block * BLOCK, (block + 1) * BLOCK)
            dv = dv_acc[rows, :]
            high = dv.astype(BF16)
            low = (dv - high.astype(F32)).astype(BF16)
            fv_t[:, rows] += dot_nt(sel_ref[...], high) + dot_nt(sel_ref[...], low)

    for chunk in range(1, chunks):

        @pl.when(step == 2 * chunk)
        def _():
            swaps[chunk - 1].wait_send()

    post_scr[lax.rem(step, 2)] = dot_nn(n1_t[...], stack_scr[...]).reshape(post_scr.shape[1:])
    for chunk in range(chunks):
        used = grads[chunk].shape[-1]

        @pl.when(step == 2 * chunk)
        def _():
            swaps[chunk].start()

        @pl.when(step == 2 * chunk + 1)
        def _():
            swaps[chunk].wait_recv()
            grads[chunk][...] += post_scr[1, ..., 0:used]
            if chunk == chunks - 1:
                swaps[chunk].wait_send()

    @pl.when(step == 0)
    def _():
        out_swap.wait()
        finish(loads)
        out_scr[0] += out_scr[1]

    if ring:
        for when, events in end_events.items():

            @pl.when(step == when)
            def _():
                run(events)

    @pl.when(step == steps - 1)
    def _():
        go(first_copies)
        sums_scr[...] = jnp.zeros_like(sums_scr)

        def leave(block):
            rows = row_block(block)
            normed, factor = norm_stats(x_scr[rows, :].astype(F32))
            grad_one = one_acc[rows, :]
            sums_scr[0:1, :] += jnp.sum(grad_one * normed, axis=0, keepdims=True)
            sums_scr[1:2, :] += jnp.sum(grad_one, axis=0, keepdims=True)
            one_acc[rows, :] = gmix_scr[rows, :] + norm_backward(
                grad_one, normed, factor, gain_ref[...][None, :]
            )

        each(blocks, leave)
        go(in_copies)
        vectors = jnp.concatenate(
            [sums_scr[0:2, :], vec2_ref[0:2, :], jnp.zeros((4, width), F32)], axis=0
        )
        if ring:
            up_out, down_out, q_out, k_out, v_out, o_out, vec_out = outs
            rows_dev = width // dp_size
            v_send[...] = jnp.zeros_like(v_send)
            for block in range(dp_size):
                v_send[block // 8, block // 4 % 2, block // 2 % 2, block % 2, :, 0:rows_dev] = vectors[
                    :, block * rows_dev : (block + 1) * rows_dev
                ]
            vec_swap.start()
            run([("p2", 2)])
            vec_swap.wait()
            v_recv[...] += v_send[...]
            run(
                [("v", 1), (1, 3), ("p1", 3), ("p2", 3), ("v", 2), (1, 4), (3, 4), ("p0", 4), ("p1", 4), ("v", 3), ("p2", 4), ("v", 4)]
            )
            ff_block = up_out.shape[-1] // 6

            def put_ffn(index, total):
                cols = slice(index * ff_block, (index + 1) * ff_block)
                down_out[:, cols] = total[:, 0:ff_block]
                up_out[:, cols] = total[:, ff_block:]

            def put_proj(index, total):
                cols = slice(index * PAIR, (index + 1) * PAIR)
                q_out[:, cols] = total[:, 0:PAIR]
                k_out[:, cols] = total[:, PAIR : 2 * PAIR]
                if total.shape[1] > 2 * PAIR:
                    last = min((index + 1) * PAIR, fresh_width)
                    v_out[:, index * PAIR : last] = total[
                        :, 2 * PAIR : 2 * PAIR + last - index * PAIR
                    ]

            for chunk in range(6):
                put_ffn(chunk, flows[chunk].total())
            o_out[...] = flows["o"].total()
            put_proj(0, flows["p0"].total())
            put_proj(1, flows["p1"].total())
            put_proj(2, flows["p2"].total())
            vec_out[...] = flows["v"].total()
        else:
            vec_out = outs[-1]
            vec_out[...] = vectors
            stores = [
                pltpu.make_async_copy(grads[chunk], outs[chunk], local_sem.at[5 + chunk])
                for chunk in range(chunks)
            ]
            stores.append(pltpu.make_async_copy(out_scr.at[0], outs[chunks], local_sem.at[8]))
            go(stores)
            finish(stores)
        finish(in_copies)
        finish(first_copies)


def back(
    dp_size,
    ring,
    tokens,
    n1,
    q,
    k,
    v,
    attended,
    grad_heads,
    lse,
    grad_mixed,
    gain,
    weights,
    select,
    og_own,
    og_peer,
    vec2,
    exports,
    fresh_width,
    own_ff,
):
    width = tokens.shape[1]
    own_width = og_own.shape[-1]
    half = own_width // PAIR
    fv_width = select.shape[0]
    side = fv_width // 2
    pair_of = lambda i: lax.rem(i + 1, 2) * half + lax.div(i, 2)
    pair_block = pl.BlockSpec((SEQ_LEN, PAIR), lambda i: (0, pair_of(i)))
    used = [3 * PAIR if n * PAIR < fresh_width else 2 * PAIR for n in range(half)]
    grad_shapes = [place(ring, width, dp_size, columns) for columns in used]
    og_shape = place(ring, width, dp_size, own_width)
    scratch = [
        pltpu.VMEM((SEQ_LEN, width), BF16),
        pltpu.VMEM((SEQ_LEN, width), F32),
        pltpu.VMEM((width, SEQ_LEN), BF16),
        pltpu.VMEM((SEQ_LEN, PAIR), F32),
        pltpu.VMEM((SEQ_LEN, PAIR), F32),
        pltpu.VMEM((PAIR, SEQ_LEN), F32),
        pltpu.VMEM((SEQ_LEN, 3 * PAIR), BF16),
        pltpu.VMEM((SEQ_LEN, width), F32),
        pltpu.VMEM((fv_width, SEQ_LEN), F32),
        pltpu.VMEM((2,) + grad_shapes[0], F32),
        pltpu.VMEM((2,) + og_shape, F32),
        pltpu.VMEM((8, width), F32),
        pltpu.SemaphoreType.DMA((11,)),
    ]
    n_sems = 3 + half + (1 + (8 + half) * HOPS if ring else 0)
    scratch += [pltpu.SemaphoreType.DMA((n_sems,))] * 2
    scratch += [pltpu.VMEM(shape, F32) for shape in grad_shapes]
    if ring:
        rows = width // dp_size

        def hops(columns, height=rows, count=None):
            lead = () if count is None else (count,)
            return [lead + shape for shape in hop_shapes(height, columns)]

        ff = exports[0].shape[-1]
        shapes = [(3,) + hops(ff)[0]] + hops(ff, count=4)[1:]
        shapes += [(2, 2, 2, rows, ff)] * 2
        shapes += [(2, 2, 2, rows, ff // 2), (2, 2, rows, ff // 2)]
        shapes += hops(own_width)
        for columns in used:
            shapes += hops(columns)
        vec_whole = place(ring, width, dp_size, PAIR)[:4] + (8, PAIR)
        shapes += [vec_whole, vec_whole] + hops(PAIR, 8)
        scratch += [pltpu.VMEM(shape, F32) for shape in shapes]
        totals = [
            (rows, own_ff),
            (rows, own_ff),
            (rows, own_width),
            (rows, own_width),
            (rows, fresh_width),
            (rows, own_width),
            (8, PAIR),
        ]
        total_specs = [fixed(shape) for shape in totals]
        export_args = list(exports)
        export_specs = [ANY] * len(export_args)
    else:
        totals = grad_shapes + [og_shape, (8, width)]
        total_specs = [ANY] * (half + 1) + [fixed((8, width))]
        export_args, export_specs = [], []
    in_specs = [
        ANY,
        fixed((SEQ_LEN, width)),
        pair_block,
        pair_block,
        pair_block,
        pair_block,
        pair_block,
        pl.BlockSpec((1, 8, SEQ_LEN), lambda i: (pair_of(i), 0, 0)),
        ANY,
        fixed((width,)),
        pl.BlockSpec((width, 3 * PAIR), lambda i: (0, pair_of(i))),
        pl.BlockSpec((fv_width, PAIR), lambda i: (0, pair_of(i))),
        ANY,
        ANY,
        fixed((8, width)),
    ] + export_specs
    return pl.pallas_call(
        functools.partial(
            back_kernel, dp_size, ring, (len(in_specs), 2 + len(totals), fresh_width)
        ),
        grid=(2 * half,),
        in_specs=in_specs,
        out_specs=[ANY, ANY] + total_specs,
        scratch_shapes=scratch,
        out_shape=[
            jax.ShapeDtypeStruct((2 * SEQ_LEN, width), F32),
            jax.ShapeDtypeStruct((side, 2 * SEQ_LEN), F32),
        ]
        + [jax.ShapeDtypeStruct(shape, F32) for shape in totals],
        compiler_params=params(2, 60),
        name="back",
    )(
        tokens,
        n1,
        q,
        k,
        v,
        attended,
        grad_heads,
        lse,
        grad_mixed,
        gain,
        weights,
        select,
        og_own,
        og_peer,
        vec2,
        *export_args,
    )


def collect_kernel(large, *refs):
    half = len(refs) // 2
    pairs = list(zip(refs[:half], refs[half:]))
    for source, target in pairs[:large]:
        target[...] = source[...]

    @pl.when(pl.program_id(0) == 0)
    def _():
        for source, target in pairs[large:]:
            target[...] = source[...]


def collect(tall, columns, small):
    blocks = 2
    rows = tall[0]
    specs = [pl.BlockSpec((rows.shape[0] // blocks, rows.shape[1]), lambda i: (i, 0))] * 2 + [
        pl.BlockSpec((columns.shape[0], columns.shape[1] // blocks), lambda i: (0, i)),
    ] + [fixed(array.shape) for array in small]
    arrays = tall + [columns] + small
    return pl.pallas_call(
        functools.partial(collect_kernel, 3),
        grid=(blocks,),
        in_specs=specs,
        out_specs=specs,
        out_shape=[jax.ShapeDtypeStruct(array.shape, array.dtype) for array in arrays],
        compiler_params=pltpu.CompilerParams(vmem_limit_bytes=60 * 1024 * 1024),
        name="collect",
    )(*arrays)


def on_device(
    dp_size,
    tokens,
    first_values,
    seq_count,
    skip_map,
    norm1_gain,
    norm1_shift,
    query_weight,
    key_weight,
    value_weight,
    out_weight,
    norm2_gain,
    norm2_shift,
    up_weight,
    down_weight,
    cotangent,
):
    width = tokens.shape[1]
    own_width = query_weight.shape[1]
    fresh_width = value_weight.shape[1]
    own_ff = up_weight.shape[1]
    ring = ring_of(dp_size, width)
    gain1, shift1, gain2, shift2 = norm1_gain, norm1_shift, norm2_gain, norm2_shift
    n1, q, k, v, attended, lse, weights, select, out_peer, up_peer, down_peer = front(
        dp_size,
        tokens,
        first_values,
        skip_map,
        gain1,
        shift1,
        query_weight,
        key_weight,
        value_weight.T,
        out_weight,
        up_weight,
        down_weight,
    )
    layer_out, grad_mixed, grad_heads, og_own, og_peer, vec2, *exports = middle(
        dp_size,
        ring,
        tokens,
        attended,
        cotangent,
        seq_count,
        gain2,
        shift2,
        out_weight,
        out_peer,
        (up_weight, down_weight),
        (up_peer, down_peer),
    )
    input_grad, first_grad, *totals = back(
        dp_size,
        ring,
        tokens,
        n1,
        q,
        k,
        v,
        attended,
        grad_heads,
        lse,
        grad_mixed,
        gain1,
        weights,
        select,
        og_own,
        og_peer,
        vec2,
        exports,
        fresh_width,
        own_ff,
    )
    if ring:
        *totals, vectors = totals
        layer_out, input_grad, first_grad, *totals = collect([layer_out, input_grad], first_grad, totals)
        up_total, down_t, query_total, key_total, value_total, out_t = totals
        rows = width // dp_size
        down_total, out_total = down_t.T, out_t.T
        gain1_total, shift1_total, gain2_total, shift2_total = (vectors[n, :rows] for n in range(4))
    else:
        *proj, out_grad, vectors = totals
        chunks = exports[0].shape[0]
        ff_block = own_ff // chunks
        vectors = vectors + lax.ppermute(vectors, "tensor", [(0, 1), (1, 0)])
        columns = list(proj) + [out_grad] + [exports[0][n] for n in range(chunks)]
        packed = jnp.concatenate(columns + [jnp.pad(vectors.T, ((0, 0), (0, 120)))], axis=1)
        summed = lax.psum_scatter(packed, "dp", scatter_dimension=0, tiled=True)
        heads, start = [[], [], []], 0
        for part in proj:
            for n in range(part.shape[1] // PAIR):
                heads[n].append(summed[:, start : start + PAIR])
                start += PAIR
        query_total, key_total, value_total = (jnp.concatenate(part, axis=1) for part in heads)
        value_total = value_total[:, :fresh_width]
        out_total = summed[:, start : start + own_width].T
        start += own_width
        pairs = summed[:, start : start + 2 * own_ff].reshape(-1, chunks, 2, ff_block)
        down_total = pairs[:, :, 0].reshape(-1, own_ff).T
        up_total = pairs[:, :, 1].reshape(-1, own_ff)
        start += 2 * own_ff
        gain1_total, shift1_total, gain2_total, shift2_total = (
            summed[:, start + n] for n in range(4)
        )
    return (
        layer_out,
        input_grad,
        first_grad.T,
        gain1_total,
        shift1_total,
        query_total,
        key_total,
        value_total,
        out_total,
        gain2_total,
        shift2_total,
        up_total,
        down_total,
    )


def solution(mesh):
    placed = (
        P("dp", None),
        P("dp", None),
        P("dp"),
        P("tensor"),
        P(),
        P(),
        P(None, "tensor"),
        P(None, "tensor"),
        P(None, "tensor"),
        P("tensor", None),
        P(),
        P(),
        P(None, "tensor"),
        P("tensor", None),
        P("dp", None),
    )
    return jax.shard_map(
        functools.partial(on_device, mesh.shape["dp"]),
        mesh=mesh,
        in_specs=placed,
        out_specs=(
            P("dp", None),
            P("dp", None),
            P("dp", "tensor"),
            P("dp"),
            P("dp"),
            P("dp", "tensor"),
            P("dp", "tensor"),
            P("dp", "tensor"),
            P("tensor", "dp"),
            P("dp"),
            P("dp"),
            P("dp", "tensor"),
            P("tensor", "dp"),
        ),
        check_vma=False,
    )
```
